32 devices in a mesh: gx: 2 (over core), gy: 4 (over z), gz: 4 (over y, x).
Axes of the slice: x: 2, y: 2, z: 4, core: 2. Of those that a mesh axis runs over, the one named last changes fastest.
Arguments:
- positions: float32 [2, 4, 4, 2, 3, 128], P('gx', 'gy', 'gz'), may hold values from 0 to 12, as said below
- features: bfloat16 [2, 4, 4, 2, 128, 128], P('gx', 'gy', 'gz'), may hold values from -6 to 6
- counts: int32 [2, 4, 4, 2], P('gx', 'gy', 'gz'), may hold values from 0 to 128, as said below
- neighbours: int32 [2, 4, 4, 2, 8], P('gx', 'gy', 'gz'), may hold values from -1 to 53, as said below
- mix_weight: bfloat16 [1024, 128], replicated, may hold values from -0.1875 to 0.1875
- readout: float32 [128], replicated, may hold values from -4 to 4
- radial_rates: float32 [4], replicated, may hold values from 0.03 to 0.6
Outputs:
- forces: float32 [2, 4, 4, 2, 3, 128], P('gx', 'gy', 'gz')
- feature_grads: float32 [2, 4, 4, 2, 128, 128], P('gx', 'gy', 'gz')
The draws below stay inside these ranges and needn't reach their ends.
Inputs may be any that keep to these rules, and one draw needn't show every extreme that they name: The atoms of a tile fill its first counts slots; a count of 0 marks a tile slot that its device doesn't own; every draw has a tile with 128 atoms. neighbours[.., t, s] names a tile of the device's neighbourhood as ((dx + 1) * 9 + (dy + 1) * 3 + (dz + 1)) * 2 + u, dx, dy, dz in -1..1 being the device offsets along gx, gy, gz and u the tile slot; slot 0 names tile t itself, every other used slot names a tile with one or more atoms, the entries of a row differ, and -1 marks unused slots, which come after the used ones. `positions`: the atoms of device (a, b, c) lie in the cube of side 3 whose lowest corner is 3 (a, b, c).
All inputs are finite; a program needn't handle non-finite values.
Results may differ from the reference program's by a relative error of at most 0.0008.
Values may be sent and summed in bfloat16 or wider, within the bound.
No kernel may reach another device: no remote copies, remote signals or barrier semaphores. Data moves between devices by JAX's collectives and lax.ppermute only.
A program may use at most 64 MiB of HBM per device.

```python
import math
import jax
import jax.numpy as jnp
from jax import lax

ATOMS = 128
CH = 128
RAD = 4
NBR = 8
TPD = 2
N_GX = 2
N_GY = 4
N_GZ = 4


box_side = 3.0


def draw_positions(key, part):
    full_shape = (N_GX, N_GY, N_GZ, TPD, 3, ATOMS)
    inside = box_side * jax.random.uniform(key, full_shape, jnp.float32)
    component = lax.broadcasted_iota(jnp.int32, full_shape, 4)
    corner = jnp.where(component == 0, lax.broadcasted_iota(jnp.int32, full_shape, 0), jnp.where(component == 1, lax.broadcasted_iota(jnp.int32, full_shape, 1), lax.broadcasted_iota(jnp.int32, full_shape, 2)))
    return corner.astype(jnp.float32) * box_side + inside


def draw_counts(key, part):
    full_shape = (N_GX, N_GY, N_GZ, TPD)
    total_slots = N_GX * N_GY * N_GZ * TPD
    key_size, key_taken, key_spot = jax.random.split(jax.random.fold_in(key, 11), 3)
    sizes = jax.random.randint(key_size, full_shape, ATOMS // 4, ATOMS + 1)
    taken = jax.random.randint(key_taken, full_shape, 0, 5) < 2
    filled = jnp.where(taken, sizes, 0).reshape(total_slots)
    spot = jax.random.randint(key_spot, (), 0, total_slots)
    filled = jnp.where(lax.broadcasted_iota(jnp.int32, (total_slots,), 0) == spot, ATOMS, filled)
    return filled.reshape(full_shape).astype(jnp.int32)


def draw_neighbours(key, part):
    rows_total = N_GX * N_GY * N_GZ * TPD
    near_total = 27 * TPD
    tile_counts = draw_counts(key, part)
    padded = jnp.pad(tile_counts, ((1, 1), (1, 1), (1, 1), (0, 0)))
    blocks = []
    for shift_x in range(3):
        for shift_y in range(3):
            for shift_z in range(3):
                blocks.append(padded[shift_x:shift_x + N_GX, shift_y:shift_y + N_GY, shift_z:shift_z + N_GZ, :])
    near_counts = jnp.stack(blocks, axis=3).reshape(N_GX * N_GY * N_GZ, near_total)
    near_counts = jnp.repeat(near_counts, TPD, axis=0)
    key_perm, key_length = jax.random.split(jax.random.fold_in(key, 23))
    row_keys = jax.random.split(key_perm, rows_total)
    ranks = jax.vmap(lambda row_key: jax.random.permutation(row_key, near_total))(row_keys).astype(jnp.int32)
    own_slot = (13 * TPD + lax.broadcasted_iota(jnp.int32, (rows_total, 1), 0) % TPD).astype(jnp.int32)
    column_all = lax.broadcasted_iota(jnp.int32, (rows_total, near_total), 1)
    eligible = (near_counts > 0) & (column_all != own_slot)
    scores = ranks + eligible.astype(jnp.int32) * near_total
    top_scores, chosen = lax.top_k(scores, NBR - 1)
    chosen = chosen.astype(jnp.int32)
    chosen_ok = top_scores >= near_total
    lengths = jax.random.randint(key_length, (rows_total, 1), max(NBR // 2, 1), NBR + 1)
    column = lax.broadcasted_iota(jnp.int32, (rows_total, NBR - 1), 1) + 1
    chosen = jnp.where(chosen_ok & (column < lengths), chosen, -1)
    listed = jnp.concatenate([own_slot, chosen], axis=1)
    return listed.reshape(N_GX, N_GY, N_GZ, TPD, NBR).astype(jnp.int32)


def steps_of(rng, extent, pieces, low, high):
    level = 1.0
    for axis_at, shards_of in pieces:
        heights = jax.random.uniform(jax.random.fold_in(jax.random.fold_in(rng, 6), axis_at), (shards_of,), jnp.float32, low / len(pieces), high / len(pieces))
        level = level * jnp.repeat(jnp.exp(heights), extent[axis_at] // shards_of).reshape((-1,) + (1,) * (len(extent) - 1 - axis_at))
    return level


def noise(key, shape, width, bound, cuts=(), kind=jnp.bfloat16):
    values = width * jax.random.normal(key, shape, jnp.float32)
    if cuts:
        values = values * steps_of(key, shape, cuts, -0.22, 0.18)
    return jnp.clip(values, -bound, bound).astype(kind)


def setup_inputs(seed: int = 0) -> dict:
    streams_of = jax.random.split(jax.random.key(seed), 8)
    positions = draw_positions(jax.random.fold_in(streams_of[7], 71), 0)
    features = noise(streams_of[1], (N_GX, N_GY, N_GZ, TPD, ATOMS, CH), 1.0, 6.0, ((0, 2), (1, 4), (2, 4)))
    counts = draw_counts(jax.random.fold_in(streams_of[7], 71), 0)
    neighbours = draw_neighbours(jax.random.fold_in(streams_of[7], 71), 0)
    mix_weight = noise(streams_of[4], (2 * RAD * CH, CH), (2 * RAD * CH) ** -0.5, 0.1875)
    readout = noise(streams_of[5], (CH,), 1.0, 4.0, (), jnp.float32)
    radial_rates = jnp.clip(jnp.exp(jax.random.uniform(streams_of[6], (RAD,), jnp.float32, math.log(0.03), math.log(0.6))), 0.03, 0.6)
    return {"positions": positions, "features": features, "counts": counts, "neighbours": neighbours, "mix_weight": mix_weight, "readout": readout, "radial_rates": radial_rates}


def build_basis(own_points, other_points, decay_rates):
    offset = other_points[None, :, :] - jnp.transpose(own_points)[:, :, None]
    square_dist = jnp.sum(offset * offset, axis=1)
    radial = jnp.exp(-decay_rates[None, :, None] * square_dist[:, None, :])
    pair_basis = jnp.concatenate([radial[:, :, None, :], radial[:, :, None, :] * offset[:, None, :, :]], axis=2)
    return offset, radial, pair_basis


def device_terms(own_points, own_valid, own_counts, near_points, near_features, neighbour_rows, mixing, readout, decay_rates):
    tile_count = own_points.shape[0]
    atom_count = own_points.shape[2]
    channel_count = near_features.shape[2]
    slot_count = neighbour_rows.shape[1]
    radial_count = decay_rates.shape[0]
    basis_count = 4 * radial_count
    scaling = (slot_count * atom_count) ** -0.5
    pair_count = tile_count * slot_count
    row_width = (3 + channel_count) * atom_count

    def locate(pair_index):
        tile_index = pair_index // slot_count
        slot_index = pair_index % slot_count
        target = neighbour_rows[tile_index, slot_index]
        is_live = target >= 0
        source_index = jnp.maximum(target, 0)
        return tile_index, source_index, is_live

    def forward_pair(pair_index, summed):
        tile_index, source_index, is_live = locate(pair_index)
        near_tile = jnp.where(is_live, near_features[source_index], jnp.zeros((), jnp.bfloat16))
        offset, radial, pair_basis = build_basis(own_points[tile_index], near_points[source_index], decay_rates)
        flat_basis = pair_basis.reshape(atom_count * basis_count, atom_count).astype(jnp.bfloat16)
        contribution = jnp.dot(flat_basis, near_tile, preferred_element_type=jnp.float32)
        return lax.dynamic_update_index_in_dim(summed, summed[tile_index] + contribution, tile_index, 0)

    summed = lax.fori_loop(0, pair_count, forward_pair, jnp.zeros((tile_count, atom_count * basis_count, channel_count), jnp.float32))
    scaled_sum = summed.reshape(tile_count, atom_count, radial_count, 4, channel_count) * scaling
    scalar_part = scaled_sum[:, :, :, 0, :]
    vector_norm = jnp.sum(scaled_sum[:, :, :, 1:, :] * scaled_sum[:, :, :, 1:, :], axis=3)
    invariant = jnp.concatenate([scalar_part, vector_norm], axis=2).reshape(tile_count * atom_count, 2 * radial_count * channel_count).astype(jnp.bfloat16)
    preact = jnp.dot(invariant, mixing, preferred_element_type=jnp.float32)
    sigmoid_value = jax.nn.sigmoid(preact)
    grad_pre = (own_valid.reshape(-1, 1) * readout[None, :] * sigmoid_value * (1.0 + preact * (1.0 - sigmoid_value))).astype(jnp.bfloat16)
    grad_invariant = lax.dot_general(grad_pre, mixing, (((1,), (1,)), ((), ())), preferred_element_type=jnp.float32)
    grad_invariant = grad_invariant.reshape(tile_count, atom_count, 2, radial_count, channel_count)
    grad_sum = jnp.concatenate([grad_invariant[:, :, 0, :, None, :], 2.0 * scaled_sum[:, :, :, 1:, :] * grad_invariant[:, :, 1, :, None, :]], axis=3) * scaling
    grad_sum = grad_sum.reshape(tile_count, atom_count * basis_count, channel_count).astype(jnp.bfloat16)

    def backward_pair(pair_index, state_pair):
        own_force, ghost_sum = state_pair
        tile_index, source_index, is_live = locate(pair_index)
        near_tile = jnp.where(is_live, near_features[source_index], jnp.zeros((), jnp.bfloat16))
        offset, radial, pair_basis = build_basis(own_points[tile_index], near_points[source_index], decay_rates)
        flat_basis = pair_basis.reshape(atom_count * basis_count, atom_count).astype(jnp.bfloat16)
        seed_rows = grad_sum[tile_index]
        grad_basis = lax.dot_general(seed_rows, near_tile, (((1,), (1,)), ((), ())), preferred_element_type=jnp.float32)
        grad_basis = grad_basis.reshape(atom_count, radial_count, 4, atom_count)
        grad_near = lax.dot_general(flat_basis, seed_rows, (((0,), (0,)), ((), ())), preferred_element_type=jnp.float32)
        inner_term = grad_basis[:, :, 0, :] + jnp.sum(grad_basis[:, :, 1:, :] * offset[:, None, :, :], axis=2)
        pair_force = jnp.sum(radial[:, :, None, :] * (grad_basis[:, :, 1:, :] - 2.0 * decay_rates[None, :, None, None] * offset[:, None, :, :] * inner_term[:, :, None, :]), axis=1)
        own_part = jnp.transpose(jnp.sum(pair_force, axis=2))
        ghost_part = jnp.concatenate([-jnp.sum(pair_force, axis=0).reshape(-1), grad_near.reshape(-1)]) * is_live.astype(jnp.float32)
        own_force = lax.dynamic_update_index_in_dim(own_force, own_force[tile_index] + own_part, tile_index, 0)
        ghost_sum = lax.dynamic_update_index_in_dim(ghost_sum, ghost_sum[source_index] + ghost_part, source_index, 0)
        return own_force, ghost_sum

    start_pair = (jnp.zeros((tile_count, 3, atom_count), jnp.float32), jnp.zeros((27 * tile_count, row_width), jnp.float32))
    return lax.fori_loop(0, pair_count, backward_pair, start_pair)


def reference(positions, features, counts, neighbours, mix_weight, readout, radial_rates):
    device_total = N_GX * N_GY * N_GZ
    row_width = (3 + CH) * ATOMS
    is_valid = lax.broadcasted_iota(jnp.int32, counts.shape + (ATOMS,), 4) < counts[..., None]
    valid_float = is_valid.astype(jnp.float32)
    masked = jnp.where(is_valid[..., None], features, jnp.zeros((), jnp.bfloat16))
    edge_pad = ((1, 1), (1, 1), (1, 1), (0, 0), (0, 0), (0, 0))
    padded_points = jnp.pad(positions, edge_pad)
    padded_features = jnp.pad(masked, edge_pad)
    flat_points = positions.reshape(device_total, TPD, 3, ATOMS)
    flat_valid = valid_float.reshape(device_total, TPD, ATOMS)
    flat_counts = counts.reshape(device_total, TPD)
    flat_rows = neighbours.reshape(device_total, TPD, NBR)
    zero_index = jnp.zeros((), jnp.int32)

    def device_step(totals, device_flat):
        coord_x = (device_flat // (N_GY * N_GZ)).astype(jnp.int32)
        coord_y = ((device_flat // N_GZ) % N_GY).astype(jnp.int32)
        coord_z = (device_flat % N_GZ).astype(jnp.int32)
        near_points = lax.dynamic_slice(padded_points, (coord_x, coord_y, coord_z, zero_index, zero_index, zero_index), (3, 3, 3, TPD, 3, ATOMS)).reshape(27 * TPD, 3, ATOMS)
        near_features = lax.dynamic_slice(padded_features, (coord_x, coord_y, coord_z, zero_index, zero_index, zero_index), (3, 3, 3, TPD, ATOMS, CH)).reshape(27 * TPD, ATOMS, CH)
        own_force, ghost_sum = device_terms(flat_points[device_flat], flat_valid[device_flat], flat_counts[device_flat], near_points, near_features, flat_rows[device_flat], mix_weight, readout, radial_rates)
        start = (coord_x, coord_y, coord_z, zero_index, zero_index)
        region = lax.dynamic_slice(totals, start, (3, 3, 3, TPD, row_width)) + ghost_sum.reshape(3, 3, 3, TPD, row_width)
        return lax.dynamic_update_slice(totals, region, start), own_force

    totals = jnp.zeros((N_GX + 2, N_GY + 2, N_GZ + 2, TPD, row_width), jnp.float32)
    totals, own_forces = lax.scan(device_step, totals, jnp.arange(device_total, dtype=jnp.int32))
    interior = totals[1:-1, 1:-1, 1:-1]
    forces = own_forces.reshape(N_GX, N_GY, N_GZ, TPD, 3, ATOMS) + interior[..., :3 * ATOMS].reshape(N_GX, N_GY, N_GZ, TPD, 3, ATOMS)
    feature_grads = interior[..., 3 * ATOMS:].reshape(N_GX, N_GY, N_GZ, TPD, ATOMS, CH) * valid_float[..., None]
    return forces, feature_grads
```

```python
import functools

import jax
import jax.numpy as jnp
from jax import lax
from jax.experimental import pallas as pl
from jax.experimental.pallas import tpu as pltpu
from jax.sharding import PartitionSpec as P

ROWS = 32
EXTRA = 8
NT = (((1,), (1,)), ((), ()))


def swaps(axis):
    count = lax.axis_size(axis)
    result = []
    for first in (0, 1):
        pairs = [(i, i + 1) for i in range(first, count - 1, 2)]
        if pairs:
            result.append(pairs + [(b, a) for a, b in pairs])
    return result


def place(step, axis):
    side = jnp.where((step == 1) == (lax.axis_index(axis) % 2 == 0), 1, 2)
    return jnp.minimum(jnp.where(step == 0, 0, side), len(swaps(axis)))


def pack_kernel(counts_ref, features_ref, points_ref, packed_ref, extra_ref):
    tiles, atoms, _ = features_ref.shape
    for t in range(tiles):
        count = counts_ref[t]
        rows = lax.broadcasted_iota(jnp.int32, features_ref.shape[1:], 0)
        values = features_ref[t].astype(jnp.float32)
        packed_ref[t, :atoms] = jnp.where(rows < count, values, 0.0).astype(jnp.bfloat16)
        rest = points_ref[t]
        extra_ref[...] = jnp.zeros_like(extra_ref)
        for term in range(3):
            part = rest.astype(jnp.bfloat16).astype(jnp.float32)
            extra_ref[3 * term : 3 * term + 3] = part
            rest = rest - part
        packed_ref[t, atoms:] = extra_ref[...].astype(jnp.bfloat16)


def main_kernel(
    planes,
    slots,
    counts_ref,
    index_ref,
    live_ref,
    rates_ref,
    points_ref,
    mixing_ref,
    readout_ref,
    *refs,
):
    plane_refs = refs[:planes]
    ghost_refs = refs[planes : 2 * planes]
    (
        near_ref,
        own_ref,
        basis_ref,
        radial_ref,
        pair_features_ref,
        sum_ref,
        seed_ref,
        seed_t_ref,
        grad_ref,
        near_grad_ref,
        near_force_ref,
        own_force_ref,
        ghost_ref,
        in_sems,
        out_sems,
    ) = refs[2 * planes :]
    tiles, _, atoms = points_ref.shape
    channels = readout_ref.shape[1]
    radials = rates_ref.shape[0]
    bases = 4 * radials
    chunk_rows = bases * ROWS
    couples = slots // 2
    plane_tiles = plane_refs[0].shape[0]
    scaling = (slots * atoms) ** (-0.5)

    loads = [
        pltpu.make_async_copy(
            plane_refs[k], near_ref.at[pl.ds(k * plane_tiles, plane_tiles)], in_sems.at[k]
        )
        for k in range(planes)
    ]
    for load in loads:
        load.start()

    for t in range(tiles):
        for m in range(3):
            line = points_ref[t, m : m + 1, :]
            own_ref[t, m] = jnp.transpose(jnp.broadcast_to(line, (atoms, atoms)))
    ghost_ref[...] = jnp.zeros_like(ghost_ref)
    own_force_ref[...] = jnp.zeros_like(own_force_ref)
    sum_ref[...] = jnp.zeros_like(sum_ref)

    for load in loads:
        load.wait()

    def near_points(tile):
        extra = near_ref[tile, atoms:, :].astype(jnp.float32)
        total = extra[0:3] + extra[3:6] + extra[6:9]
        return [total[m : m + 1, :] for m in range(3)]

    def members(t, couple):
        first = t * slots + 2 * couple
        return index_ref[first], index_ref[first + 1], 2 * couple + 1 < live_ref[t]

    rates = [rates_ref[r] for r in range(radials)]

    for t in range(tiles):
        count = counts_ref[t]
        chunks = (count + (ROWS - 1)) // ROWS
        active = jnp.where(count > 0, (live_ref[t] + 1) // 2, 0)

        def forward(couple, carry, t=t, chunks=chunks):
            one, two, both = members(t, couple)
            slot = t * couples + couple
            pair_features_ref[slot, :atoms] = near_ref[one, :atoms, :]
            second = near_ref[two, :atoms, :]
            pair_features_ref[slot, atoms:] = jnp.where(both, second, jnp.zeros_like(second))
            points = (near_points(one), near_points(two))

            def chunk_step(chunk, carry):
                start = pl.multiple_of(chunk * ROWS, ROWS)
                base = pl.multiple_of(chunk * chunk_rows, chunk_rows)
                for half in range(2):
                    lanes = slice(half * atoms, (half + 1) * atoms)
                    for sub in range(0, ROWS, 16):
                        offset = [
                            points[half][m] - own_ref[t, m, pl.ds(start + sub, 16), :]
                            for m in range(3)
                        ]
                        square = (
                            offset[0] * offset[0] + offset[1] * offset[1] + offset[2] * offset[2]
                        )
                        for r in range(radials):
                            radial = jnp.exp(-rates[r] * square)
                            radial_ref[slot, half, r, pl.ds(start + sub, 16), :] = radial
                            for m in range(4):
                                value = radial if m == 0 else radial * offset[m - 1]
                                row = base + (4 * r + m) * ROWS + sub
                                basis_ref[slot, pl.ds(row, 16), lanes] = value.astype(jnp.bfloat16)
                sum_ref[t, pl.ds(base, chunk_rows), :] += jnp.dot(
                    basis_ref[slot, pl.ds(base, chunk_rows), :],
                    pair_features_ref[slot],
                    preferred_element_type=jnp.float32,
                )
                return carry

            return lax.fori_loop(0, chunks, chunk_step, carry)

        lax.fori_loop(0, active, forward, 0)

        def middle(chunk, carry, t=t, count=count):
            base = pl.multiple_of(chunk * chunk_rows, chunk_rows)
            parts = []
            norms = []
            for r in range(radials):
                for m in range(4):
                    value = sum_ref[t, pl.ds(base + (4 * r + m) * ROWS, ROWS), :] * scaling
                    if m == 0:
                        parts.append(value)
                    elif m == 1:
                        norm = value * value
                    else:
                        norm = norm + value * value
                norms.append(norm)
            invariant = jnp.concatenate(parts + norms, axis=1).astype(jnp.bfloat16)
            preact = jnp.dot(invariant, mixing_ref[...], preferred_element_type=jnp.float32)
            sigmoid = jax.nn.sigmoid(preact)
            row = lax.broadcasted_iota(jnp.int32, (ROWS, channels), 0) + chunk * ROWS
            valid = (row < count).astype(jnp.float32)
            grad_pre = valid * readout_ref[...] * sigmoid * (1.0 + preact * (1.0 - sigmoid))
            grad = lax.dot_general(
                grad_pre.astype(jnp.bfloat16),
                mixing_ref[...],
                NT,
                preferred_element_type=jnp.float32,
            )
            for r in range(radials):
                scalar = grad[:, r * channels : (r + 1) * channels]
                square = grad[:, (radials + r) * channels : (radials + r + 1) * channels]
                for m in range(4):
                    row = base + (4 * r + m) * ROWS
                    if m == 0:
                        value = scalar * scaling
                    else:
                        value = sum_ref[t, pl.ds(row, ROWS), :] * scaling
                        value = 2.0 * value * square * scaling
                    value = value.astype(jnp.bfloat16)
                    seed_ref[t, pl.ds(row, ROWS), :] = value
            seed_t_ref[t, chunk] = jnp.transpose(seed_ref[t, pl.ds(base, chunk_rows), :])
            return carry

        lax.fori_loop(0, jnp.where(count > 0, chunks, 0), middle, 0)

        def backward(couple, carry, t=t, chunks=chunks):
            one, two, both = members(t, couple)
            slot = t * couples + couple
            points = (near_points(one), near_points(two))
            near_grad_ref[...] = jnp.zeros_like(near_grad_ref)
            near_force_ref[...] = jnp.zeros_like(near_force_ref)

            def chunk_step(chunk, carry):
                start = pl.multiple_of(chunk * ROWS, ROWS)
                base = pl.multiple_of(chunk * chunk_rows, chunk_rows)
                grad_ref[...] = lax.dot_general(
                    seed_ref[t, pl.ds(base, chunk_rows), :],
                    pair_features_ref[slot],
                    NT,
                    preferred_element_type=jnp.float32,
                )
                near_grad_ref[...] += jnp.dot(
                    seed_t_ref[t, chunk],
                    basis_ref[slot, pl.ds(base, chunk_rows), :],
                    preferred_element_type=jnp.float32,
                )
                for half in range(2):
                    lanes = slice(half * atoms, (half + 1) * atoms)
                    pulled = [None] * 3
                    for sub in range(0, ROWS, 8):
                        where = pl.ds(start + sub, 8)
                        offset = [points[half][m] - own_ref[t, m, where, :] for m in range(3)]
                        direct = [None] * 4
                        decayed = [None] * 4
                        for r in range(radials):
                            radial = radial_ref[slot, half, r, where, :]
                            steep = radial * (2.0 * rates[r])
                            for m in range(4):
                                row = (4 * r + m) * ROWS + sub
                                grad = grad_ref[row : row + 8, lanes]
                                if m > 0:
                                    part = radial * grad
                                    direct[m] = part if r == 0 else direct[m] + part
                                part = steep * grad
                                decayed[m] = part if r == 0 else decayed[m] + part
                        inner = decayed[0]
                        for m in range(3):
                            inner = inner + decayed[m + 1] * offset[m]
                        for m in range(3):
                            force = direct[m + 1] - offset[m] * inner
                            own_force_ref[t, m, where, :] += force
                            pulled[m] = force if sub == 0 else pulled[m] + force
                    for m in range(3):
                        near_force_ref[half, m] += pulled[m]
                return carry

            lax.fori_loop(0, chunks, chunk_step, 0)

            def give(half, tile):
                lanes = slice(half * atoms, (half + 1) * atoms)
                ghost_ref[tile, :channels, :] += near_grad_ref[:, lanes]
                for m in range(3):
                    ghost_ref[tile, channels + m : channels + m + 1, :] -= jnp.sum(
                        near_force_ref[half, m], axis=0, keepdims=True
                    )

            give(0, one)

            @pl.when(both)
            def _():
                give(1, two)

            return carry

        lax.fori_loop(0, active, backward, 0)
        for m in range(3):
            ghost_ref[t, channels + m : channels + m + 1, :] += jnp.sum(
                jnp.transpose(own_force_ref[t, m]), axis=0, keepdims=True
            )

    stores = [
        pltpu.make_async_copy(
            ghost_ref.at[pl.ds(k * plane_tiles, plane_tiles)], ghost_refs[k], out_sems.at[k]
        )
        for k in range(planes)
    ]
    for store in stores:
        store.start()
    for store in stores:
        store.wait()


def final_kernel(counts_ref, *refs):
    part_refs = refs[:-2]
    forces_ref, grads_ref = refs[-2:]
    tiles, channels, atoms = grads_ref.shape
    for t in range(tiles):
        total = part_refs[0][t]
        for part in part_refs[1:]:
            total = total + part[t]
        forces_ref[t] = total[channels : channels + 3]
        column = lax.broadcasted_iota(jnp.int32, (channels, atoms), 1)
        masked = jnp.where(column < counts_ref[t], total[:channels], 0.0)
        grads_ref[t] = jnp.transpose(masked)


def body(positions, features, counts, neighbours, mix_weight, readout, radial_rates):
    tiles, atoms = positions.shape[3], positions.shape[5]
    channels = features.shape[5]
    slots = neighbours.shape[4]
    radials = radial_rates.shape[0]
    vmem = pl.BlockSpec(memory_space=pltpu.VMEM)
    smem = pl.BlockSpec(memory_space=pltpu.SMEM)
    hbm = pl.BlockSpec(memory_space=pl.ANY)

    own_counts = counts.reshape(tiles)
    points = positions.reshape(tiles, 3, atoms)
    packed = pl.pallas_call(
        pack_kernel,
        out_shape=jax.ShapeDtypeStruct((tiles, atoms + 16, channels), jnp.bfloat16),
        in_specs=[smem, vmem, vmem],
        out_specs=vmem,
        scratch_shapes=[pltpu.VMEM((16, channels), jnp.float32)],
        name="pack",
    )(own_counts, features.reshape(tiles, atoms, channels), points)

    block = packed
    for axis in ("gz", "gy"):
        parts = [block] + [lax.ppermute(block, axis, pairs) for pairs in swaps(axis)]
        block = jnp.concatenate(parts, axis=0)
    planes = [block] + [lax.ppermute(block, "gx", pairs) for pairs in swaps("gx")]

    rows = neighbours.reshape(tiles, slots)
    live = jnp.sum((rows >= 0).astype(jnp.int32), axis=1)
    target = jnp.maximum(rows, 0)
    step = target // tiles
    spot = place(step // 9 - 1, "gx")
    spot = spot * (len(swaps("gy")) + 1) + place(step // 3 % 3 - 1, "gy")
    spot = spot * (len(swaps("gz")) + 1) + place(step % 3 - 1, "gz")
    index = spot * tiles + target % tiles
    if slots % 2:
        index = jnp.pad(index, ((0, 0), (0, 1)))
    even_slots = slots + slots % 2

    count = len(planes)
    plane_tiles = block.shape[0]
    total = count * plane_tiles
    couples = even_slots // 2
    bases = 4 * radials
    chunks = atoms // ROWS
    ghost_rows = channels + EXTRA
    ghosts = pl.pallas_call(
        functools.partial(main_kernel, count, even_slots),
        out_shape=[jax.ShapeDtypeStruct((plane_tiles, ghost_rows, atoms), jnp.float32)] * count,
        in_specs=[smem] * 4 + [vmem] * 3 + [hbm] * count,
        out_specs=[hbm] * count,
        scratch_shapes=[
            pltpu.VMEM((total, atoms + 16, channels), jnp.bfloat16),
            pltpu.VMEM((tiles, 3, atoms, atoms), jnp.float32),
            pltpu.VMEM((tiles * couples, bases * atoms, 2 * atoms), jnp.bfloat16),
            pltpu.VMEM((tiles * couples, 2, radials, atoms, atoms), jnp.float32),
            pltpu.VMEM((tiles * couples, 2 * atoms, channels), jnp.bfloat16),
            pltpu.VMEM((tiles, bases * atoms, channels), jnp.float32),
            pltpu.VMEM((tiles, bases * atoms, channels), jnp.bfloat16),
            pltpu.VMEM((tiles, chunks, channels, bases * ROWS), jnp.bfloat16),
            pltpu.VMEM((bases * ROWS, 2 * atoms), jnp.float32),
            pltpu.VMEM((channels, 2 * atoms), jnp.float32),
            pltpu.VMEM((2, 3, 8, atoms), jnp.float32),
            pltpu.VMEM((tiles, 3, atoms, atoms), jnp.float32),
            pltpu.VMEM((total, ghost_rows, atoms), jnp.float32),
            pltpu.SemaphoreType.DMA((count,)),
            pltpu.SemaphoreType.DMA((count,)),
        ],
        name="pairs",
    )(
        own_counts,
        index.reshape(-1),
        live,
        radial_rates,
        points,
        mix_weight,
        readout.reshape(1, channels),
        *planes,
    )

    folded = ghosts[0]
    for ghost, pairs in zip(ghosts[1:], swaps("gx")):
        folded = folded + lax.ppermute(ghost, "gx", pairs)
    sides = len(swaps("gy")) + 1
    folded = folded.reshape(sides, plane_tiles // sides, ghost_rows, atoms)
    total_part = folded[0]
    for k, pairs in enumerate(swaps("gy")):
        total_part = total_part + lax.ppermute(folded[k + 1], "gy", pairs)
    sides = len(swaps("gz")) + 1
    folded = total_part.reshape(sides, tiles, ghost_rows, atoms)
    parts = [folded[0]]
    for k, pairs in enumerate(swaps("gz")):
        parts.append(lax.ppermute(folded[k + 1], "gz", pairs))

    forces, grads = pl.pallas_call(
        final_kernel,
        out_shape=[
            jax.ShapeDtypeStruct((tiles, 3, atoms), jnp.float32),
            jax.ShapeDtypeStruct((tiles, channels, atoms), jnp.float32),
        ],
        in_specs=[smem] + [vmem] * len(parts),
        out_specs=[vmem, vmem],
        name="finish",
    )(own_counts, *parts)
    return (
        forces.reshape(1, 1, 1, tiles, 3, atoms),
        grads.reshape(1, 1, 1, tiles, atoms, channels),
    )


def solution(mesh):
    in_specs = (
        P("gx", "gy", "gz", None, None, None),
        P("gx", "gy", "gz", None, None, None),
        P("gx", "gy", "gz", None),
        P("gx", "gy", "gz", None, None),
        P(),
        P(),
        P(),
    )
    out_specs = (P("gx", "gy", "gz", None, None, None), P("gx", "gy", "gz", None, None, None))
    return jax.shard_map(body, mesh=mesh, in_specs=in_specs, out_specs=out_specs, check_vma=False)
```

```python
import functools

import jax
import jax.numpy as jnp
from jax import lax
from jax.experimental import pallas as pl
from jax.experimental.pallas import tpu as pltpu
from jax.sharding import PartitionSpec as P

ROWS = 32
EXTRA = 8
SMALL = 8 << 20
LARGE = 30 << 20
NT = (((1,), (1,)), ((), ()))


def swaps(axis):
    count = lax.axis_size(axis)
    result = []
    for first in (0, 1):
        pairs = [(i, i + 1) for i in range(first, count - 1, 2)]
        if pairs:
            result.append(pairs + [(b, a) for a, b in pairs])
    return result


def side_of(step, parity, sides):
    side = jnp.where((step == 1) == (parity == 0), 1, 2)
    return jnp.minimum(jnp.where(step == 0, 0, side), sides)


def pack_kernel(counts_ref, features_ref, points_ref, packed_ref, extra_ref):
    tiles, atoms, _ = features_ref.shape
    for t in range(tiles):
        count = counts_ref[t]
        rows = lax.broadcasted_iota(jnp.int32, features_ref.shape[1:], 0)
        values = features_ref[t].astype(jnp.float32)
        packed_ref[t, :atoms] = jnp.where(rows < count, values, 0.0).astype(jnp.bfloat16)
        rest = points_ref[:, t, :]
        extra_ref[...] = jnp.zeros_like(extra_ref)
        for term in range(3):
            part = rest.astype(jnp.bfloat16).astype(jnp.float32)
            extra_ref[3 * term : 3 * term + 3] = part
            rest = rest - part
        packed_ref[t, atoms:] = extra_ref[...].astype(jnp.bfloat16)


def join_kernel(groups, *refs):
    inputs = refs[: -len(groups)]
    for group, out_ref in zip(groups, refs[-len(groups) :]):
        at = 0
        for k in group:
            count = inputs[k].shape[0]
            out_ref[at : at + count] = inputs[k][...]
            at += count


def join(groups, *arrays):
    shapes = [
        jax.ShapeDtypeStruct(
            (sum(arrays[k].shape[0] for k in group),) + arrays[0].shape[1:], arrays[0].dtype
        )
        for group in groups
    ]
    vmem = pl.BlockSpec(memory_space=pltpu.VMEM)
    return pl.pallas_call(
        functools.partial(join_kernel, groups),
        out_shape=shapes,
        in_specs=[vmem] * len(arrays),
        out_specs=[vmem] * len(groups),
        compiler_params=pltpu.CompilerParams(vmem_limit_bytes=SMALL),
        name="join",
    )(*arrays)


def fold_kernel(cuts, count, *refs):
    outs = refs[count:]
    at = 0
    for (source, low, high), out_ref in zip(cuts, outs):
        value = None
        for ref, start in zip(refs[:count], source):
            if start is None:
                continue
            part = ref[low - start : high - start]
            value = part if value is None else value + part
        out_ref[...] = value


def fold(cuts, *arrays):
    shapes = [
        jax.ShapeDtypeStruct((high - low,) + arrays[0].shape[1:], arrays[0].dtype)
        for _, low, high in cuts
    ]
    vmem = pl.BlockSpec(memory_space=pltpu.VMEM)
    return pl.pallas_call(
        functools.partial(fold_kernel, cuts, len(arrays)),
        out_shape=shapes,
        in_specs=[vmem] * len(arrays),
        out_specs=[vmem] * len(cuts),
        compiler_params=pltpu.CompilerParams(vmem_limit_bytes=SMALL),
        name="fold",
    )(*arrays)


def main_kernel(
    pieces,
    sides,
    slots,
    axis_ref,
    counts_ref,
    neighbours_ref,
    rates_ref,
    points_ref,
    mixing_ref,
    readout_ref,
    *refs,
):
    piece_refs = refs[:pieces]
    ghost_refs = refs[pieces : 2 * pieces]
    (
        near_ref,
        own_ref,
        basis_ref,
        radial_ref,
        pair_features_ref,
        sum_ref,
        seed_ref,
        seed_t_ref,
        grad_ref,
        near_grad_ref,
        near_force_ref,
        own_force_ref,
        ghost_ref,
        in_sems,
        out_sems,
    ) = refs[2 * pieces :]
    _, tiles, atoms = points_ref.shape
    channels = readout_ref.shape[1]
    radials = rates_ref.shape[0]
    bases = 4 * radials
    chunk_rows = bases * ROWS
    couples = (slots + 1) // 2
    scaling = (slots * atoms) ** (-0.5)
    starts = [sum(ref.shape[0] for ref in piece_refs[:k]) for k in range(pieces)]
    cross = 1 + sides[1] + sides[2]
    blocks = (sides[1] + 1) * (sides[2] + 1)

    loads = [
        pltpu.make_async_copy(
            piece_refs[k], near_ref.at[pl.ds(starts[k], piece_refs[k].shape[0])], in_sems.at[k]
        )
        for k in range(pieces)
    ]
    for load in loads:
        load.start()

    for t in range(tiles):
        for m in range(3):
            line = points_ref[m, t : t + 1, :]
            own_ref[t, m] = jnp.transpose(jnp.broadcast_to(line, (atoms, atoms)))
    ghost_ref[...] = jnp.zeros_like(ghost_ref)
    own_force_ref[...] = jnp.zeros_like(own_force_ref)
    sum_ref[...] = jnp.zeros_like(sum_ref)

    for load in loads:
        load.wait()

    def near_points(tile):
        extra = near_ref[tile, atoms:, :].astype(jnp.float32)
        total = extra[0:3] + extra[3:6] + extra[6:9]
        return [total[m : m + 1, :] for m in range(3)]

    def located(target):
        target = jnp.maximum(target, 0)
        block = lax.div(target, tiles)
        steps = (lax.div(block, 9), lax.rem(lax.div(block, 3), 3), lax.rem(block, 3))
        x, y, z = (side_of(steps[k] - 1, axis_ref[k], sides[k]) for k in range(3))
        diagonal = cross + (y - 1) * sides[2] + (z - 1)
        straight = jnp.where(y == 0, z, sides[2] + y)
        block = jnp.where((y > 0) & (z > 0), diagonal, straight)
        return (x * blocks + block) * tiles + lax.rem(target, tiles)

    def members(t, couple):
        first = t * slots + 2 * couple
        last = jnp.minimum(first + 1, (t + 1) * slots - 1)
        one, two = neighbours_ref[first], neighbours_ref[last]
        return located(one), located(two), (two >= 0) & (last > first)

    rates = [rates_ref[r] for r in range(radials)]

    for t in range(tiles):
        count = counts_ref[t]
        chunks = (count + (ROWS - 1)) // ROWS
        live = 0
        for k in range(slots):
            live = live + jnp.where(neighbours_ref[t * slots + k] >= 0, 1, 0)
        active = jnp.where(count > 0, (live + 1) // 2, 0)

        def forward(couple, carry, t=t, chunks=chunks):
            one, two, both = members(t, couple)
            slot = t * couples + couple
            pair_features_ref[slot, :atoms] = near_ref[one, :atoms, :]
            second = near_ref[two, :atoms, :]
            pair_features_ref[slot, atoms:] = jnp.where(both, second, jnp.zeros_like(second))
            points = (near_points(one), near_points(two))

            def chunk_step(chunk, carry):
                start = pl.multiple_of(chunk * ROWS, ROWS)
                base = pl.multiple_of(chunk * chunk_rows, chunk_rows)
                for half in range(2):
                    lanes = slice(half * atoms, (half + 1) * atoms)
                    for sub in range(0, ROWS, 16):
                        offset = [
                            points[half][m] - own_ref[t, m, pl.ds(start + sub, 16), :]
                            for m in range(3)
                        ]
                        square = (
                            offset[0] * offset[0] + offset[1] * offset[1] + offset[2] * offset[2]
                        )
                        for r in range(radials):
                            radial = jnp.exp(-rates[r] * square)
                            radial_ref[slot, half, r, pl.ds(start + sub, 16), :] = radial
                            for m in range(4):
                                value = radial if m == 0 else radial * offset[m - 1]
                                row = base + (4 * r + m) * ROWS + sub
                                basis_ref[slot, pl.ds(row, 16), lanes] = value.astype(jnp.bfloat16)
                sum_ref[t, pl.ds(base, chunk_rows), :] += jnp.dot(
                    basis_ref[slot, pl.ds(base, chunk_rows), :],
                    pair_features_ref[slot],
                    preferred_element_type=jnp.float32,
                )
                return carry

            return lax.fori_loop(0, chunks, chunk_step, carry)

        lax.fori_loop(0, active, forward, 0)

        def middle(chunk, carry, t=t, count=count):
            base = pl.multiple_of(chunk * chunk_rows, chunk_rows)
            parts = []
            norms = []
            for r in range(radials):
                for m in range(4):
                    value = sum_ref[t, pl.ds(base + (4 * r + m) * ROWS, ROWS), :] * scaling
                    if m == 0:
                        parts.append(value)
                    elif m == 1:
                        norm = value * value
                    else:
                        norm = norm + value * value
                norms.append(norm)
            invariant = jnp.concatenate(parts + norms, axis=1).astype(jnp.bfloat16)
            preact = jnp.dot(invariant, mixing_ref[...], preferred_element_type=jnp.float32)
            sigmoid = jax.nn.sigmoid(preact)
            row = lax.broadcasted_iota(jnp.int32, (ROWS, channels), 0) + chunk * ROWS
            valid = (row < count).astype(jnp.float32)
            grad_pre = valid * readout_ref[...] * sigmoid * (1.0 + preact * (1.0 - sigmoid))
            grad = lax.dot_general(
                grad_pre.astype(jnp.bfloat16),
                mixing_ref[...],
                NT,
                preferred_element_type=jnp.float32,
            )
            for r in range(radials):
                scalar = grad[:, r * channels : (r + 1) * channels]
                square = grad[:, (radials + r) * channels : (radials + r + 1) * channels]
                for m in range(4):
                    row = base + (4 * r + m) * ROWS
                    if m == 0:
                        value = scalar * scaling
                    else:
                        value = sum_ref[t, pl.ds(row, ROWS), :] * scaling
                        value = 2.0 * value * square * scaling
                    value = value.astype(jnp.bfloat16)
                    seed_ref[t, pl.ds(row, ROWS), :] = value
            seed_t_ref[t, chunk] = jnp.transpose(seed_ref[t, pl.ds(base, chunk_rows), :])
            return carry

        lax.fori_loop(0, jnp.where(count > 0, chunks, 0), middle, 0)

        def backward(couple, carry, t=t, chunks=chunks):
            one, two, both = members(t, couple)
            slot = t * couples + couple
            points = (near_points(one), near_points(two))
            near_grad_ref[...] = jnp.zeros_like(near_grad_ref)
            near_force_ref[...] = jnp.zeros_like(near_force_ref)

            def chunk_step(chunk, carry):
                start = pl.multiple_of(chunk * ROWS, ROWS)
                base = pl.multiple_of(chunk * chunk_rows, chunk_rows)
                grad_ref[...] = lax.dot_general(
                    seed_ref[t, pl.ds(base, chunk_rows), :],
                    pair_features_ref[slot],
                    NT,
                    preferred_element_type=jnp.float32,
                )
                near_grad_ref[...] += jnp.dot(
                    seed_t_ref[t, chunk],
                    basis_ref[slot, pl.ds(base, chunk_rows), :],
                    preferred_element_type=jnp.float32,
                )
                for half in range(2):
                    lanes = slice(half * atoms, (half + 1) * atoms)
                    pulled = [None] * 3
                    for sub in range(0, ROWS, 8):
                        where = pl.ds(start + sub, 8)
                        offset = [points[half][m] - own_ref[t, m, where, :] for m in range(3)]
                        direct = [None] * 4
                        decayed = [None] * 4
                        for r in range(radials):
                            radial = radial_ref[slot, half, r, where, :]
                            steep = radial * (2.0 * rates[r])
                            for m in range(4):
                                row = (4 * r + m) * ROWS + sub
                                grad = grad_ref[row : row + 8, lanes]
                                if m > 0:
                                    part = radial * grad
                                    direct[m] = part if r == 0 else direct[m] + part
                                part = steep * grad
                                decayed[m] = part if r == 0 else decayed[m] + part
                        inner = decayed[0]
                        for m in range(3):
                            inner = inner + decayed[m + 1] * offset[m]
                        for m in range(3):
                            force = direct[m + 1] - offset[m] * inner
                            own_force_ref[t, m, where, :] += force
                            pulled[m] = force if sub == 0 else pulled[m] + force
                    for m in range(3):
                        near_force_ref[half, m] += pulled[m]
                return carry

            lax.fori_loop(0, chunks, chunk_step, 0)

            def give(half, tile):
                lanes = slice(half * atoms, (half + 1) * atoms)
                ghost_ref[tile, :channels, :] += near_grad_ref[:, lanes]
                for m in range(3):
                    ghost_ref[tile, channels + m : channels + m + 1, :] -= jnp.sum(
                        near_force_ref[half, m], axis=0, keepdims=True
                    )

            give(0, one)

            @pl.when(both)
            def _():
                give(1, two)

            return carry

        lax.fori_loop(0, active, backward, 0)
        for m in range(3):
            ghost_ref[t, channels + m : channels + m + 1, :] += jnp.sum(
                jnp.transpose(own_force_ref[t, m]), axis=0, keepdims=True
            )

    stores = [
        pltpu.make_async_copy(
            ghost_ref.at[pl.ds(starts[k], piece_refs[k].shape[0])], ghost_refs[k], out_sems.at[k]
        )
        for k in range(pieces)
    ]
    for store in stores:
        store.start()
    for store in stores:
        store.wait()


def final_kernel(counts_ref, *refs):
    part_refs = refs[:-2]
    forces_ref, grads_ref = refs[-2:]
    tiles, channels, atoms = grads_ref.shape
    for t in range(tiles):
        total = part_refs[0][t]
        for part in part_refs[1:]:
            total = total + part[t]
        forces_ref[:, t, :] = total[channels : channels + 3]
        column = lax.broadcasted_iota(jnp.int32, (channels, atoms), 1)
        masked = jnp.where(column < counts_ref[t], total[:channels], 0.0)
        grads_ref[t] = jnp.transpose(masked)


def body(positions, features, counts, neighbours, mix_weight, readout, radial_rates):
    tiles, atoms = positions.shape[3], positions.shape[5]
    channels = features.shape[5]
    slots = neighbours.shape[4]
    radials = radial_rates.shape[0]
    vmem = pl.BlockSpec(memory_space=pltpu.VMEM)
    smem = pl.BlockSpec(memory_space=pltpu.SMEM)
    hbm = pl.BlockSpec(memory_space=pl.ANY)
    small = pltpu.CompilerParams(vmem_limit_bytes=SMALL)

    def swap(value, axis):
        return [lax.ppermute(value, axis, pairs) for pairs in swaps(axis)]

    sides = tuple(len(swaps(axis)) for axis in ("gx", "gy", "gz"))
    own_counts = counts.reshape(tiles)
    points = jnp.transpose(positions, (0, 1, 2, 4, 3, 5)).reshape(3, tiles, atoms)
    packed = pl.pallas_call(
        pack_kernel,
        out_shape=jax.ShapeDtypeStruct((tiles, atoms + 16, channels), jnp.bfloat16),
        in_specs=[smem, vmem, vmem],
        out_specs=vmem,
        scratch_shapes=[pltpu.VMEM((16, channels), jnp.float32)],
        compiler_params=small,
        name="pack",
    )(own_counts, features.reshape(tiles, atoms, channels), points)

    along_z = swap(packed, "gz")
    along_y = swap(packed, "gy")
    (line,) = join([list(range(len(along_z)))], *along_z)
    diagonal = swap(line, "gy")
    (cross,) = join([list(range(2 + len(along_y)))], packed, line, *along_y)
    pieces = [[cross] + diagonal]
    for pairs in swaps("gx"):
        pieces.append([lax.ppermute(piece, "gx", pairs) for piece in pieces[0]])
    flat = [piece for plane in pieces for piece in plane]

    total = sum(piece.shape[0] for piece in flat)
    couples = (slots + 1) // 2
    bases = 4 * radials
    chunks = atoms // ROWS
    ghost_rows = channels + EXTRA
    position = jnp.stack([lax.axis_index(axis) % 2 for axis in ("gx", "gy", "gz")])
    ghosts = pl.pallas_call(
        functools.partial(main_kernel, len(flat), sides, slots),
        out_shape=[
            jax.ShapeDtypeStruct((piece.shape[0], ghost_rows, atoms), jnp.float32)
            for piece in flat
        ],
        in_specs=[smem] * 4 + [vmem] * 3 + [hbm] * len(flat),
        out_specs=[hbm] * len(flat),
        scratch_shapes=[
            pltpu.VMEM((total, atoms + 16, channels), jnp.bfloat16),
            pltpu.VMEM((tiles, 3, atoms, atoms), jnp.float32),
            pltpu.VMEM((tiles * couples, bases * atoms, 2 * atoms), jnp.bfloat16),
            pltpu.VMEM((tiles * couples, 2, radials, atoms, atoms), jnp.float32),
            pltpu.VMEM((tiles * couples, 2 * atoms, channels), jnp.bfloat16),
            pltpu.VMEM((tiles, bases * atoms, channels), jnp.float32),
            pltpu.VMEM((tiles, bases * atoms, channels), jnp.bfloat16),
            pltpu.VMEM((tiles, chunks, channels, bases * ROWS), jnp.bfloat16),
            pltpu.VMEM((bases * ROWS, 2 * atoms), jnp.float32),
            pltpu.VMEM((channels, 2 * atoms), jnp.float32),
            pltpu.VMEM((2, 3, 8, atoms), jnp.float32),
            pltpu.VMEM((tiles, 3, atoms, atoms), jnp.float32),
            pltpu.VMEM((total, ghost_rows, atoms), jnp.float32),
            pltpu.SemaphoreType.DMA((len(flat),)),
            pltpu.SemaphoreType.DMA((len(flat),)),
        ],
        compiler_params=pltpu.CompilerParams(vmem_limit_bytes=LARGE),
        name="pairs",
    )(
        position,
        own_counts,
        neighbours.reshape(-1),
        radial_rates,
        points,
        mix_weight,
        readout.reshape(1, channels),
        *flat,
    )

    width = len(pieces[0])
    ghosts = [ghosts[k * width : (k + 1) * width] for k in range(len(pieces))]

    def gather(k):
        arrays = [ghosts[0][k]]
        for plane, pairs in zip(ghosts[1:], swaps("gx")):
            arrays.append(lax.ppermute(plane[k], "gx", pairs))
        return arrays

    diagonal = []
    for k, pairs in enumerate(swaps("gy")):
        arrays = gather(k + 1)
        (value,) = fold([((0,) * len(arrays), 0, arrays[0].shape[0])], *arrays)
        diagonal.append(lax.ppermute(value, "gy", pairs))
    arrays = gather(0)
    line = (sides[2] + 1) * tiles
    cuts = [((0,) * len(arrays), 0, tiles), ((0,) * len(arrays), tiles, line)]
    for k in range(sides[1]):
        cuts.append(((0,) * len(arrays), line + k * tiles, line + (k + 1) * tiles))
    center, along_z, *along_y = fold(cuts, *arrays)
    cuts = [((0,) * (1 + len(diagonal)), k * tiles, (k + 1) * tiles) for k in range(sides[2])]
    along_z = fold(cuts, along_z, *diagonal)
    parts = [center]
    for values, axis in ((along_z, "gz"), (along_y, "gy")):
        for value, pairs in zip(values, swaps(axis)):
            parts.append(lax.ppermute(value, axis, pairs))

    forces, grads = pl.pallas_call(
        final_kernel,
        out_shape=[
            jax.ShapeDtypeStruct((3, tiles, atoms), jnp.float32),
            jax.ShapeDtypeStruct((tiles, channels, atoms), jnp.float32),
        ],
        in_specs=[smem] + [vmem] * len(parts),
        out_specs=[vmem, vmem],
        compiler_params=small,
        name="finish",
    )(own_counts, *parts)
    forces = jnp.transpose(forces.reshape(1, 1, 1, 3, tiles, atoms), (0, 1, 2, 4, 3, 5))
    return forces, grads.reshape(1, 1, 1, tiles, atoms, channels)


def solution(mesh):
    in_specs = (
        P("gx", "gy", "gz", None, None, None),
        P("gx", "gy", "gz", None, None, None),
        P("gx", "gy", "gz", None),
        P("gx", "gy", "gz", None, None),
        P(),
        P(),
        P(),
    )
    out_specs = (P("gx", "gy", "gz", None, None, None), P("gx", "gy", "gz", None, None, None))
    return jax.shard_map(body, mesh=mesh, in_specs=in_specs, out_specs=out_specs, check_vma=False)
```

```python
import functools

import jax
import jax.numpy as jnp
from jax import lax
from jax.experimental import pallas as pl
from jax.experimental.pallas import tpu as pltpu
from jax.sharding import PartitionSpec as P

ROWS = 32
EXTRA = 8
GROUP = 8
LOG2E = 1.4426950408889634
SMALL = 8 << 20
LARGE = 30 << 20
NT = (((1,), (1,)), ((), ()))


def swaps(axis):
    count = lax.axis_size(axis)
    result = []
    for first in (0, 1):
        pairs = [(i, i + 1) for i in range(first, count - 1, 2)]
        if pairs:
            result.append(pairs + [(b, a) for a, b in pairs])
    return result


def side_of(step, parity, sides):
    side = jnp.where((step == 1) == (parity == 0), 1, 2)
    return jnp.minimum(jnp.where(step == 0, 0, side), sides)


def pack_kernel(counts_ref, features_ref, points_ref, packed_ref, extra_ref):
    tiles, atoms, _ = features_ref.shape
    for t in range(tiles):
        count = counts_ref[t]
        rows = lax.broadcasted_iota(jnp.int32, features_ref.shape[1:], 0)
        values = features_ref[t].astype(jnp.float32)
        packed_ref[t, :atoms] = jnp.where(rows < count, values, 0.0).astype(jnp.bfloat16)
        rest = points_ref[:, t, :]
        extra_ref[...] = jnp.zeros_like(extra_ref)
        for term in range(3):
            part = rest.astype(jnp.bfloat16).astype(jnp.float32)
            extra_ref[3 * term : 3 * term + 3] = part
            rest = rest - part
        packed_ref[t, atoms:] = extra_ref[...].astype(jnp.bfloat16)


def join_kernel(groups, *refs):
    inputs = refs[: -len(groups)]
    for group, out_ref in zip(groups, refs[-len(groups) :]):
        at = 0
        for k in group:
            count = inputs[k].shape[0]
            out_ref[at : at + count] = inputs[k][...]
            at += count


def join(groups, *arrays):
    shapes = [
        jax.ShapeDtypeStruct(
            (sum(arrays[k].shape[0] for k in group),) + arrays[0].shape[1:], arrays[0].dtype
        )
        for group in groups
    ]
    vmem = pl.BlockSpec(memory_space=pltpu.VMEM)
    return pl.pallas_call(
        functools.partial(join_kernel, groups),
        out_shape=shapes,
        in_specs=[vmem] * len(arrays),
        out_specs=[vmem] * len(groups),
        compiler_params=pltpu.CompilerParams(vmem_limit_bytes=SMALL),
        name="join",
    )(*arrays)


def fold_kernel(cuts, count, *refs):
    outs = refs[count:]
    at = 0
    for (source, low, high), out_ref in zip(cuts, outs):
        value = None
        for ref, start in zip(refs[:count], source):
            if start is None:
                continue
            part = ref[low - start : high - start]
            value = part if value is None else value + part
        out_ref[...] = value


def fold(cuts, *arrays):
    shapes = [
        jax.ShapeDtypeStruct((high - low,) + arrays[0].shape[1:], arrays[0].dtype)
        for _, low, high in cuts
    ]
    vmem = pl.BlockSpec(memory_space=pltpu.VMEM)
    return pl.pallas_call(
        functools.partial(fold_kernel, cuts, len(arrays)),
        out_shape=shapes,
        in_specs=[vmem] * len(arrays),
        out_specs=[vmem] * len(cuts),
        compiler_params=pltpu.CompilerParams(vmem_limit_bytes=SMALL),
        name="fold",
    )(*arrays)


def main_kernel(
    pieces,
    sides,
    slots,
    axis_ref,
    counts_ref,
    neighbours_ref,
    rates_ref,
    points_ref,
    mixing_ref,
    readout_ref,
    *refs,
):
    piece_refs = refs[:pieces]
    ghost_refs = refs[pieces : 2 * pieces]
    (
        near_ref,
        own_ref,
        other_ref,
        features_ref,
        basis_ref,
        sum_ref,
        seed_ref,
        seed_t_ref,
        grad_a_ref,
        grad_b_ref,
        near_grad_ref,
        near_force_ref,
        own_force_ref,
        ghost_ref,
        in_sems,
        out_sems,
    ) = refs[2 * pieces :]
    _, tiles, atoms = points_ref.shape
    channels = readout_ref.shape[1]
    radials = rates_ref.shape[0]
    bases = 4 * radials
    group_rows = bases * GROUP
    groups = ROWS // GROUP
    chunk_rows = bases * ROWS
    couples = (slots + 1) // 2
    scaling = (slots * atoms) ** (-0.5)
    starts = [sum(ref.shape[0] for ref in piece_refs[:k]) for k in range(pieces)]
    cross = 1 + sides[1] + sides[2]
    blocks = (sides[1] + 1) * (sides[2] + 1)

    loads = [
        pltpu.make_async_copy(
            piece_refs[k], near_ref.at[pl.ds(starts[k], piece_refs[k].shape[0])], in_sems.at[k]
        )
        for k in range(pieces)
    ]
    for load in loads:
        load.start()

    for t in range(tiles):
        lines = [points_ref[m, t : t + 1, :] for m in range(3)]
        lines.append(jnp.zeros((atoms - 3, atoms), jnp.float32))
        columns = jnp.transpose(jnp.concatenate(lines, axis=0))
        for m in range(3):
            own_ref[t, m] = jnp.broadcast_to(columns[:, m : m + 1], (atoms, atoms))
    ghost_ref[...] = jnp.zeros_like(ghost_ref)
    own_force_ref[...] = jnp.zeros_like(own_force_ref)

    for load in loads:
        load.wait()

    def located(target):
        target = jnp.maximum(target, 0)
        block = lax.div(target, tiles)
        steps = (lax.div(block, 9), lax.rem(lax.div(block, 3), 3), lax.rem(block, 3))
        x, y, z = (side_of(steps[k] - 1, axis_ref[k], sides[k]) for k in range(3))
        diagonal = cross + (y - 1) * sides[2] + (z - 1)
        straight = jnp.where(y == 0, z, sides[2] + y)
        block = jnp.where((y > 0) & (z > 0), diagonal, straight)
        return (x * blocks + block) * tiles + lax.rem(target, tiles)

    rates = [rates_ref[r] for r in range(radials)]
    powers = [-rate * LOG2E for rate in rates]

    def geometry(t, slot, where):
        offset = [other_ref[t, slot, m] - own_ref[t, m, where, :] for m in range(3)]
        square = offset[0] * offset[0] + offset[1] * offset[1] + offset[2] * offset[2]
        return offset, [jnp.exp2(power * square) for power in powers]

    for t in range(tiles):
        count = counts_ref[t]
        chunks = (count + (ROWS - 1)) // ROWS

        def work(t=t, count=count, chunks=chunks):
            live = 0
            for k in range(slots):
                target = neighbours_ref[t * slots + k]
                live = live + jnp.where(target >= 0, 1, 0)
                tile = located(target)
                values = near_ref[tile, :atoms, :]
                features_ref[t, k * atoms : (k + 1) * atoms] = jnp.where(
                    target >= 0, values, jnp.zeros_like(values)
                )
                extra = near_ref[tile, atoms:, :].astype(jnp.float32)
                total = extra[0:3] + extra[3:6] + extra[6:9]
                for m in range(3):
                    other_ref[t, k, m] = jnp.broadcast_to(total[m : m + 1, :], (GROUP, atoms))
            for k in range(slots, 2 * couples + 2):
                features_ref[t, k * atoms : (k + 1) * atoms] = jnp.zeros((atoms, channels), jnp.bfloat16)
                for m in range(3):
                    other_ref[t, k, m] = jnp.zeros((GROUP, atoms), jnp.float32)

            def forward(chunk, carry):
                start = pl.multiple_of(chunk * ROWS, ROWS)
                base = pl.multiple_of(chunk * chunk_rows, chunk_rows)
                for slot in range(2 * couples):
                    for g in range(groups):
                        offset, radial = geometry(t, slot, pl.ds(start + g * GROUP, GROUP))
                        for r in range(radials):
                            values = [radial[r]] + [radial[r] * offset[m] for m in range(3)]
                            for k in range(2):
                                pair = jnp.concatenate(values[2 * k : 2 * k + 2], axis=0)
                                row = base + g * group_rows + (4 * r + 2 * k) * GROUP
                                basis_ref[t, slot, pl.ds(row, 2 * GROUP), :] = pair.astype(
                                    jnp.bfloat16
                                )
                where = pl.ds(base, chunk_rows)
                basis = [basis_ref[t, slot, where, :] for slot in range(2 * couples)]
                sum_ref[t, where, :] = (
                    jnp.dot(
                        jnp.concatenate(basis, axis=1),
                        features_ref[t, : 2 * couples * atoms],
                        preferred_element_type=jnp.float32,
                    )
                    * scaling
                )
                return carry

            lax.fori_loop(0, chunks, forward, 0)

            def clear(chunk, carry):
                where = pl.ds(pl.multiple_of(chunk * chunk_rows, chunk_rows), chunk_rows)
                sum_ref[t, where, :] = jnp.zeros((chunk_rows, channels), jnp.float32)
                return carry

            lax.fori_loop(chunks, atoms // ROWS, clear, 0)

            def sums(r, m):
                first = (4 * r + m) * GROUP
                return jnp.concatenate(
                    [
                        sum_ref[t, g * group_rows + first : g * group_rows + first + GROUP, :]
                        for g in range(atoms // GROUP)
                    ],
                    axis=0,
                )

            parts = [sums(r, 0) for r in range(radials)]
            for r in range(radials):
                norm = None
                for m in range(1, 4):
                    value = sums(r, m)
                    norm = value * value if norm is None else norm + value * value
                parts.append(norm)
            invariant = jnp.concatenate([part.astype(jnp.bfloat16) for part in parts], axis=1)
            preact = jnp.dot(invariant, mixing_ref[...], preferred_element_type=jnp.float32)
            sigmoid = jax.nn.sigmoid(preact)
            row = lax.broadcasted_iota(jnp.int32, (atoms, channels), 0)
            valid = (row < count).astype(jnp.float32)
            grad_pre = valid * readout_ref[...] * sigmoid * (1.0 + preact * (1.0 - sigmoid))
            grad = lax.dot_general(
                grad_pre.astype(jnp.bfloat16),
                mixing_ref[...],
                NT,
                preferred_element_type=jnp.float32,
            )
            for r in range(radials):
                scalar = grad[:, r * channels : (r + 1) * channels] * scaling
                square = grad[:, (radials + r) * channels : (radials + r + 1) * channels]
                square = square * (2.0 * scaling)
                values = [scalar] + [square * sums(r, m) for m in range(1, 4)]
                for g in range(atoms // GROUP):
                    rows = slice(g * GROUP, (g + 1) * GROUP)
                    for k in range(2):
                        pair = jnp.concatenate(
                            [value[rows] for value in values[2 * k : 2 * k + 2]], axis=0
                        )
                        first = g * group_rows + (4 * r + 2 * k) * GROUP
                        seed_ref[t, first : first + 2 * GROUP, :] = pair.astype(jnp.bfloat16)
            for chunk in range(atoms // ROWS):
                rows = slice(chunk * chunk_rows, (chunk + 1) * chunk_rows)
                seed_t_ref[t, chunk] = jnp.transpose(seed_ref[t, rows, :])

            near_grad_ref[...] = jnp.zeros_like(near_grad_ref)
            near_force_ref[...] = jnp.zeros_like(near_force_ref)
            active = (live + 1) // 2
            steps = active * chunks

            def following(place):
                couple, chunk = place
                wrap = chunk + 1 >= chunks
                couple = jnp.where(wrap, couple + 1, couple)
                return jnp.where(couple < active, couple, couples), jnp.where(wrap, 0, chunk + 1)

            def multiply(place, grad_ref):
                couple, chunk = place
                base = pl.multiple_of(chunk * chunk_rows, chunk_rows)
                where = pl.ds(base, chunk_rows)
                grad_ref[...] = lax.dot_general(
                    seed_ref[t, where, :],
                    features_ref[
                        t, pl.ds(pl.multiple_of(couple * 2 * atoms, 2 * atoms), 2 * atoms), :
                    ],
                    NT,
                    preferred_element_type=jnp.float32,
                )
                stored = jnp.minimum(couple, couples - 1)
                basis = [basis_ref[t, 2 * stored + half, where, :] for half in range(2)]
                near_grad_ref[couple] += jnp.dot(
                    seed_t_ref[t, chunk],
                    jnp.concatenate(basis, axis=1),
                    preferred_element_type=jnp.float32,
                )

            def pull(place, grad_ref):
                couple, chunk = place
                start = pl.multiple_of(chunk * ROWS, ROWS)
                pulled = [[None] * 3 for _ in range(2)]
                for g in range(groups):
                    rows = pl.ds(start + g * GROUP, GROUP)
                    total = [None] * 3
                    for half in range(2):
                        lanes = slice(half * atoms, (half + 1) * atoms)
                        offset, radial = geometry(t, 2 * couple + half, rows)
                        direct = [None] * 3
                        inner = None
                        for r in range(radials):
                            row = g * group_rows + 4 * r * GROUP
                            grad = [
                                grad_ref[row + m * GROUP : row + (m + 1) * GROUP, lanes]
                                for m in range(4)
                            ]
                            along = grad[0]
                            for m in range(3):
                                along = along + grad[m + 1] * offset[m]
                                part = radial[r] * grad[m + 1]
                                direct[m] = part if r == 0 else direct[m] + part
                            part = (radial[r] * (2.0 * rates[r])) * along
                            inner = part if r == 0 else inner + part
                        for m in range(3):
                            force = direct[m] - offset[m] * inner
                            total[m] = force if half == 0 else total[m] + force
                            old = pulled[half][m]
                            pulled[half][m] = force if g == 0 else old + force
                    for m in range(3):
                        own_force_ref[t, m, rows, :] += total[m]
                for half in range(2):
                    for m in range(3):
                        near_force_ref[couple, half, m] += pulled[half][m]

            zero = jnp.zeros((), jnp.int32)
            multiply((zero, zero), grad_a_ref)

            def backward(k, place):
                second = following(place)
                third = following(second)
                pull(place, grad_a_ref)
                multiply(second, grad_b_ref)
                pull(second, grad_b_ref)
                multiply(third, grad_a_ref)
                return third

            lax.fori_loop(0, (steps + 1) // 2, backward, (zero, zero))

            for slot in range(slots):
                target = neighbours_ref[t * slots + slot]

                def give(slot=slot, target=target):
                    tile = located(target)
                    couple, half = divmod(slot, 2)
                    lanes = slice(half * atoms, (half + 1) * atoms)
                    ghost_ref[tile, :channels, :] += near_grad_ref[couple, :, lanes]
                    for m in range(3):
                        ghost_ref[tile, channels + m : channels + m + 1, :] -= jnp.sum(
                            near_force_ref[couple, half, m], axis=0, keepdims=True
                        )

                pl.when(target >= 0)(give)
            for m in range(3):
                ghost_ref[t, channels + m : channels + m + 1, :] += jnp.sum(
                    jnp.transpose(own_force_ref[t, m]), axis=0, keepdims=True
                )

        pl.when(count > 0)(work)

    stores = [
        pltpu.make_async_copy(
            ghost_ref.at[pl.ds(starts[k], piece_refs[k].shape[0])], ghost_refs[k], out_sems.at[k]
        )
        for k in range(pieces)
    ]
    for store in stores:
        store.start()
    for store in stores:
        store.wait()


def final_kernel(counts_ref, *refs):
    part_refs = refs[:-2]
    forces_ref, grads_ref = refs[-2:]
    tiles, channels, atoms = grads_ref.shape
    for t in range(tiles):
        total = part_refs[0][t]
        for part in part_refs[1:]:
            total = total + part[t]
        forces_ref[:, t, :] = total[channels : channels + 3]
        column = lax.broadcasted_iota(jnp.int32, (channels, atoms), 1)
        masked = jnp.where(column < counts_ref[t], total[:channels], 0.0)
        grads_ref[t] = jnp.transpose(masked)


def body(positions, features, counts, neighbours, mix_weight, readout, radial_rates):
    tiles, atoms = positions.shape[3], positions.shape[5]
    channels = features.shape[5]
    slots = neighbours.shape[4]
    radials = radial_rates.shape[0]
    vmem = pl.BlockSpec(memory_space=pltpu.VMEM)
    smem = pl.BlockSpec(memory_space=pltpu.SMEM)
    hbm = pl.BlockSpec(memory_space=pl.ANY)
    small = pltpu.CompilerParams(vmem_limit_bytes=SMALL)

    def swap(value, axis):
        return [lax.ppermute(value, axis, pairs) for pairs in swaps(axis)]

    sides = tuple(len(swaps(axis)) for axis in ("gx", "gy", "gz"))
    own_counts = counts.reshape(tiles)
    points = jnp.transpose(positions, (0, 1, 2, 4, 3, 5)).reshape(3, tiles, atoms)
    packed = pl.pallas_call(
        pack_kernel,
        out_shape=jax.ShapeDtypeStruct((tiles, atoms + 16, channels), jnp.bfloat16),
        in_specs=[smem, vmem, vmem],
        out_specs=vmem,
        scratch_shapes=[pltpu.VMEM((16, channels), jnp.float32)],
        compiler_params=small,
        name="pack",
    )(own_counts, features.reshape(tiles, atoms, channels), points)

    along_z = swap(packed, "gz")
    along_y = swap(packed, "gy")
    (line,) = join([list(range(len(along_z)))], *along_z)
    diagonal = swap(line, "gy")
    (cross,) = join([list(range(2 + len(along_y)))], packed, line, *along_y)
    pieces = [[cross] + diagonal]
    for pairs in swaps("gx"):
        pieces.append([lax.ppermute(piece, "gx", pairs) for piece in pieces[0]])
    flat = [piece for plane in pieces for piece in plane]

    total = sum(piece.shape[0] for piece in flat)
    couples = (slots + 1) // 2
    bases = 4 * radials
    chunks = atoms // ROWS
    ghost_rows = channels + EXTRA
    position = jnp.stack([lax.axis_index(axis) % 2 for axis in ("gx", "gy", "gz")])
    ghosts = pl.pallas_call(
        functools.partial(main_kernel, len(flat), sides, slots),
        out_shape=[
            jax.ShapeDtypeStruct((piece.shape[0], ghost_rows, atoms), jnp.float32)
            for piece in flat
        ],
        in_specs=[smem] * 4 + [vmem] * 3 + [hbm] * len(flat),
        out_specs=[hbm] * len(flat),
        scratch_shapes=[
            pltpu.VMEM((total, atoms + 16, channels), jnp.bfloat16),
            pltpu.VMEM((tiles, 3, atoms, atoms), jnp.float32),
            pltpu.VMEM((tiles, 2 * couples + 2, 3, GROUP, atoms), jnp.float32),
            pltpu.VMEM((tiles, (2 * couples + 2) * atoms, channels), jnp.bfloat16),
            pltpu.VMEM((tiles, 2 * couples, bases * atoms, atoms), jnp.bfloat16),
            pltpu.VMEM((tiles, bases * atoms, channels), jnp.float32),
            pltpu.VMEM((tiles, bases * atoms, channels), jnp.bfloat16),
            pltpu.VMEM((tiles, chunks, channels, bases * ROWS), jnp.bfloat16),
            pltpu.VMEM((bases * ROWS, 2 * atoms), jnp.float32),
            pltpu.VMEM((bases * ROWS, 2 * atoms), jnp.float32),
            pltpu.VMEM((couples + 1, channels, 2 * atoms), jnp.float32),
            pltpu.VMEM((couples + 1, 2, 3, GROUP, atoms), jnp.float32),
            pltpu.VMEM((tiles, 3, atoms, atoms), jnp.float32),
            pltpu.VMEM((total, ghost_rows, atoms), jnp.float32),
            pltpu.SemaphoreType.DMA((len(flat),)),
            pltpu.SemaphoreType.DMA((len(flat),)),
        ],
        compiler_params=pltpu.CompilerParams(vmem_limit_bytes=LARGE),
        name="pairs",
    )(
        position,
        own_counts,
        neighbours.reshape(-1),
        radial_rates,
        points,
        mix_weight,
        readout.reshape(1, channels),
        *flat,
    )

    width = len(pieces[0])
    ghosts = [ghosts[k * width : (k + 1) * width] for k in range(len(pieces))]

    def gather(k):
        arrays = [ghosts[0][k]]
        for plane, pairs in zip(ghosts[1:], swaps("gx")):
            arrays.append(lax.ppermute(plane[k], "gx", pairs))
        return arrays

    diagonal = []
    for k, pairs in enumerate(swaps("gy")):
        arrays = gather(k + 1)
        (value,) = fold([((0,) * len(arrays), 0, arrays[0].shape[0])], *arrays)
        diagonal.append(lax.ppermute(value, "gy", pairs))
    arrays = gather(0)
    line = (sides[2] + 1) * tiles
    cuts = [((0,) * len(arrays), 0, tiles), ((0,) * len(arrays), tiles, line)]
    for k in range(sides[1]):
        cuts.append(((0,) * len(arrays), line + k * tiles, line + (k + 1) * tiles))
    center, along_z, *along_y = fold(cuts, *arrays)
    cuts = [((0,) * (1 + len(diagonal)), k * tiles, (k + 1) * tiles) for k in range(sides[2])]
    along_z = fold(cuts, along_z, *diagonal)
    parts = [center]
    for values, axis in ((along_z, "gz"), (along_y, "gy")):
        for value, pairs in zip(values, swaps(axis)):
            parts.append(lax.ppermute(value, axis, pairs))

    forces, grads = pl.pallas_call(
        final_kernel,
        out_shape=[
            jax.ShapeDtypeStruct((3, tiles, atoms), jnp.float32),
            jax.ShapeDtypeStruct((tiles, channels, atoms), jnp.float32),
        ],
        in_specs=[smem] + [vmem] * len(parts),
        out_specs=[vmem, vmem],
        compiler_params=small,
        name="finish",
    )(own_counts, *parts)
    forces = jnp.transpose(forces.reshape(1, 1, 1, 3, tiles, atoms), (0, 1, 2, 4, 3, 5))
    return forces, grads.reshape(1, 1, 1, tiles, atoms, channels)


def solution(mesh):
    in_specs = (
        P("gx", "gy", "gz", None, None, None),
        P("gx", "gy", "gz", None, None, None),
        P("gx", "gy", "gz", None),
        P("gx", "gy", "gz", None, None),
        P(),
        P(),
        P(),
    )
    out_specs = (P("gx", "gy", "gz", None, None, None), P("gx", "gy", "gz", None, None, None))
    return jax.shard_map(body, mesh=mesh, in_specs=in_specs, out_specs=out_specs, check_vma=False)
```

```python
import functools

import jax
import jax.numpy as jnp
from jax import lax
from jax.experimental import pallas as pl
from jax.experimental.pallas import tpu as pltpu
from jax.sharding import PartitionSpec as P


ROWS = 32
EXTRA = 8
TOP = 14.0
TINY = 1e-30
GROUP = 8
LOG2E = 1.4426950408889634
SMALL = 8 << 20
LARGE = 30 << 20
NT = (((1,), (1,)), ((), ()))


def swaps(axis):
    count = lax.axis_size(axis)
    result = []
    for first in (0, 1):
        pairs = [(i, i + 1) for i in range(first, count - 1, 2)]
        if pairs:
            result.append(pairs + [(b, a) for a, b in pairs])
    return result


def side_of(step, parity, sides):
    side = jnp.where((step == 1) == (parity == 0), 1, 2)
    return jnp.minimum(jnp.where(step == 0, 0, side), sides)


def pack_kernel(
    counts_ref,
    neighbours_ref,
    rates_ref,
    readout_ref,
    features_ref,
    points_ref,
    packed_ref,
    out_neighbours_ref,
    out_rates_ref,
    out_readout_ref,
    buffer_ref,
    place_ref,
    extra_ref,
    sems,
):
    loads = [
        pltpu.make_async_copy(features_ref, buffer_ref, sems.at[0]),
        pltpu.make_async_copy(points_ref, place_ref, sems.at[1]),
    ]
    for load in loads:
        load.start()
    tiles, atoms, _ = features_ref.shape
    for t in range(tiles):
        for k in range(neighbours_ref.shape[1]):
            out_neighbours_ref[t, k] = neighbours_ref[t, k]
    for r in range(rates_ref.shape[0]):
        out_rates_ref[r] = rates_ref[r]
    out_readout_ref[...] = readout_ref[...]
    extra_ref[...] = jnp.zeros_like(extra_ref)
    for load in loads:
        load.wait()
    for t in range(tiles):
        count = counts_ref[t]
        rows = lax.broadcasted_iota(jnp.int32, features_ref.shape[1:], 0)
        values = buffer_ref[t].astype(jnp.float32)
        packed_ref[t, :atoms] = jnp.where(rows < count, values, 0.0).astype(jnp.bfloat16)
        rest = place_ref[:, t, :]
        for term in range(3):
            part = rest.astype(jnp.bfloat16).astype(jnp.float32)
            extra_ref[t, 3 * term : 3 * term + 3] = part
            rest = rest - part
        packed_ref[t, atoms:] = extra_ref[t].astype(jnp.bfloat16)


def join_kernel(groups, *refs):
    inputs = refs[: -len(groups)]
    for group, out_ref in zip(groups, refs[-len(groups) :]):
        at = 0
        for k in group:
            count = inputs[k].shape[0]
            out_ref[at : at + count] = inputs[k][...]
            at += count


def join(groups, *arrays):
    shapes = [
        jax.ShapeDtypeStruct(
            (sum(arrays[k].shape[0] for k in group),) + arrays[0].shape[1:], arrays[0].dtype
        )
        for group in groups
    ]
    vmem = pl.BlockSpec(memory_space=pltpu.VMEM)
    return pl.pallas_call(
        functools.partial(join_kernel, groups),
        out_shape=shapes,
        in_specs=[vmem] * len(arrays),
        out_specs=[vmem] * len(groups),
        compiler_params=pltpu.CompilerParams(vmem_limit_bytes=SMALL),
        name="join",
    )(*arrays)


def decoded(ref, rows):
    value = ref[rows]
    channels = value.shape[1] - EXTRA
    grads = value[:, :channels] * jnp.exp2(value[:, channels + 3 : channels + 4] - TOP)
    forces = value[:, channels : channels + 3] * jnp.exp2(
        value[:, channels + 4 : channels + 5] - TOP
    )
    return grads, forces


def fold_kernel(cuts, plain, coded, *refs):
    plain_refs, coded_refs = refs[:plain], refs[plain : plain + coded]
    for (low, high, code), out_ref in zip(cuts, refs[plain + coded :]):
        channels = out_ref.shape[1] - EXTRA
        rows = slice(low, high)
        grads = forces = None
        for ref in plain_refs:
            part = ref[rows]
            grads = part[:, :channels] if grads is None else grads + part[:, :channels]
            part = part[:, channels : channels + 3]
            forces = part if forces is None else forces + part
        for ref in coded_refs:
            one, two = decoded(ref, rows)
            grads, forces = grads + one, forces + two
        if not code:
            out_ref[:, :channels] = grads
            out_ref[:, channels : channels + 3] = forces
            continue
        for first, value, at in ((0, grads, 3), (channels, forces, 4)):
            bound = jnp.max(jnp.abs(value), axis=1, keepdims=True)
            exponent = jnp.ceil(jnp.log2(jnp.maximum(bound, TINY)))
            out_ref[:, first : first + value.shape[1]] = value * jnp.exp2(TOP - exponent)
            out_ref[:, channels + at : channels + at + 1] = exponent


def fold(cuts, plain, coded):
    arrays = list(plain) + list(coded)
    shapes = [
        jax.ShapeDtypeStruct((high - low,) + arrays[0].shape[1:], jnp.float32)
        for low, high, _ in cuts
    ]
    vmem = pl.BlockSpec(memory_space=pltpu.VMEM)
    return pl.pallas_call(
        functools.partial(fold_kernel, cuts, len(plain), len(coded)),
        out_shape=shapes,
        in_specs=[vmem] * len(arrays),
        out_specs=[vmem] * len(cuts),
        compiler_params=pltpu.CompilerParams(vmem_limit_bytes=SMALL),
        name="fold",
    )(*arrays)


def send(value, axis, pairs):
    return lax.ppermute(value.astype(jnp.float16), axis, pairs).astype(jnp.float32)


def main_kernel(
    pieces,
    sides,
    slots,
    axis_ref,
    counts_ref,
    neighbours_ref,
    rates_ref,
    points_ref,
    mixing_ref,
    readout_ref,
    *refs,
):
    piece_refs = refs[:pieces]
    ghost_refs = refs[pieces : 2 * pieces]
    (
        near_ref,
        own_ref,
        other_ref,
        features_ref,
        basis_ref,
        sum_ref,
        seed_ref,
        seed_t_ref,
        near_grad_ref,
        near_force_ref,
        own_force_ref,
        ghost_ref,
        in_sems,
        out_sems,
        *grad_refs,
    ) = refs[2 * pieces :]
    _, tiles, atoms = points_ref.shape
    channels = readout_ref.shape[1]
    radials = rates_ref.shape[0]
    bases = 4 * radials
    group_rows = bases * GROUP
    groups = ROWS // GROUP
    chunk_rows = bases * ROWS
    couples = (slots + 1) // 2
    scaling = (slots * atoms) ** (-0.5)
    starts = [sum(ref.shape[0] for ref in piece_refs[:k]) for k in range(pieces)]
    cross = 1 + sides[1] + sides[2]
    blocks = (sides[1] + 1) * (sides[2] + 1)

    loads = [
        pltpu.make_async_copy(
            piece_refs[k], near_ref.at[pl.ds(starts[k], piece_refs[k].shape[0])], in_sems.at[k]
        )
        for k in range(pieces)
    ]
    for load in loads:
        load.start()

    for t in range(tiles):
        lines = [points_ref[m, t : t + 1, :] for m in range(3)]
        lines.append(jnp.zeros((atoms - 3, atoms), jnp.float32))
        columns = jnp.transpose(jnp.concatenate(lines, axis=0))
        for m in range(3):
            own_ref[t, m] = jnp.broadcast_to(columns[:, m : m + 1], (atoms, atoms))
    ghost_ref[...] = jnp.zeros_like(ghost_ref)
    own_force_ref[...] = jnp.zeros_like(own_force_ref)

    for load in loads:
        load.wait()

    def located(target):
        target = jnp.maximum(target, 0)
        block = lax.div(target, tiles)
        steps = (lax.div(block, 9), lax.rem(lax.div(block, 3), 3), lax.rem(block, 3))
        x, y, z = (side_of(steps[k] - 1, axis_ref[k], sides[k]) for k in range(3))
        diagonal = cross + (y - 1) * sides[2] + (z - 1)
        straight = jnp.where(y == 0, z, sides[2] + y)
        block = jnp.where((y > 0) & (z > 0), diagonal, straight)
        return (x * blocks + block) * tiles + lax.rem(target, tiles)

    rates = [rates_ref[r] for r in range(radials)]
    powers = [-rate * LOG2E for rate in rates]

    def geometry(t, slot, where):
        offset = [other_ref[t, slot, m] - own_ref[t, m, where, :] for m in range(3)]
        square = offset[0] * offset[0] + offset[1] * offset[1] + offset[2] * offset[2]
        return offset, [jnp.exp2(power * square) for power in powers]

    for t in range(tiles):
        count = counts_ref[t]
        chunks = (count + (ROWS - 1)) // ROWS

        def work(t=t, count=count, chunks=chunks):
            live = 0
            for k in range(slots):
                target = neighbours_ref[t, k]
                live = live + jnp.where(target >= 0, 1, 0)
                tile = located(target)
                values = near_ref[tile, :atoms, :]
                features_ref[t, k * atoms : (k + 1) * atoms] = jnp.where(
                    target >= 0, values, jnp.zeros_like(values)
                )
                extra = near_ref[tile, atoms:, :].astype(jnp.float32)
                total = extra[0:3] + extra[3:6] + extra[6:9]
                for m in range(3):
                    other_ref[t, k, m] = jnp.broadcast_to(total[m : m + 1, :], (GROUP, atoms))
            for k in range(slots, 2 * couples + 2):
                features_ref[t, k * atoms : (k + 1) * atoms] = jnp.zeros((atoms, channels), jnp.bfloat16)
                for m in range(3):
                    other_ref[t, k, m] = jnp.zeros((GROUP, atoms), jnp.float32)

            def forward(chunk, carry):
                start = pl.multiple_of(chunk * ROWS, ROWS)
                base = pl.multiple_of(chunk * chunk_rows, chunk_rows)
                for slot in range(2 * couples):
                    for g in range(groups):
                        offset, radial = geometry(t, slot, pl.ds(start + g * GROUP, GROUP))
                        for r in range(radials):
                            values = [radial[r]] + [radial[r] * offset[m] for m in range(3)]
                            for k in range(2):
                                pair = jnp.concatenate(values[2 * k : 2 * k + 2], axis=0)
                                row = base + g * group_rows + (4 * r + 2 * k) * GROUP
                                basis_ref[t, slot, pl.ds(row, 2 * GROUP), :] = pair.astype(
                                    jnp.bfloat16
                                )
                where = pl.ds(base, chunk_rows)
                basis = [basis_ref[t, slot, where, :] for slot in range(2 * couples)]
                sum_ref[t, where, :] = (
                    jnp.dot(
                        jnp.concatenate(basis, axis=1),
                        features_ref[t, : 2 * couples * atoms],
                        preferred_element_type=jnp.float32,
                    )
                    * scaling
                )
                return carry

            lax.fori_loop(0, chunks, forward, 0)

            def clear(chunk, carry):
                where = pl.ds(pl.multiple_of(chunk * chunk_rows, chunk_rows), chunk_rows)
                sum_ref[t, where, :] = jnp.zeros((chunk_rows, channels), jnp.float32)
                return carry

            lax.fori_loop(chunks, atoms // ROWS, clear, 0)

            def sums(r, m):
                first = (4 * r + m) * GROUP
                return jnp.concatenate(
                    [
                        sum_ref[t, g * group_rows + first : g * group_rows + first + GROUP, :]
                        for g in range(atoms // GROUP)
                    ],
                    axis=0,
                )

            parts = [sums(r, 0) for r in range(radials)]
            for r in range(radials):
                norm = None
                for m in range(1, 4):
                    value = sums(r, m)
                    norm = value * value if norm is None else norm + value * value
                parts.append(norm)
            invariant = jnp.concatenate([part.astype(jnp.bfloat16) for part in parts], axis=1)
            preact = jnp.dot(invariant, mixing_ref[...], preferred_element_type=jnp.float32)
            sigmoid = jax.nn.sigmoid(preact)
            row = lax.broadcasted_iota(jnp.int32, (atoms, channels), 0)
            valid = (row < count).astype(jnp.float32)
            grad_pre = valid * readout_ref[...] * sigmoid * (1.0 + preact * (1.0 - sigmoid))
            grad = lax.dot_general(
                grad_pre.astype(jnp.bfloat16),
                mixing_ref[...],
                NT,
                preferred_element_type=jnp.float32,
            )
            for r in range(radials):
                scalar = grad[:, r * channels : (r + 1) * channels] * scaling
                square = grad[:, (radials + r) * channels : (radials + r + 1) * channels]
                square = square * (2.0 * scaling)
                values = [scalar] + [square * sums(r, m) for m in range(1, 4)]
                for g in range(atoms // GROUP):
                    rows = slice(g * GROUP, (g + 1) * GROUP)
                    for k in range(2):
                        pair = jnp.concatenate(
                            [value[rows] for value in values[2 * k : 2 * k + 2]], axis=0
                        )
                        first = g * group_rows + (4 * r + 2 * k) * GROUP
                        seed_ref[t, first : first + 2 * GROUP, :] = pair.astype(jnp.bfloat16)
            for chunk in range(atoms // ROWS):
                rows = slice(chunk * chunk_rows, (chunk + 1) * chunk_rows)
                seed_t_ref[t, chunk] = jnp.transpose(seed_ref[t, rows, :])

            near_grad_ref[...] = jnp.zeros_like(near_grad_ref)
            near_force_ref[...] = jnp.zeros_like(near_force_ref)
            active = (live + 1) // 2
            steps = active * chunks

            def following(place):
                couple, chunk = place
                wrap = chunk + 1 >= chunks
                couple = jnp.where(wrap, couple + 1, couple)
                return jnp.where(couple < active, couple, couples), jnp.where(wrap, 0, chunk + 1)

            def multiply(place, grad_ref):
                couple, chunk = place
                base = pl.multiple_of(chunk * chunk_rows, chunk_rows)
                where = pl.ds(base, chunk_rows)
                grad_ref[...] = lax.dot_general(
                    seed_ref[t, where, :],
                    features_ref[
                        t, pl.ds(pl.multiple_of(couple * 2 * atoms, 2 * atoms), 2 * atoms), :
                    ],
                    NT,
                    preferred_element_type=jnp.float32,
                )
                stored = jnp.minimum(couple, couples - 1)
                basis = [basis_ref[t, 2 * stored + half, where, :] for half in range(2)]
                near_grad_ref[couple] += jnp.dot(
                    seed_t_ref[t, chunk],
                    jnp.concatenate(basis, axis=1),
                    preferred_element_type=jnp.float32,
                )

            def pull(place, grad_ref):
                couple, chunk = place
                start = pl.multiple_of(chunk * ROWS, ROWS)
                pulled = [[None] * 3 for _ in range(2)]
                for g in range(groups):
                    rows = pl.ds(start + g * GROUP, GROUP)
                    total = [None] * 3
                    for half in range(2):
                        lanes = slice(half * atoms, (half + 1) * atoms)
                        offset, radial = geometry(t, 2 * couple + half, rows)
                        direct = [None] * 3
                        inner = None
                        for r in range(radials):
                            row = g * group_rows + 4 * r * GROUP
                            grad = [
                                grad_ref[row + m * GROUP : row + (m + 1) * GROUP, lanes]
                                for m in range(4)
                            ]
                            along = grad[0]
                            for m in range(3):
                                along = along + grad[m + 1] * offset[m]
                                part = radial[r] * grad[m + 1]
                                direct[m] = part if r == 0 else direct[m] + part
                            part = (radial[r] * (2.0 * rates[r])) * along
                            inner = part if r == 0 else inner + part
                        for m in range(3):
                            force = direct[m] - offset[m] * inner
                            total[m] = force if half == 0 else total[m] + force
                            old = pulled[half][m]
                            pulled[half][m] = force if g == 0 else old + force
                    for m in range(3):
                        own_force_ref[t, m, rows, :] += total[m]
                for half in range(2):
                    for m in range(3):
                        near_force_ref[couple, half, m] += pulled[half][m]

            zero = jnp.zeros((), jnp.int32)
            first = (zero, zero)
            places = (first, following(first))
            multiply(places[0], grad_refs[0])
            multiply(places[1], grad_refs[1])

            def backward(k, places):
                one, two = places
                three = following(two)
                four = following(three)
                five = following(four)
                six = following(five)
                pull(one, grad_refs[0])
                multiply(three, grad_refs[2])
                pull(two, grad_refs[1])
                multiply(four, grad_refs[3])
                pull(three, grad_refs[2])
                multiply(five, grad_refs[0])
                pull(four, grad_refs[3])
                multiply(six, grad_refs[1])
                return five, six

            lax.fori_loop(0, (steps + 3) // 4, backward, places)

            for slot in range(slots):
                target = neighbours_ref[t, slot]

                def give(slot=slot, target=target):
                    tile = located(target)
                    couple, half = divmod(slot, 2)
                    lanes = slice(half * atoms, (half + 1) * atoms)
                    ghost_ref[tile, :channels, :] += near_grad_ref[couple, :, lanes]
                    for m in range(3):
                        ghost_ref[tile, channels + m : channels + m + 1, :] -= jnp.sum(
                            near_force_ref[couple, half, m], axis=0, keepdims=True
                        )

                pl.when(target >= 0)(give)
            for m in range(3):
                ghost_ref[t, channels + m : channels + m + 1, :] += jnp.sum(
                    jnp.transpose(own_force_ref[t, m]), axis=0, keepdims=True
                )

        pl.when(count > 0)(work)

    stores = [
        pltpu.make_async_copy(
            ghost_ref.at[pl.ds(starts[k], piece_refs[k].shape[0])], ghost_refs[k], out_sems.at[k]
        )
        for k in range(pieces)
    ]
    for store in stores:
        store.start()
    for store in stores:
        store.wait()


def final_kernel(counts_ref, center_ref, *refs):
    coded_refs = refs[:-2]
    forces_ref, grads_ref = refs[-2:]
    tiles, channels, atoms = grads_ref.shape
    for t in range(tiles):
        rows = slice(t, t + 1)
        grads = center_ref[rows, :channels]
        forces = center_ref[rows, channels : channels + 3]
        for ref in coded_refs:
            one, two = decoded(ref, rows)
            grads, forces = grads + one, forces + two
        forces_ref[:, t, :] = forces[0]
        column = lax.broadcasted_iota(jnp.int32, (channels, atoms), 1)
        masked = jnp.where(column < counts_ref[t], grads[0], 0.0)
        grads_ref[t] = jnp.transpose(masked)


def step(positions, features, counts, neighbours, mix_weight, readout, radial_rates):
    tiles, atoms = positions.shape[3], positions.shape[5]
    channels = features.shape[5]
    slots = neighbours.shape[4]
    radials = radial_rates.shape[0]
    vmem = pl.BlockSpec(memory_space=pltpu.VMEM)
    smem = pl.BlockSpec(memory_space=pltpu.SMEM)
    hbm = pl.BlockSpec(memory_space=pl.ANY)
    far = pl.BlockSpec(memory_space=pltpu.HBM)
    small = pltpu.CompilerParams(vmem_limit_bytes=SMALL)

    def swap(value, axis):
        return [lax.ppermute(value, axis, pairs) for pairs in swaps(axis)]

    sides = tuple(len(swaps(axis)) for axis in ("gx", "gy", "gz"))
    own_counts = counts.reshape(tiles)
    points = jnp.transpose(positions, (0, 1, 2, 4, 3, 5)).reshape(3, tiles, atoms)
    packed, neighbours, rates, readout = pl.pallas_call(
        pack_kernel,
        out_shape=[
            jax.ShapeDtypeStruct((tiles, atoms + 16, channels), jnp.bfloat16),
            jax.ShapeDtypeStruct((tiles, slots), jnp.int32),
            jax.ShapeDtypeStruct((radials,), jnp.float32),
            jax.ShapeDtypeStruct((1, channels), jnp.float32),
        ],
        in_specs=[smem, smem, smem, vmem, far, far],
        out_specs=[vmem, smem, smem, vmem],
        scratch_shapes=[
            pltpu.VMEM((tiles, atoms, channels), jnp.bfloat16),
            pltpu.VMEM((3, tiles, atoms), jnp.float32),
            pltpu.VMEM((tiles, 16, channels), jnp.float32),
            pltpu.SemaphoreType.DMA((2,)),
        ],
        compiler_params=pltpu.CompilerParams(vmem_limit_bytes=60 << 20),
        name="pack",
    )(
        own_counts,
        neighbours.reshape(tiles, slots),
        radial_rates,
        readout.reshape(1, channels),
        features.reshape(tiles, atoms, channels),
        points,
    )

    along_z = swap(packed, "gz")
    (line,) = join([list(range(len(along_z)))], *along_z)
    along_y = swap(packed, "gy")
    diagonal = swap(line, "gy")
    (cross,) = join([list(range(2 + len(along_y)))], packed, line, *along_y)
    pieces = [[cross] + diagonal]
    for pairs in swaps("gx"):
        plane = [lax.ppermute(cross, "gx", pairs)]
        pieces.append(plane + [lax.ppermute(piece, "gx", pairs) for piece in diagonal])
    flat = [piece for plane in pieces for piece in plane]

    total = sum(piece.shape[0] for piece in flat)
    couples = (slots + 1) // 2
    bases = 4 * radials
    chunks = atoms // ROWS
    ghost_rows = channels + EXTRA
    position = jnp.stack([lax.axis_index(axis) % 2 for axis in ("gx", "gy", "gz")])
    ghosts = pl.pallas_call(
        functools.partial(main_kernel, len(flat), sides, slots),
        out_shape=[
            jax.ShapeDtypeStruct((piece.shape[0], ghost_rows, atoms), jnp.float32)
            for piece in flat
        ],
        in_specs=[smem] * 4 + [vmem] * 3 + [hbm] * len(flat),
        out_specs=[hbm] * len(flat),
        scratch_shapes=[
            pltpu.VMEM((total, atoms + 16, channels), jnp.bfloat16),
            pltpu.VMEM((tiles, 3, atoms, atoms), jnp.float32),
            pltpu.VMEM((tiles, 2 * couples + 2, 3, GROUP, atoms), jnp.float32),
            pltpu.VMEM((tiles, (2 * couples + 2) * atoms, channels), jnp.bfloat16),
            pltpu.VMEM((tiles, 2 * couples, bases * atoms, atoms), jnp.bfloat16),
            pltpu.VMEM((tiles, bases * atoms, channels), jnp.float32),
            pltpu.VMEM((tiles, bases * atoms, channels), jnp.bfloat16),
            pltpu.VMEM((tiles, chunks, channels, bases * ROWS), jnp.bfloat16),
            pltpu.VMEM((couples + 1, channels, 2 * atoms), jnp.float32),
            pltpu.VMEM((couples + 1, 2, 3, GROUP, atoms), jnp.float32),
            pltpu.VMEM((tiles, 3, atoms, atoms), jnp.float32),
            pltpu.VMEM((total, ghost_rows, atoms), jnp.float32),
            pltpu.SemaphoreType.DMA((len(flat),)),
            pltpu.SemaphoreType.DMA((len(flat),)),
        ]
        + [pltpu.VMEM((bases * ROWS, 2 * atoms), jnp.float32)] * 4,
        compiler_params=pltpu.CompilerParams(vmem_limit_bytes=LARGE),
        name="pairs",
    )(
        position,
        own_counts,
        neighbours,
        rates,
        points,
        mix_weight,
        readout,
        *flat,
    )

    width = len(pieces[0])
    ghosts = [ghosts[k * width : (k + 1) * width] for k in range(len(pieces))]

    def gather(k):
        arrays = [ghosts[0][k]]
        for plane, pairs in zip(ghosts[1:], swaps("gx")):
            arrays.append(lax.ppermute(plane[k], "gx", pairs))
        return arrays

    diagonal = []
    for k, pairs in enumerate(swaps("gy")):
        arrays = gather(k + 1)
        (value,) = fold([(0, arrays[0].shape[0], True)], arrays, [])
        diagonal.append(send(value, "gy", pairs))
    arrays = gather(0)
    line = (sides[2] + 1) * tiles
    cuts = [(0, tiles, False), (tiles, line, False)]
    for k in range(sides[1]):
        cuts.append((line + k * tiles, line + (k + 1) * tiles, True))
    center, along_z, *along_y = fold(cuts, arrays, [])
    cuts = [(k * tiles, (k + 1) * tiles, True) for k in range(sides[2])]
    along_z = fold(cuts, [along_z], diagonal)
    parts = [center]
    for values, axis in ((along_z, "gz"), (along_y, "gy")):
        for value, pairs in zip(values, swaps(axis)):
            parts.append(send(value, axis, pairs))

    forces, grads = pl.pallas_call(
        final_kernel,
        out_shape=[
            jax.ShapeDtypeStruct((3, tiles, atoms), jnp.float32),
            jax.ShapeDtypeStruct((tiles, channels, atoms), jnp.float32),
        ],
        in_specs=[smem] + [vmem] * len(parts),
        out_specs=[vmem, vmem],
        compiler_params=small,
        name="finish",
    )(own_counts, *parts)
    forces = jnp.transpose(forces.reshape(1, 1, 1, 3, tiles, atoms), (0, 1, 2, 4, 3, 5))
    return forces, grads.reshape(1, 1, 1, tiles, atoms, channels)


def solution(mesh):
    in_specs = (
        P("gx", "gy", "gz", None, None, None),
        P("gx", "gy", "gz", None, None, None),
        P("gx", "gy", "gz", None),
        P("gx", "gy", "gz", None, None),
        P(),
        P(),
        P(),
    )
    out_specs = (P("gx", "gy", "gz", None, None, None), P("gx", "gy", "gz", None, None, None))
    return jax.shard_map(step, mesh=mesh, in_specs=in_specs, out_specs=out_specs, check_vma=False)
```

```python
import functools

import jax
import jax.numpy as jnp
from jax import lax
from jax.experimental import pallas as pl
from jax.experimental.pallas import tpu as pltpu
from jax.sharding import PartitionSpec as P


ROWS = 32
EXTRA = 8
TOP = 14.0
TINY = 1e-30
GROUP = 8
LOG2E = 1.4426950408889634
SMALL = 8 << 20
LARGE = 30 << 20
NT = (((1,), (1,)), ((), ()))


def swaps(axis):
    count = lax.axis_size(axis)
    result = []
    for first in (0, 1):
        pairs = [(i, i + 1) for i in range(first, count - 1, 2)]
        if pairs:
            result.append(pairs + [(b, a) for a, b in pairs])
    return result


def side_of(step, parity, sides):
    side = jnp.where((step == 1) == (parity == 0), 1, 2)
    return jnp.minimum(jnp.where(step == 0, 0, side), sides)


def pack_kernel(counts_ref, features_ref, points_ref, packed_ref, extra_ref):
    tiles, atoms, _ = features_ref.shape
    extra_ref[...] = jnp.zeros_like(extra_ref)
    for t in range(tiles):
        count = counts_ref[t]
        rows = lax.broadcasted_iota(jnp.int32, features_ref.shape[1:], 0)
        values = features_ref[t].astype(jnp.float32)
        packed_ref[t, :atoms] = jnp.where(rows < count, values, 0.0).astype(jnp.bfloat16)
        rest = points_ref[:, t, :]
        for term in range(3):
            part = rest.astype(jnp.bfloat16).astype(jnp.float32)
            extra_ref[t, 3 * term : 3 * term + 3] = part
            rest = rest - part
        packed_ref[t, atoms:] = extra_ref[t].astype(jnp.bfloat16)


def side_kernel(
    counts_ref,
    neighbours_ref,
    rates_ref,
    points_ref,
    readout_ref,
    out_counts_ref,
    out_neighbours_ref,
    out_rates_ref,
    out_points_ref,
    out_readout_ref,
):
    tiles, slots = neighbours_ref.shape
    for t in range(tiles):
        out_counts_ref[t] = counts_ref[t]
        for k in range(slots):
            out_neighbours_ref[t, k] = neighbours_ref[t, k]
    for r in range(rates_ref.shape[0]):
        out_rates_ref[r] = rates_ref[r]
    out_points_ref[...] = points_ref[...]
    out_readout_ref[...] = readout_ref[...]


def join_kernel(groups, *refs):
    inputs = refs[: -len(groups)]
    for group, out_ref in zip(groups, refs[-len(groups) :]):
        at = 0
        for k in group:
            count = inputs[k].shape[0]
            out_ref[at : at + count] = inputs[k][...]
            at += count


def join(groups, *arrays):
    shapes = [
        jax.ShapeDtypeStruct(
            (sum(arrays[k].shape[0] for k in group),) + arrays[0].shape[1:], arrays[0].dtype
        )
        for group in groups
    ]
    vmem = pl.BlockSpec(memory_space=pltpu.VMEM)
    return pl.pallas_call(
        functools.partial(join_kernel, groups),
        out_shape=shapes,
        in_specs=[vmem] * len(arrays),
        out_specs=[vmem] * len(groups),
        compiler_params=pltpu.CompilerParams(vmem_limit_bytes=SMALL),
        name="join",
    )(*arrays)


def decoded(ref, rows):
    value = ref[rows]
    channels = value.shape[1] - EXTRA
    grads = value[:, :channels] * jnp.exp2(value[:, channels + 3 : channels + 4] - TOP)
    forces = value[:, channels : channels + 3] * jnp.exp2(
        value[:, channels + 4 : channels + 5] - TOP
    )
    return grads, forces


def fold_kernel(cuts, plain, coded, *refs):
    plain_refs, coded_refs = refs[:plain], refs[plain : plain + coded]
    for (low, high, code), out_ref in zip(cuts, refs[plain + coded :]):
        channels = out_ref.shape[1] - EXTRA
        rows = slice(low, high)
        grads = forces = None
        for ref in plain_refs:
            part = ref[rows]
            grads = part[:, :channels] if grads is None else grads + part[:, :channels]
            part = part[:, channels : channels + 3]
            forces = part if forces is None else forces + part
        for ref in coded_refs:
            one, two = decoded(ref, rows)
            grads, forces = grads + one, forces + two
        if not code:
            out_ref[:, :channels] = grads
            out_ref[:, channels : channels + 3] = forces
            continue
        for first, value, at in ((0, grads, 3), (channels, forces, 4)):
            bound = jnp.max(jnp.abs(value), axis=1, keepdims=True)
            exponent = jnp.ceil(jnp.log2(jnp.maximum(bound, TINY)))
            out_ref[:, first : first + value.shape[1]] = value * jnp.exp2(TOP - exponent)
            out_ref[:, channels + at : channels + at + 1] = exponent


def fold(cuts, plain, coded):
    arrays = list(plain) + list(coded)
    shapes = [
        jax.ShapeDtypeStruct((high - low,) + arrays[0].shape[1:], jnp.float32)
        for low, high, _ in cuts
    ]
    vmem = pl.BlockSpec(memory_space=pltpu.VMEM)
    return pl.pallas_call(
        functools.partial(fold_kernel, cuts, len(plain), len(coded)),
        out_shape=shapes,
        in_specs=[vmem] * len(arrays),
        out_specs=[vmem] * len(cuts),
        compiler_params=pltpu.CompilerParams(vmem_limit_bytes=SMALL),
        name="fold",
    )(*arrays)


def send(value, axis, pairs):
    return lax.ppermute(value.astype(jnp.float16), axis, pairs).astype(jnp.float32)


def main_kernel(
    pieces,
    sides,
    slots,
    axis_ref,
    counts_ref,
    neighbours_ref,
    rates_ref,
    points_ref,
    mixing_ref,
    readout_ref,
    *refs,
):
    piece_refs = refs[:pieces]
    ghost_refs = refs[pieces : 2 * pieces]
    (
        near_ref,
        own_ref,
        other_ref,
        features_ref,
        basis_ref,
        sum_ref,
        seed_ref,
        seed_t_ref,
        near_grad_ref,
        near_force_ref,
        own_force_ref,
        ghost_ref,
        in_sems,
        out_sems,
        *grad_refs,
    ) = refs[2 * pieces :]
    _, tiles, atoms = points_ref.shape
    channels = readout_ref.shape[1]
    radials = rates_ref.shape[0]
    bases = 4 * radials
    group_rows = bases * GROUP
    groups = ROWS // GROUP
    chunk_rows = bases * ROWS
    couples = (slots + 1) // 2
    scaling = (slots * atoms) ** (-0.5)
    starts = [sum(ref.shape[0] for ref in piece_refs[:k]) for k in range(pieces)]
    cross = 1 + sides[1] + sides[2]
    blocks = (sides[1] + 1) * (sides[2] + 1)

    loads = [
        pltpu.make_async_copy(
            piece_refs[k], near_ref.at[pl.ds(starts[k], piece_refs[k].shape[0])], in_sems.at[k]
        )
        for k in range(pieces)
    ]
    for load in loads:
        load.start()

    for t in range(tiles):
        lines = [points_ref[m, t : t + 1, :] for m in range(3)]
        lines.append(jnp.zeros((atoms - 3, atoms), jnp.float32))
        columns = jnp.transpose(jnp.concatenate(lines, axis=0))
        for m in range(3):
            own_ref[t, m] = jnp.broadcast_to(columns[:, m : m + 1], (atoms, atoms))
    ghost_ref[...] = jnp.zeros_like(ghost_ref)
    own_force_ref[...] = jnp.zeros_like(own_force_ref)

    for load in loads:
        load.wait()

    def located(target):
        target = jnp.maximum(target, 0)
        block = lax.div(target, tiles)
        steps = (lax.div(block, 9), lax.rem(lax.div(block, 3), 3), lax.rem(block, 3))
        x, y, z = (side_of(steps[k] - 1, axis_ref[k], sides[k]) for k in range(3))
        diagonal = cross + (y - 1) * sides[2] + (z - 1)
        straight = jnp.where(y == 0, z, sides[2] + y)
        block = jnp.where((y > 0) & (z > 0), diagonal, straight)
        return (x * blocks + block) * tiles + lax.rem(target, tiles)

    rates = [rates_ref[r] for r in range(radials)]
    powers = [-rate * LOG2E for rate in rates]

    def geometry(t, slot, where):
        offset = [other_ref[t, slot, m] - own_ref[t, m, where, :] for m in range(3)]
        square = offset[0] * offset[0] + offset[1] * offset[1] + offset[2] * offset[2]
        return offset, [jnp.exp2(power * square) for power in powers]

    for t in range(tiles):
        count = counts_ref[t]
        chunks = (count + (ROWS - 1)) // ROWS

        def work(t=t, count=count, chunks=chunks):
            live = 0
            for k in range(slots):
                target = neighbours_ref[t, k]
                live = live + jnp.where(target >= 0, 1, 0)
                tile = located(target)
                values = near_ref[tile, :atoms, :]
                features_ref[t, k * atoms : (k + 1) * atoms] = jnp.where(
                    target >= 0, values, jnp.zeros_like(values)
                )
                extra = near_ref[tile, atoms:, :].astype(jnp.float32)
                total = extra[0:3] + extra[3:6] + extra[6:9]
                for m in range(3):
                    other_ref[t, k, m] = jnp.broadcast_to(total[m : m + 1, :], (GROUP, atoms))
            for k in range(slots, 2 * couples + 2):
                features_ref[t, k * atoms : (k + 1) * atoms] = jnp.zeros((atoms, channels), jnp.bfloat16)
                for m in range(3):
                    other_ref[t, k, m] = jnp.zeros((GROUP, atoms), jnp.float32)

            def forward(chunk, carry):
                start = pl.multiple_of(chunk * ROWS, ROWS)
                base = pl.multiple_of(chunk * chunk_rows, chunk_rows)
                for slot in range(2 * couples):
                    for g in range(groups):
                        offset, radial = geometry(t, slot, pl.ds(start + g * GROUP, GROUP))
                        for r in range(radials):
                            values = [radial[r]] + [radial[r] * offset[m] for m in range(3)]
                            for k in range(2):
                                pair = jnp.concatenate(values[2 * k : 2 * k + 2], axis=0)
                                row = base + g * group_rows + (4 * r + 2 * k) * GROUP
                                basis_ref[t, slot, pl.ds(row, 2 * GROUP), :] = pair.astype(
                                    jnp.bfloat16
                                )
                where = pl.ds(base, chunk_rows)
                basis = [basis_ref[t, slot, where, :] for slot in range(2 * couples)]
                sum_ref[t, where, :] = (
                    jnp.dot(
                        jnp.concatenate(basis, axis=1),
                        features_ref[t, : 2 * couples * atoms],
                        preferred_element_type=jnp.float32,
                    )
                    * scaling
                )
                return carry

            lax.fori_loop(0, chunks, forward, 0)

            def clear(chunk, carry):
                where = pl.ds(pl.multiple_of(chunk * chunk_rows, chunk_rows), chunk_rows)
                sum_ref[t, where, :] = jnp.zeros((chunk_rows, channels), jnp.float32)
                return carry

            lax.fori_loop(chunks, atoms // ROWS, clear, 0)

            def sums(r, m):
                first = (4 * r + m) * GROUP
                return jnp.concatenate(
                    [
                        sum_ref[t, g * group_rows + first : g * group_rows + first + GROUP, :]
                        for g in range(atoms // GROUP)
                    ],
                    axis=0,
                )

            parts = [sums(r, 0) for r in range(radials)]
            for r in range(radials):
                norm = None
                for m in range(1, 4):
                    value = sums(r, m)
                    norm = value * value if norm is None else norm + value * value
                parts.append(norm)
            invariant = jnp.concatenate([part.astype(jnp.bfloat16) for part in parts], axis=1)
            preact = jnp.dot(invariant, mixing_ref[...], preferred_element_type=jnp.float32)
            sigmoid = jax.nn.sigmoid(preact)
            row = lax.broadcasted_iota(jnp.int32, (atoms, channels), 0)
            valid = (row < count).astype(jnp.float32)
            grad_pre = valid * readout_ref[...] * sigmoid * (1.0 + preact * (1.0 - sigmoid))
            grad = lax.dot_general(
                grad_pre.astype(jnp.bfloat16),
                mixing_ref[...],
                NT,
                preferred_element_type=jnp.float32,
            )
            for r in range(radials):
                scalar = grad[:, r * channels : (r + 1) * channels] * scaling
                square = grad[:, (radials + r) * channels : (radials + r + 1) * channels]
                square = square * (2.0 * scaling)
                values = [scalar] + [square * sums(r, m) for m in range(1, 4)]
                for g in range(atoms // GROUP):
                    rows = slice(g * GROUP, (g + 1) * GROUP)
                    for k in range(2):
                        pair = jnp.concatenate(
                            [value[rows] for value in values[2 * k : 2 * k + 2]], axis=0
                        )
                        first = g * group_rows + (4 * r + 2 * k) * GROUP
                        seed_ref[t, first : first + 2 * GROUP, :] = pair.astype(jnp.bfloat16)
            for chunk in range(atoms // ROWS):
                rows = slice(chunk * chunk_rows, (chunk + 1) * chunk_rows)
                seed_t_ref[t, chunk] = jnp.transpose(seed_ref[t, rows, :])

            near_grad_ref[...] = jnp.zeros_like(near_grad_ref)
            near_force_ref[...] = jnp.zeros_like(near_force_ref)
            active = (live + 1) // 2
            steps = active * chunks

            def following(place):
                couple, chunk = place
                wrap = chunk + 1 >= chunks
                couple = jnp.where(wrap, couple + 1, couple)
                return jnp.where(couple < active, couple, couples), jnp.where(wrap, 0, chunk + 1)

            def multiply(place, grad_ref):
                couple, chunk = place
                base = pl.multiple_of(chunk * chunk_rows, chunk_rows)
                where = pl.ds(base, chunk_rows)
                grad_ref[...] = lax.dot_general(
                    seed_ref[t, where, :],
                    features_ref[
                        t, pl.ds(pl.multiple_of(couple * 2 * atoms, 2 * atoms), 2 * atoms), :
                    ],
                    NT,
                    preferred_element_type=jnp.float32,
                )
                stored = jnp.minimum(couple, couples - 1)
                basis = [basis_ref[t, 2 * stored + half, where, :] for half in range(2)]
                near_grad_ref[couple] += jnp.dot(
                    seed_t_ref[t, chunk],
                    jnp.concatenate(basis, axis=1),
                    preferred_element_type=jnp.float32,
                )

            def pull(place, grad_ref):
                couple, chunk = place
                start = pl.multiple_of(chunk * ROWS, ROWS)
                pulled = [[None] * 3 for _ in range(2)]
                for g in range(groups):
                    rows = pl.ds(start + g * GROUP, GROUP)
                    total = [None] * 3
                    for half in range(2):
                        lanes = slice(half * atoms, (half + 1) * atoms)
                        offset, radial = geometry(t, 2 * couple + half, rows)
                        direct = [None] * 3
                        inner = None
                        for r in range(radials):
                            row = g * group_rows + 4 * r * GROUP
                            grad = [
                                grad_ref[row + m * GROUP : row + (m + 1) * GROUP, lanes]
                                for m in range(4)
                            ]
                            along = grad[0]
                            for m in range(3):
                                along = along + grad[m + 1] * offset[m]
                                part = radial[r] * grad[m + 1]
                                direct[m] = part if r == 0 else direct[m] + part
                            part = (radial[r] * (2.0 * rates[r])) * along
                            inner = part if r == 0 else inner + part
                        for m in range(3):
                            force = direct[m] - offset[m] * inner
                            total[m] = force if half == 0 else total[m] + force
                            old = pulled[half][m]
                            pulled[half][m] = force if g == 0 else old + force
                    for m in range(3):
                        own_force_ref[t, m, rows, :] += total[m]
                for half in range(2):
                    for m in range(3):
                        near_force_ref[couple, half, m] += pulled[half][m]

            zero = jnp.zeros((), jnp.int32)
            first = (zero, zero)
            places = (first, following(first))
            multiply(places[0], grad_refs[0])
            multiply(places[1], grad_refs[1])

            def backward(k, places):
                one, two = places
                three = following(two)
                four = following(three)
                five = following(four)
                six = following(five)
                pull(one, grad_refs[0])
                multiply(three, grad_refs[2])
                pull(two, grad_refs[1])
                multiply(four, grad_refs[3])
                pull(three, grad_refs[2])
                multiply(five, grad_refs[0])
                pull(four, grad_refs[3])
                multiply(six, grad_refs[1])
                return five, six

            lax.fori_loop(0, (steps + 3) // 4, backward, places)

            for slot in range(slots):
                target = neighbours_ref[t, slot]

                def give(slot=slot, target=target):
                    tile = located(target)
                    couple, half = divmod(slot, 2)
                    lanes = slice(half * atoms, (half + 1) * atoms)
                    ghost_ref[tile, :channels, :] += near_grad_ref[couple, :, lanes]
                    for m in range(3):
                        ghost_ref[tile, channels + m : channels + m + 1, :] -= jnp.sum(
                            near_force_ref[couple, half, m], axis=0, keepdims=True
                        )

                pl.when(target >= 0)(give)
            for m in range(3):
                ghost_ref[t, channels + m : channels + m + 1, :] += jnp.sum(
                    jnp.transpose(own_force_ref[t, m]), axis=0, keepdims=True
                )

        pl.when(count > 0)(work)

    stores = [
        pltpu.make_async_copy(
            ghost_ref.at[pl.ds(starts[k], piece_refs[k].shape[0])], ghost_refs[k], out_sems.at[k]
        )
        for k in range(pieces)
    ]
    for store in stores:
        store.start()
    for store in stores:
        store.wait()


def final_kernel(counts_ref, center_ref, *refs):
    coded_refs = refs[:-2]
    forces_ref, grads_ref = refs[-2:]
    tiles, channels, atoms = grads_ref.shape
    for t in range(tiles):
        rows = slice(t, t + 1)
        grads = center_ref[rows, :channels]
        forces = center_ref[rows, channels : channels + 3]
        for ref in coded_refs:
            one, two = decoded(ref, rows)
            grads, forces = grads + one, forces + two
        forces_ref[:, t, :] = forces[0]
        column = lax.broadcasted_iota(jnp.int32, (channels, atoms), 1)
        masked = jnp.where(column < counts_ref[t], grads[0], 0.0)
        grads_ref[t] = jnp.transpose(masked)


def step(positions, features, counts, neighbours, mix_weight, readout, radial_rates):
    tiles, atoms = positions.shape[3], positions.shape[5]
    channels = features.shape[5]
    slots = neighbours.shape[4]
    radials = radial_rates.shape[0]
    vmem = pl.BlockSpec(memory_space=pltpu.VMEM)
    smem = pl.BlockSpec(memory_space=pltpu.SMEM)
    hbm = pl.BlockSpec(memory_space=pl.ANY)
    small = pltpu.CompilerParams(vmem_limit_bytes=SMALL)

    def swap(value, axis):
        return [lax.ppermute(value, axis, pairs) for pairs in swaps(axis)]

    sides = tuple(len(swaps(axis)) for axis in ("gx", "gy", "gz"))
    own_counts = counts.reshape(tiles)
    points = jnp.transpose(positions, (0, 1, 2, 4, 3, 5)).reshape(3, tiles, atoms)
    packed = pl.pallas_call(
        pack_kernel,
        out_shape=jax.ShapeDtypeStruct((tiles, atoms + 16, channels), jnp.bfloat16),
        in_specs=[smem, vmem, vmem],
        out_specs=vmem,
        scratch_shapes=[pltpu.VMEM((tiles, 16, channels), jnp.float32)],
        compiler_params=pltpu.CompilerParams(vmem_limit_bytes=60 << 20),
        name="pack",
    )(own_counts, features.reshape(tiles, atoms, channels), points)
    along_z = swap(packed, "gz")
    own_counts, neighbours, rates, points, readout = pl.pallas_call(
        side_kernel,
        out_shape=[
            jax.ShapeDtypeStruct((tiles,), jnp.int32),
            jax.ShapeDtypeStruct((tiles, slots), jnp.int32),
            jax.ShapeDtypeStruct((radials,), jnp.float32),
            jax.ShapeDtypeStruct((3, tiles, atoms), jnp.float32),
            jax.ShapeDtypeStruct((1, channels), jnp.float32),
        ],
        in_specs=[smem, smem, smem, vmem, vmem],
        out_specs=[smem, smem, smem, vmem, vmem],
        compiler_params=small,
        name="sides",
    )(
        own_counts,
        neighbours.reshape(tiles, slots),
        radial_rates,
        points,
        readout.reshape(1, channels),
    )
    (line,) = join([list(range(len(along_z)))], *along_z)
    diagonal = swap(line, "gy")
    along_y = swap(packed, "gy")
    (cross,) = join([list(range(2 + len(along_y)))], packed, line, *along_y)
    pieces = [[cross] + diagonal]
    for pairs in swaps("gx"):
        plane = [lax.ppermute(cross, "gx", pairs)]
        pieces.append(plane + [lax.ppermute(piece, "gx", pairs) for piece in diagonal])
    flat = [piece for plane in pieces for piece in plane]

    total = sum(piece.shape[0] for piece in flat)
    couples = (slots + 1) // 2
    bases = 4 * radials
    chunks = atoms // ROWS
    ghost_rows = channels + EXTRA
    position = jnp.stack([lax.axis_index(axis) % 2 for axis in ("gx", "gy", "gz")])
    ghosts = pl.pallas_call(
        functools.partial(main_kernel, len(flat), sides, slots),
        out_shape=[
            jax.ShapeDtypeStruct((piece.shape[0], ghost_rows, atoms), jnp.float32)
            for piece in flat
        ],
        in_specs=[smem] * 4 + [vmem] * 3 + [hbm] * len(flat),
        out_specs=[hbm] * len(flat),
        scratch_shapes=[
            pltpu.VMEM((total, atoms + 16, channels), jnp.bfloat16),
            pltpu.VMEM((tiles, 3, atoms, atoms), jnp.float32),
            pltpu.VMEM((tiles, 2 * couples + 2, 3, GROUP, atoms), jnp.float32),
            pltpu.VMEM((tiles, (2 * couples + 2) * atoms, channels), jnp.bfloat16),
            pltpu.VMEM((tiles, 2 * couples, bases * atoms, atoms), jnp.bfloat16),
            pltpu.VMEM((tiles, bases * atoms, channels), jnp.float32),
            pltpu.VMEM((tiles, bases * atoms, channels), jnp.bfloat16),
            pltpu.VMEM((tiles, chunks, channels, bases * ROWS), jnp.bfloat16),
            pltpu.VMEM((couples + 1, channels, 2 * atoms), jnp.float32),
            pltpu.VMEM((couples + 1, 2, 3, GROUP, atoms), jnp.float32),
            pltpu.VMEM((tiles, 3, atoms, atoms), jnp.float32),
            pltpu.VMEM((total, ghost_rows, atoms), jnp.float32),
            pltpu.SemaphoreType.DMA((len(flat),)),
            pltpu.SemaphoreType.DMA((len(flat),)),
        ]
        + [pltpu.VMEM((bases * ROWS, 2 * atoms), jnp.float32)] * 4,
        compiler_params=pltpu.CompilerParams(vmem_limit_bytes=LARGE),
        name="pairs",
    )(
        position,
        own_counts,
        neighbours,
        rates,
        points,
        mix_weight,
        readout,
        *flat,
    )

    width = len(pieces[0])
    ghosts = [ghosts[k * width : (k + 1) * width] for k in range(len(pieces))]

    def gather(k):
        arrays = [ghosts[0][k]]
        for plane, pairs in zip(ghosts[1:], swaps("gx")):
            arrays.append(lax.ppermute(plane[k], "gx", pairs))
        return arrays

    diagonal = []
    for k, pairs in enumerate(swaps("gy")):
        arrays = gather(k + 1)
        (value,) = fold([(0, arrays[0].shape[0], True)], arrays, [])
        diagonal.append(send(value, "gy", pairs))
    arrays = gather(0)
    line = (sides[2] + 1) * tiles
    cuts = [(0, tiles, False), (tiles, line, False)]
    for k in range(sides[1]):
        cuts.append((line + k * tiles, line + (k + 1) * tiles, True))
    center, along_z, *along_y = fold(cuts, arrays, [])
    parts = [center]
    for value, pairs in zip(along_y, swaps("gy")):
        parts.append(send(value, "gy", pairs))
    cuts = [(k * tiles, (k + 1) * tiles, True) for k in range(sides[2])]
    along_z = fold(cuts, [along_z], diagonal)
    for value, pairs in zip(along_z, swaps("gz")):
        parts.append(send(value, "gz", pairs))

    forces, grads = pl.pallas_call(
        final_kernel,
        out_shape=[
            jax.ShapeDtypeStruct((3, tiles, atoms), jnp.float32),
            jax.ShapeDtypeStruct((tiles, channels, atoms), jnp.float32),
        ],
        in_specs=[smem] + [vmem] * len(parts),
        out_specs=[vmem, vmem],
        compiler_params=small,
        name="finish",
    )(own_counts, *parts)
    forces = jnp.transpose(forces.reshape(1, 1, 1, 3, tiles, atoms), (0, 1, 2, 4, 3, 5))
    return forces, grads.reshape(1, 1, 1, tiles, atoms, channels)


def solution(mesh):
    in_specs = (
        P("gx", "gy", "gz", None, None, None),
        P("gx", "gy", "gz", None, None, None),
        P("gx", "gy", "gz", None),
        P("gx", "gy", "gz", None, None),
        P(),
        P(),
        P(),
    )
    out_specs = (P("gx", "gy", "gz", None, None, None), P("gx", "gy", "gz", None, None, None))
    return jax.shard_map(step, mesh=mesh, in_specs=in_specs, out_specs=out_specs, check_vma=False)
```

```python
import functools

import jax
import jax.numpy as jnp
from jax import lax
from jax.experimental import pallas as pl
from jax.experimental.pallas import tpu as pltpu
from jax.sharding import PartitionSpec as P


ROWS = 32
EXTRA = 8
TOP = 14.0
TINY = 1e-30
GROUP = 8
LOG2E = 1.4426950408889634
SMALL = 8 << 20
LARGE = 30 << 20
NT = (((1,), (1,)), ((), ()))


def swaps(axis):
    count = lax.axis_size(axis)
    result = []
    for first in (0, 1):
        pairs = [(i, i + 1) for i in range(first, count - 1, 2)]
        if pairs:
            result.append(pairs + [(b, a) for a, b in pairs])
    return result


def side_of(step, parity, sides):
    side = jnp.where((step == 1) == (parity == 0), 1, 2)
    return jnp.minimum(jnp.where(step == 0, 0, side), sides)


def pack_kernel(counts_ref, features_ref, points_ref, packed_ref, extra_ref):
    tiles, atoms, _ = features_ref.shape
    extra_ref[...] = jnp.zeros_like(extra_ref)
    for t in range(tiles):
        count = counts_ref[t]
        rows = lax.broadcasted_iota(jnp.int32, features_ref.shape[1:], 0)
        values = features_ref[t].astype(jnp.float32)
        packed_ref[t, :atoms] = jnp.where(rows < count, values, 0.0).astype(jnp.bfloat16)
        rest = points_ref[:, t, :]
        for term in range(3):
            part = rest.astype(jnp.bfloat16).astype(jnp.float32)
            extra_ref[t, 3 * term : 3 * term + 3] = part
            rest = rest - part
        packed_ref[t, atoms:] = extra_ref[t].astype(jnp.bfloat16)


def side_kernel(
    counts_ref,
    neighbours_ref,
    rates_ref,
    points_ref,
    readout_ref,
    out_counts_ref,
    out_neighbours_ref,
    out_rates_ref,
    out_points_ref,
    out_readout_ref,
):
    tiles, slots = neighbours_ref.shape
    for t in range(tiles):
        out_counts_ref[t] = counts_ref[t]
        for k in range(slots):
            out_neighbours_ref[t, k] = neighbours_ref[t, k]
    for r in range(rates_ref.shape[0]):
        out_rates_ref[r] = rates_ref[r]
    out_points_ref[...] = points_ref[...]
    out_readout_ref[...] = readout_ref[...]


def join_kernel(groups, *refs):
    inputs = refs[: -len(groups)]
    for group, out_ref in zip(groups, refs[-len(groups) :]):
        at = 0
        for k in group:
            count = inputs[k].shape[0]
            out_ref[at : at + count] = inputs[k][...]
            at += count


def join(groups, *arrays):
    shapes = [
        jax.ShapeDtypeStruct(
            (sum(arrays[k].shape[0] for k in group),) + arrays[0].shape[1:], arrays[0].dtype
        )
        for group in groups
    ]
    vmem = pl.BlockSpec(memory_space=pltpu.VMEM)
    return pl.pallas_call(
        functools.partial(join_kernel, groups),
        out_shape=shapes,
        in_specs=[vmem] * len(arrays),
        out_specs=[vmem] * len(groups),
        compiler_params=pltpu.CompilerParams(vmem_limit_bytes=SMALL),
        name="join",
    )(*arrays)


def decoded(ref, rows):
    value = ref[rows]
    channels = value.shape[1] - EXTRA
    grads = value[:, :channels] * jnp.exp2(value[:, channels + 3 : channels + 4] - TOP)
    forces = value[:, channels : channels + 3] * jnp.exp2(
        value[:, channels + 4 : channels + 5] - TOP
    )
    return grads, forces


def fold_kernel(cuts, plain, coded, *refs):
    plain_refs, coded_refs = refs[:plain], refs[plain : plain + coded]
    for (low, high, code), out_ref in zip(cuts, refs[plain + coded :]):
        channels = out_ref.shape[1] - EXTRA
        rows = slice(low, high)
        grads = forces = None
        for ref in plain_refs:
            part = ref[rows]
            grads = part[:, :channels] if grads is None else grads + part[:, :channels]
            part = part[:, channels : channels + 3]
            forces = part if forces is None else forces + part
        for ref in coded_refs:
            one, two = decoded(ref, rows)
            grads, forces = grads + one, forces + two
        if not code:
            out_ref[:, :channels] = grads
            out_ref[:, channels : channels + 3] = forces
            continue
        for first, value, at in ((0, grads, 3), (channels, forces, 4)):
            bound = jnp.max(jnp.abs(value), axis=1, keepdims=True)
            exponent = jnp.ceil(jnp.log2(jnp.maximum(bound, TINY)))
            out_ref[:, first : first + value.shape[1]] = value * jnp.exp2(TOP - exponent)
            out_ref[:, channels + at : channels + at + 1] = exponent


def fold(cuts, plain, coded):
    arrays = list(plain) + list(coded)
    shapes = [
        jax.ShapeDtypeStruct((high - low,) + arrays[0].shape[1:], jnp.float32)
        for low, high, _ in cuts
    ]
    vmem = pl.BlockSpec(memory_space=pltpu.VMEM)
    return pl.pallas_call(
        functools.partial(fold_kernel, cuts, len(plain), len(coded)),
        out_shape=shapes,
        in_specs=[vmem] * len(arrays),
        out_specs=[vmem] * len(cuts),
        compiler_params=pltpu.CompilerParams(vmem_limit_bytes=SMALL),
        name="fold",
    )(*arrays)


def send(value, axis, pairs):
    return lax.ppermute(value.astype(jnp.float16), axis, pairs).astype(jnp.float32)


def main_kernel(
    pieces,
    sides,
    slots,
    axis_ref,
    counts_ref,
    neighbours_ref,
    rates_ref,
    points_ref,
    mixing_ref,
    readout_ref,
    *refs,
):
    piece_refs = refs[:pieces]
    ghost_refs = refs[pieces : 2 * pieces]
    (
        near_ref,
        own_ref,
        other_ref,
        features_ref,
        basis_ref,
        sum_ref,
        seed_ref,
        seed_t_ref,
        near_grad_ref,
        near_force_ref,
        own_force_ref,
        ghost_ref,
        in_sems,
        out_sems,
        *grad_refs,
    ) = refs[2 * pieces :]
    _, tiles, atoms = points_ref.shape
    channels = readout_ref.shape[1]
    radials = rates_ref.shape[0]
    bases = 4 * radials
    group_rows = bases * GROUP
    groups = ROWS // GROUP
    chunk_rows = bases * ROWS
    couples = (slots + 1) // 2
    scaling = (slots * atoms) ** (-0.5)
    starts = [sum(ref.shape[0] for ref in piece_refs[:k]) for k in range(pieces)]

    loads = [
        pltpu.make_async_copy(
            piece_refs[k], near_ref.at[pl.ds(starts[k], piece_refs[k].shape[0])], in_sems.at[k]
        )
        for k in range(pieces)
    ]
    for load in loads:
        load.start()

    for t in range(tiles):
        lines = [points_ref[m, t : t + 1, :] for m in range(3)]
        lines.append(jnp.zeros((atoms - 3, atoms), jnp.float32))
        columns = jnp.transpose(jnp.concatenate(lines, axis=0))
        for m in range(3):
            own_ref[t, m] = jnp.broadcast_to(columns[:, m : m + 1], (atoms, atoms))
    ghost_ref[...] = jnp.zeros_like(ghost_ref)
    own_force_ref[...] = jnp.zeros_like(own_force_ref)

    for load in loads:
        load.wait()

    def located(target):
        target = jnp.maximum(target, 0)
        block = lax.div(target, tiles)
        steps = (lax.div(block, 9), lax.rem(lax.div(block, 3), 3), lax.rem(block, 3))
        x, y, z = (side_of(steps[k] - 1, axis_ref[k], sides[k]) for k in range(3))
        block = (x * (sides[1] + 1) + y) * (sides[2] + 1) + z
        return block * tiles + lax.rem(target, tiles)

    rates = [rates_ref[r] for r in range(radials)]
    powers = [-rate * LOG2E for rate in rates]

    def geometry(t, slot, where):
        offset = [other_ref[t, slot, m] - own_ref[t, m, where, :] for m in range(3)]
        square = offset[0] * offset[0] + offset[1] * offset[1] + offset[2] * offset[2]
        return offset, [jnp.exp2(power * square) for power in powers]

    for t in range(tiles):
        count = counts_ref[t]
        chunks = (count + (ROWS - 1)) // ROWS

        def work(t=t, count=count, chunks=chunks):
            live = 0
            for k in range(slots):
                target = neighbours_ref[t, k]
                live = live + jnp.where(target >= 0, 1, 0)
                tile = located(target)
                values = near_ref[tile, :atoms, :]
                features_ref[t, k * atoms : (k + 1) * atoms] = jnp.where(
                    target >= 0, values, jnp.zeros_like(values)
                )
                extra = near_ref[tile, atoms:, :].astype(jnp.float32)
                total = extra[0:3] + extra[3:6] + extra[6:9]
                for m in range(3):
                    other_ref[t, k, m] = jnp.broadcast_to(total[m : m + 1, :], (GROUP, atoms))
            for k in range(slots, 2 * couples + 2):
                features_ref[t, k * atoms : (k + 1) * atoms] = jnp.zeros((atoms, channels), jnp.bfloat16)
                for m in range(3):
                    other_ref[t, k, m] = jnp.zeros((GROUP, atoms), jnp.float32)

            def forward(chunk, carry):
                start = pl.multiple_of(chunk * ROWS, ROWS)
                base = pl.multiple_of(chunk * chunk_rows, chunk_rows)
                for slot in range(2 * couples):
                    for g in range(groups):
                        offset, radial = geometry(t, slot, pl.ds(start + g * GROUP, GROUP))
                        for r in range(radials):
                            values = [radial[r]] + [radial[r] * offset[m] for m in range(3)]
                            for k in range(2):
                                pair = jnp.concatenate(values[2 * k : 2 * k + 2], axis=0)
                                row = base + g * group_rows + (4 * r + 2 * k) * GROUP
                                basis_ref[t, slot, pl.ds(row, 2 * GROUP), :] = pair.astype(
                                    jnp.bfloat16
                                )
                where = pl.ds(base, chunk_rows)
                basis = [basis_ref[t, slot, where, :] for slot in range(2 * couples)]
                sum_ref[t, where, :] = (
                    jnp.dot(
                        jnp.concatenate(basis, axis=1),
                        features_ref[t, : 2 * couples * atoms],
                        preferred_element_type=jnp.float32,
                    )
                    * scaling
                )
                return carry

            lax.fori_loop(0, chunks, forward, 0)

            def clear(chunk, carry):
                where = pl.ds(pl.multiple_of(chunk * chunk_rows, chunk_rows), chunk_rows)
                sum_ref[t, where, :] = jnp.zeros((chunk_rows, channels), jnp.float32)
                return carry

            lax.fori_loop(chunks, atoms // ROWS, clear, 0)

            def sums(r, m):
                first = (4 * r + m) * GROUP
                return jnp.concatenate(
                    [
                        sum_ref[t, g * group_rows + first : g * group_rows + first + GROUP, :]
                        for g in range(atoms // GROUP)
                    ],
                    axis=0,
                )

            parts = [sums(r, 0) for r in range(radials)]
            for r in range(radials):
                norm = None
                for m in range(1, 4):
                    value = sums(r, m)
                    norm = value * value if norm is None else norm + value * value
                parts.append(norm)
            invariant = jnp.concatenate([part.astype(jnp.bfloat16) for part in parts], axis=1)
            preact = jnp.dot(invariant, mixing_ref[...], preferred_element_type=jnp.float32)
            sigmoid = jax.nn.sigmoid(preact)
            row = lax.broadcasted_iota(jnp.int32, (atoms, channels), 0)
            valid = (row < count).astype(jnp.float32)
            grad_pre = valid * readout_ref[...] * sigmoid * (1.0 + preact * (1.0 - sigmoid))
            grad = lax.dot_general(
                grad_pre.astype(jnp.bfloat16),
                mixing_ref[...],
                NT,
                preferred_element_type=jnp.float32,
            )
            for r in range(radials):
                scalar = grad[:, r * channels : (r + 1) * channels] * scaling
                square = grad[:, (radials + r) * channels : (radials + r + 1) * channels]
                square = square * (2.0 * scaling)
                values = [scalar] + [square * sums(r, m) for m in range(1, 4)]
                for g in range(atoms // GROUP):
                    rows = slice(g * GROUP, (g + 1) * GROUP)
                    for k in range(2):
                        pair = jnp.concatenate(
                            [value[rows] for value in values[2 * k : 2 * k + 2]], axis=0
                        )
                        first = g * group_rows + (4 * r + 2 * k) * GROUP
                        seed_ref[t, first : first + 2 * GROUP, :] = pair.astype(jnp.bfloat16)
            for chunk in range(atoms // ROWS):
                rows = slice(chunk * chunk_rows, (chunk + 1) * chunk_rows)
                seed_t_ref[t, chunk] = jnp.transpose(seed_ref[t, rows, :])

            near_grad_ref[...] = jnp.zeros_like(near_grad_ref)
            near_force_ref[...] = jnp.zeros_like(near_force_ref)
            active = (live + 1) // 2
            steps = active * chunks

            def following(place):
                couple, chunk = place
                wrap = chunk + 1 >= chunks
                couple = jnp.where(wrap, couple + 1, couple)
                return jnp.where(couple < active, couple, couples), jnp.where(wrap, 0, chunk + 1)

            def multiply(place, grad_ref):
                couple, chunk = place
                base = pl.multiple_of(chunk * chunk_rows, chunk_rows)
                where = pl.ds(base, chunk_rows)
                grad_ref[...] = lax.dot_general(
                    seed_ref[t, where, :],
                    features_ref[
                        t, pl.ds(pl.multiple_of(couple * 2 * atoms, 2 * atoms), 2 * atoms), :
                    ],
                    NT,
                    preferred_element_type=jnp.float32,
                )
                stored = jnp.minimum(couple, couples - 1)
                basis = [basis_ref[t, 2 * stored + half, where, :] for half in range(2)]
                near_grad_ref[couple] += jnp.dot(
                    seed_t_ref[t, chunk],
                    jnp.concatenate(basis, axis=1),
                    preferred_element_type=jnp.float32,
                )

            def pull(place, grad_ref):
                couple, chunk = place
                start = pl.multiple_of(chunk * ROWS, ROWS)
                pulled = [[None] * 3 for _ in range(2)]
                for g in range(groups):
                    rows = pl.ds(start + g * GROUP, GROUP)
                    total = [None] * 3
                    for half in range(2):
                        lanes = slice(half * atoms, (half + 1) * atoms)
                        offset, radial = geometry(t, 2 * couple + half, rows)
                        direct = [None] * 3
                        inner = None
                        for r in range(radials):
                            row = g * group_rows + 4 * r * GROUP
                            grad = [
                                grad_ref[row + m * GROUP : row + (m + 1) * GROUP, lanes]
                                for m in range(4)
                            ]
                            along = grad[0]
                            for m in range(3):
                                along = along + grad[m + 1] * offset[m]
                                part = radial[r] * grad[m + 1]
                                direct[m] = part if r == 0 else direct[m] + part
                            part = (radial[r] * (2.0 * rates[r])) * along
                            inner = part if r == 0 else inner + part
                        for m in range(3):
                            force = direct[m] - offset[m] * inner
                            total[m] = force if half == 0 else total[m] + force
                            old = pulled[half][m]
                            pulled[half][m] = force if g == 0 else old + force
                    for m in range(3):
                        own_force_ref[t, m, rows, :] += total[m]
                for half in range(2):
                    for m in range(3):
                        near_force_ref[couple, half, m] += pulled[half][m]

            zero = jnp.zeros((), jnp.int32)
            first = (zero, zero)
            places = (first, following(first))
            multiply(places[0], grad_refs[0])
            multiply(places[1], grad_refs[1])

            def backward(k, places):
                one, two = places
                three = following(two)
                four = following(three)
                five = following(four)
                six = following(five)
                pull(one, grad_refs[0])
                multiply(three, grad_refs[2])
                pull(two, grad_refs[1])
                multiply(four, grad_refs[3])
                pull(three, grad_refs[2])
                multiply(five, grad_refs[0])
                pull(four, grad_refs[3])
                multiply(six, grad_refs[1])
                return five, six

            lax.fori_loop(0, (steps + 3) // 4, backward, places)

            for slot in range(slots):
                target = neighbours_ref[t, slot]

                def give(slot=slot, target=target):
                    tile = located(target)
                    couple, half = divmod(slot, 2)
                    lanes = slice(half * atoms, (half + 1) * atoms)
                    ghost_ref[tile, :channels, :] += near_grad_ref[couple, :, lanes]
                    for m in range(3):
                        ghost_ref[tile, channels + m : channels + m + 1, :] -= jnp.sum(
                            near_force_ref[couple, half, m], axis=0, keepdims=True
                        )

                pl.when(target >= 0)(give)
            for m in range(3):
                ghost_ref[t, channels + m : channels + m + 1, :] += jnp.sum(
                    jnp.transpose(own_force_ref[t, m]), axis=0, keepdims=True
                )

        pl.when(count > 0)(work)

    stores = [
        pltpu.make_async_copy(
            ghost_ref.at[pl.ds(starts[k], piece_refs[k].shape[0])], ghost_refs[k], out_sems.at[k]
        )
        for k in range(pieces)
    ]
    for store in stores:
        store.start()
    for store in stores:
        store.wait()


def final_kernel(counts_ref, center_ref, *refs):
    coded_refs = refs[:-2]
    forces_ref, grads_ref = refs[-2:]
    tiles, channels, atoms = grads_ref.shape
    for t in range(tiles):
        rows = slice(t, t + 1)
        grads = center_ref[rows, :channels]
        forces = center_ref[rows, channels : channels + 3]
        for ref in coded_refs:
            one, two = decoded(ref, rows)
            grads, forces = grads + one, forces + two
        forces_ref[:, t, :] = forces[0]
        column = lax.broadcasted_iota(jnp.int32, (channels, atoms), 1)
        masked = jnp.where(column < counts_ref[t], grads[0], 0.0)
        grads_ref[t] = jnp.transpose(masked)


def step(positions, features, counts, neighbours, mix_weight, readout, radial_rates):
    tiles, atoms = positions.shape[3], positions.shape[5]
    channels = features.shape[5]
    slots = neighbours.shape[4]
    radials = radial_rates.shape[0]
    vmem = pl.BlockSpec(memory_space=pltpu.VMEM)
    smem = pl.BlockSpec(memory_space=pltpu.SMEM)
    hbm = pl.BlockSpec(memory_space=pl.ANY)
    small = pltpu.CompilerParams(vmem_limit_bytes=SMALL)

    def swap(value, axis):
        return [lax.ppermute(value, axis, pairs) for pairs in swaps(axis)]

    sides = tuple(len(swaps(axis)) for axis in ("gx", "gy", "gz"))
    own_counts = counts.reshape(tiles)
    points = jnp.transpose(positions, (0, 1, 2, 4, 3, 5)).reshape(3, tiles, atoms)
    packed = pl.pallas_call(
        pack_kernel,
        out_shape=jax.ShapeDtypeStruct((tiles, atoms + 16, channels), jnp.bfloat16),
        in_specs=[smem, vmem, vmem],
        out_specs=vmem,
        scratch_shapes=[pltpu.VMEM((tiles, 16, channels), jnp.float32)],
        compiler_params=pltpu.CompilerParams(vmem_limit_bytes=60 << 20),
        name="pack",
    )(own_counts, features.reshape(tiles, atoms, channels), points)
    along_z = swap(packed, "gz")
    own_counts, neighbours, rates, points, readout = pl.pallas_call(
        side_kernel,
        out_shape=[
            jax.ShapeDtypeStruct((tiles,), jnp.int32),
            jax.ShapeDtypeStruct((tiles, slots), jnp.int32),
            jax.ShapeDtypeStruct((radials,), jnp.float32),
            jax.ShapeDtypeStruct((3, tiles, atoms), jnp.float32),
            jax.ShapeDtypeStruct((1, channels), jnp.float32),
        ],
        in_specs=[smem, smem, smem, vmem, vmem],
        out_specs=[smem, smem, smem, vmem, vmem],
        compiler_params=small,
        name="sides",
    )(
        own_counts,
        neighbours.reshape(tiles, slots),
        radial_rates,
        points,
        readout.reshape(1, channels),
    )
    (line,) = join([list(range(1 + len(along_z)))], packed, *along_z)
    lines = [line] + swap(line, "gy")
    pieces = [lines]
    for pairs in swaps("gx"):
        plane = [lax.ppermute(line, "gx", pairs)]
        pieces.append(plane + [lax.ppermute(piece, "gx", pairs) for piece in lines[1:]])
    flat = [piece for plane in pieces for piece in plane]

    total = sum(piece.shape[0] for piece in flat)
    couples = (slots + 1) // 2
    bases = 4 * radials
    chunks = atoms // ROWS
    ghost_rows = channels + EXTRA
    position = jnp.stack([lax.axis_index(axis) % 2 for axis in ("gx", "gy", "gz")])
    ghosts = pl.pallas_call(
        functools.partial(main_kernel, len(flat), sides, slots),
        out_shape=[
            jax.ShapeDtypeStruct((piece.shape[0], ghost_rows, atoms), jnp.float32)
            for piece in flat
        ],
        in_specs=[smem] * 4 + [vmem] * 3 + [hbm] * len(flat),
        out_specs=[hbm] * len(flat),
        scratch_shapes=[
            pltpu.VMEM((total, atoms + 16, channels), jnp.bfloat16),
            pltpu.VMEM((tiles, 3, atoms, atoms), jnp.float32),
            pltpu.VMEM((tiles, 2 * couples + 2, 3, GROUP, atoms), jnp.float32),
            pltpu.VMEM((tiles, (2 * couples + 2) * atoms, channels), jnp.bfloat16),
            pltpu.VMEM((tiles, 2 * couples, bases * atoms, atoms), jnp.bfloat16),
            pltpu.VMEM((tiles, bases * atoms, channels), jnp.float32),
            pltpu.VMEM((tiles, bases * atoms, channels), jnp.bfloat16),
            pltpu.VMEM((tiles, chunks, channels, bases * ROWS), jnp.bfloat16),
            pltpu.VMEM((couples + 1, channels, 2 * atoms), jnp.float32),
            pltpu.VMEM((couples + 1, 2, 3, GROUP, atoms), jnp.float32),
            pltpu.VMEM((tiles, 3, atoms, atoms), jnp.float32),
            pltpu.VMEM((total, ghost_rows, atoms), jnp.float32),
            pltpu.SemaphoreType.DMA((len(flat),)),
            pltpu.SemaphoreType.DMA((len(flat),)),
        ]
        + [pltpu.VMEM((bases * ROWS, 2 * atoms), jnp.float32)] * 4,
        compiler_params=pltpu.CompilerParams(vmem_limit_bytes=LARGE),
        name="pairs",
    )(
        position,
        own_counts,
        neighbours,
        rates,
        points,
        mix_weight,
        readout,
        *flat,
    )

    width = len(pieces[0])
    ghosts = [ghosts[k * width : (k + 1) * width] for k in range(len(pieces))]

    def gather(k):
        arrays = [ghosts[0][k]]
        for plane, pairs in zip(ghosts[1:], swaps("gx")):
            arrays.append(lax.ppermute(plane[k], "gx", pairs))
        return arrays

    received = []
    for k, pairs in enumerate(swaps("gy")):
        arrays = gather(k + 1)
        (value,) = fold([(0, arrays[0].shape[0], True)], arrays, [])
        received.append(send(value, "gy", pairs))
    arrays = gather(0)
    cuts = [(k * tiles, (k + 1) * tiles, k > 0) for k in range(sides[2] + 1)]
    center, *along_z = fold(cuts, arrays, received)
    parts = [center]
    for value, pairs in zip(along_z, swaps("gz")):
        parts.append(send(value, "gz", pairs))

    forces, grads = pl.pallas_call(
        final_kernel,
        out_shape=[
            jax.ShapeDtypeStruct((3, tiles, atoms), jnp.float32),
            jax.ShapeDtypeStruct((tiles, channels, atoms), jnp.float32),
        ],
        in_specs=[smem] + [vmem] * len(parts),
        out_specs=[vmem, vmem],
        compiler_params=small,
        name="finish",
    )(own_counts, *parts)
    forces = jnp.transpose(forces.reshape(1, 1, 1, 3, tiles, atoms), (0, 1, 2, 4, 3, 5))
    return forces, grads.reshape(1, 1, 1, tiles, atoms, channels)


def solution(mesh):
    in_specs = (
        P("gx", "gy", "gz", None, None, None),
        P("gx", "gy", "gz", None, None, None),
        P("gx", "gy", "gz", None),
        P("gx", "gy", "gz", None, None),
        P(),
        P(),
        P(),
    )
    out_specs = (P("gx", "gy", "gz", None, None, None), P("gx", "gy", "gz", None, None, None))
    return jax.shard_map(step, mesh=mesh, in_specs=in_specs, out_specs=out_specs, check_vma=False)
```

```python
import functools

import jax
import jax.numpy as jnp
from jax import lax
from jax.experimental import pallas as pl
from jax.experimental.pallas import tpu as pltpu
from jax.sharding import PartitionSpec as P


ROWS = 32
EXTRA = 8
TOP = 14.0
TINY = 1e-30
GROUP = 8
LOG2E = 1.4426950408889634
SMALL = 8 << 20
LARGE = 20 << 20
NT = (((1,), (1,)), ((), ()))


def swaps(axis):
    count = lax.axis_size(axis)
    result = []
    for first in (0, 1):
        pairs = [(i, i + 1) for i in range(first, count - 1, 2)]
        if pairs:
            result.append(pairs + [(b, a) for a, b in pairs])
    return result


def side_of(step, parity, sides):
    side = jnp.where((step == 1) == (parity == 0), 1, 2)
    return jnp.minimum(jnp.where(step == 0, 0, side), sides)


def pack_kernel(counts_ref, features_ref, points_ref, packed_ref, extra_ref):
    tiles, atoms, _ = features_ref.shape
    extra_ref[...] = jnp.zeros_like(extra_ref)
    for t in range(tiles):
        count = counts_ref[t]
        rows = lax.broadcasted_iota(jnp.int32, features_ref.shape[1:], 0)
        values = features_ref[t].astype(jnp.float32)
        packed_ref[t, :atoms] = jnp.where(rows < count, values, 0.0).astype(jnp.bfloat16)
        rest = points_ref[:, t, :]
        for term in range(3):
            part = rest.astype(jnp.bfloat16).astype(jnp.float32)
            extra_ref[t, 3 * term : 3 * term + 3] = part
            rest = rest - part
        packed_ref[t, atoms:] = extra_ref[t].astype(jnp.bfloat16)


def side_kernel(
    sides,
    axis_ref,
    counts_ref,
    neighbours_ref,
    rates_ref,
    points_ref,
    readout_ref,
    packed_ref,
    out_counts_ref,
    out_table_ref,
    out_rates_ref,
    out_points_ref,
    out_readout_ref,
    out_packed_ref,
):
    tiles, slots = neighbours_ref.shape
    for t in range(tiles):
        out_counts_ref[t] = counts_ref[t]
        spots = []
        for k in range(slots):
            target = jnp.maximum(neighbours_ref[t, k], 0)
            block = lax.div(target, tiles)
            steps = (lax.div(block, 9), lax.rem(lax.div(block, 3), 3), lax.rem(block, 3))
            x, y, z = (side_of(steps[m] - 1, axis_ref[m], sides[m]) for m in range(3))
            block = (x * (sides[1] + 1) + y) * (sides[2] + 1) + z
            live = neighbours_ref[t, k] >= 0
            spots.append((block * tiles + lax.rem(target, tiles), live, live & (y == 0)))
            out_table_ref[t, k] = -1
        near = sum(jnp.where(line, 1, 0) for _, _, line in spots)
        total = sum(jnp.where(live, 1, 0) for _, live, _ in spots)
        out_table_ref[t, slots] = near
        out_table_ref[t, slots + 1] = total
        at_near, at_far = jnp.zeros((), jnp.int32), near
        for spot, live, line in spots:

            def put(spot=spot, at=jnp.where(line, at_near, at_far)):
                out_table_ref[t, at] = spot

            pl.when(live)(put)
            at_near = at_near + jnp.where(line, 1, 0)
            at_far = at_far + jnp.where(live & ~line, 1, 0)
    for r in range(rates_ref.shape[0]):
        out_rates_ref[r] = rates_ref[r]
    out_points_ref[...] = points_ref[...]
    out_readout_ref[...] = readout_ref[...]
    out_packed_ref[...] = packed_ref[...]


def join_kernel(groups, *refs):
    inputs = refs[: -len(groups)]
    for group, out_ref in zip(groups, refs[-len(groups) :]):
        at = 0
        for k in group:
            count = inputs[k].shape[0]
            out_ref[at : at + count] = inputs[k][...]
            at += count


def join(groups, *arrays):
    shapes = [
        jax.ShapeDtypeStruct(
            (sum(arrays[k].shape[0] for k in group),) + arrays[0].shape[1:], arrays[0].dtype
        )
        for group in groups
    ]
    vmem = pl.BlockSpec(memory_space=pltpu.VMEM)
    return pl.pallas_call(
        functools.partial(join_kernel, groups),
        out_shape=shapes,
        in_specs=[vmem] * len(arrays),
        out_specs=[vmem] * len(groups),
        compiler_params=pltpu.CompilerParams(vmem_limit_bytes=SMALL),
        name="join",
    )(*arrays)


def decoded(ref, rows):
    value = ref[rows]
    channels = value.shape[1] - EXTRA
    grads = value[:, :channels] * jnp.exp2(value[:, channels + 3 : channels + 4] - TOP)
    forces = value[:, channels : channels + 3] * jnp.exp2(
        value[:, channels + 4 : channels + 5] - TOP
    )
    return grads, forces


def fold_kernel(cuts, plain, coded, *refs):
    plain_refs, coded_refs = refs[:plain], refs[plain : plain + coded]
    for (low, high, code), out_ref in zip(cuts, refs[plain + coded :]):
        channels = out_ref.shape[1] - EXTRA
        rows = slice(low, high)
        grads = forces = None
        for ref in plain_refs:
            part = ref[rows]
            grads = part[:, :channels] if grads is None else grads + part[:, :channels]
            part = part[:, channels : channels + 3]
            forces = part if forces is None else forces + part
        for ref in coded_refs:
            one, two = decoded(ref, rows)
            grads, forces = grads + one, forces + two
        if not code:
            out_ref[:, :channels] = grads
            out_ref[:, channels : channels + 3] = forces
            continue
        for first, value, at in ((0, grads, 3), (channels, forces, 4)):
            bound = jnp.max(jnp.abs(value), axis=1, keepdims=True)
            exponent = jnp.ceil(jnp.log2(jnp.maximum(bound, TINY)))
            out_ref[:, first : first + value.shape[1]] = value * jnp.exp2(TOP - exponent)
            out_ref[:, channels + at : channels + at + 1] = exponent


def fold(cuts, plain, coded):
    arrays = list(plain) + list(coded)
    shapes = [
        jax.ShapeDtypeStruct((high - low,) + arrays[0].shape[1:], jnp.float32)
        for low, high, _ in cuts
    ]
    vmem = pl.BlockSpec(memory_space=pltpu.VMEM)
    return pl.pallas_call(
        functools.partial(fold_kernel, cuts, len(plain), len(coded)),
        out_shape=shapes,
        in_specs=[vmem] * len(arrays),
        out_specs=[vmem] * len(cuts),
        compiler_params=pltpu.CompilerParams(vmem_limit_bytes=SMALL),
        name="fold",
    )(*arrays)


def send(value, axis, pairs):
    return lax.ppermute(value.astype(jnp.float16), axis, pairs).astype(jnp.float32)


class Pairs:
    def __init__(self, rates_ref, own_ref, other_ref, channels, atoms):
        self.rates = [rates_ref[r] for r in range(rates_ref.shape[0])]
        self.powers = [-rate * LOG2E for rate in self.rates]
        self.own_ref, self.other_ref = own_ref, other_ref
        self.channels, self.atoms = channels, atoms
        self.group_rows = 4 * len(self.rates) * GROUP
        self.groups = ROWS // GROUP
        self.chunk_rows = self.group_rows * self.groups

    def geometry(self, t, slot, where):
        offset = [self.other_ref[t, slot, m] - self.own_ref[t, m, where, :] for m in range(3)]
        square = offset[0] * offset[0] + offset[1] * offset[1] + offset[2] * offset[2]
        return offset, [jnp.exp2(power * square) for power in self.powers]

    def backward(
        self,
        t,
        chunks,
        first,
        last,
        masked,
        block,
        couples,
        seed_ref,
        seed_t_ref,
        features_ref,
        basis_ref,
        near_grad_ref,
        near_force_ref,
        own_force_ref,
        grad_refs,
    ):
        atoms, group_rows, chunk_rows = self.atoms, self.group_rows, self.chunk_rows
        near_grad_ref[...] = jnp.zeros_like(near_grad_ref)
        near_force_ref[...] = jnp.zeros_like(near_force_ref)
        steps = (last - first) * chunks

        def following(place):
            couple, chunk = place
            wrap = chunk + 1 >= chunks
            couple = jnp.where(wrap, couple + 1, couple)
            return jnp.where(couple < last, couple, couples), jnp.where(wrap, 0, chunk + 1)

        def multiply(place, grad_ref):
            couple, chunk = place
            base = pl.multiple_of(chunk * chunk_rows, chunk_rows)
            where = pl.ds(base, chunk_rows)
            spot = jnp.where(couple == masked, block, couple)
            spot = pl.multiple_of(spot * 2 * atoms, 2 * atoms)
            grad_ref[...] = lax.dot_general(
                seed_ref[t, where, :],
                features_ref[t, pl.ds(spot, 2 * atoms), :],
                NT,
                preferred_element_type=jnp.float32,
            )
            stored = jnp.minimum(couple, couples - 1)
            basis = [basis_ref[t, 2 * stored + half, where, :] for half in range(2)]
            near_grad_ref[couple] += jnp.dot(
                seed_t_ref[t, chunk],
                jnp.concatenate(basis, axis=1),
                preferred_element_type=jnp.float32,
            )

        def pull(place, grad_ref):
            couple, chunk = place
            start = pl.multiple_of(chunk * ROWS, ROWS)
            pulled = [[None] * 3 for _ in range(2)]
            for g in range(self.groups):
                rows = pl.ds(start + g * GROUP, GROUP)
                total = [None] * 3
                for half in range(2):
                    lanes = slice(half * atoms, (half + 1) * atoms)
                    offset, radial = self.geometry(t, 2 * couple + half, rows)
                    direct = [None] * 3
                    inner = None
                    for r, rate in enumerate(self.rates):
                        row = g * group_rows + 4 * r * GROUP
                        grad = [
                            grad_ref[row + m * GROUP : row + (m + 1) * GROUP, lanes]
                            for m in range(4)
                        ]
                        along = grad[0]
                        for m in range(3):
                            along = along + grad[m + 1] * offset[m]
                            part = radial[r] * grad[m + 1]
                            direct[m] = part if r == 0 else direct[m] + part
                        part = (radial[r] * (2.0 * rate)) * along
                        inner = part if r == 0 else inner + part
                    for m in range(3):
                        force = direct[m] - offset[m] * inner
                        total[m] = force if half == 0 else total[m] + force
                        old = pulled[half][m]
                        pulled[half][m] = force if g == 0 else old + force
                for m in range(3):
                    own_force_ref[t, m, rows, :] += total[m]
            for half in range(2):
                for m in range(3):
                    near_force_ref[couple, half, m] += pulled[half][m]

        one = (first, jnp.zeros((), jnp.int32))
        two = following(one)
        multiply(one, grad_refs[0])
        multiply(two, grad_refs[1])

        def loop(k, places):
            one, two = places
            three = following(two)
            four = following(three)
            five = following(four)
            six = following(five)
            pull(one, grad_refs[0])
            multiply(three, grad_refs[2])
            pull(two, grad_refs[1])
            multiply(four, grad_refs[3])
            pull(three, grad_refs[2])
            multiply(five, grad_refs[0])
            pull(four, grad_refs[3])
            multiply(six, grad_refs[1])
            return five, six

        lax.fori_loop(0, (steps + 3) // 4, loop, (one, two))

    def give(self, slot, tile, near_grad_ref, near_force_ref, ghost_ref):
        couple, half = divmod(slot, 2)
        channels, atoms = self.channels, self.atoms
        lanes = slice(half * atoms, (half + 1) * atoms)
        ghost_ref[tile, :channels, :] += near_grad_ref[couple, :, lanes]
        for m in range(3):
            ghost_ref[tile, channels + m : channels + m + 1, :] -= jnp.sum(
                near_force_ref[couple, half, m], axis=0, keepdims=True
            )


def starts_of(piece_refs):
    return [sum(ref.shape[0] for ref in piece_refs[:k]) for k in range(len(piece_refs))]


def copies(pairs, sems):
    result = [
        pltpu.make_async_copy(source, target, sems.at[k])
        for k, (source, target) in enumerate(pairs)
    ]
    for copy in result:
        copy.start()
    return result


def main_kernel(
    pieces,
    outs,
    slots,
    line,
    counts_ref,
    table_ref,
    rates_ref,
    points_ref,
    mixing_ref,
    readout_ref,
    *refs,
):
    piece_refs = refs[:pieces]
    ghost_refs = refs[pieces : pieces + outs]
    (
        own_ref,
        other_ref,
        features_ref,
        basis_ref,
        seed_ref,
        seed_t_ref,
        own_force_ref,
        near_ref,
        sum_ref,
        near_grad_ref,
        near_force_ref,
        ghost_ref,
        in_sems,
        out_sems,
        *grad_refs,
    ) = refs[pieces + outs :]
    _, tiles, atoms = points_ref.shape
    channels = readout_ref.shape[1]
    couples = (slots + 1) // 2
    scaling = (slots * atoms) ** (-0.5)
    starts = starts_of(piece_refs)
    loads = copies(
        [
            (ref, near_ref.at[pl.ds(start, ref.shape[0])])
            for ref, start in zip(piece_refs, starts)
        ],
        in_sems,
    )

    for t in range(tiles):
        lines = [points_ref[m, t : t + 1, :] for m in range(3)]
        lines.append(jnp.zeros((atoms - 3, atoms), jnp.float32))
        columns = jnp.transpose(jnp.concatenate(lines, axis=0))
        for m in range(3):
            own_ref[t, m] = jnp.broadcast_to(columns[:, m : m + 1], (atoms, atoms))
    ghost_ref[...] = jnp.zeros_like(ghost_ref)
    own_force_ref[...] = jnp.zeros_like(own_force_ref)

    for load in loads:
        load.wait()

    pairs = Pairs(rates_ref, own_ref, other_ref, channels, atoms)
    radials, groups = len(pairs.rates), pairs.groups
    group_rows, chunk_rows = pairs.group_rows, pairs.chunk_rows

    for t in range(tiles):
        count = counts_ref[t]
        chunks = (count + (ROWS - 1)) // ROWS
        near = table_ref[t, slots]
        total_live = table_ref[t, slots + 1]

        def work(t=t, count=count, chunks=chunks, near=near, total_live=total_live):
            for k in range(slots):
                tile = table_ref[t, k]
                live = tile >= 0
                tile = jnp.maximum(tile, 0)
                values = near_ref[tile, :atoms, :]
                features_ref[t, k * atoms : (k + 1) * atoms] = jnp.where(
                    live, values, jnp.zeros_like(values)
                )
                extra = near_ref[tile, atoms:, :].astype(jnp.float32)
                total = extra[0:3] + extra[3:6] + extra[6:9]
                for m in range(3):
                    other_ref[t, k, m] = jnp.broadcast_to(total[m : m + 1, :], (GROUP, atoms))
            for k in range(slots, 2 * couples + 2):
                for m in range(3):
                    other_ref[t, k, m] = jnp.zeros((GROUP, atoms), jnp.float32)
            features_ref[t, slots * atoms :] = jnp.zeros(
                ((2 * couples + 6 - slots) * atoms, channels), jnp.bfloat16
            )
            ahead = pl.ds(pl.multiple_of(near * atoms, atoms), atoms)
            behind = pl.ds(pl.multiple_of((near - 1) * atoms, atoms), atoms)
            spare = (2 * couples + 2) * atoms
            features_ref[t, spare + atoms : spare + 2 * atoms] = features_ref[t, ahead, :]
            features_ref[t, spare + 2 * atoms : spare + 3 * atoms] = features_ref[t, behind, :]

            def forward(chunk, carry):
                start = pl.multiple_of(chunk * ROWS, ROWS)
                base = pl.multiple_of(chunk * chunk_rows, chunk_rows)
                for slot in range(2 * couples):
                    for g in range(groups):
                        where = pl.ds(start + g * GROUP, GROUP)
                        offset, radial = pairs.geometry(t, slot, where)
                        for r in range(radials):
                            values = [radial[r]] + [radial[r] * offset[m] for m in range(3)]
                            for k in range(2):
                                pair = jnp.concatenate(values[2 * k : 2 * k + 2], axis=0)
                                row = base + g * group_rows + (4 * r + 2 * k) * GROUP
                                basis_ref[t, slot, pl.ds(row, 2 * GROUP), :] = pair.astype(
                                    jnp.bfloat16
                                )
                where = pl.ds(base, chunk_rows)
                basis = [basis_ref[t, slot, where, :] for slot in range(2 * couples)]
                sum_ref[t, where, :] = (
                    jnp.dot(
                        jnp.concatenate(basis, axis=1),
                        features_ref[t, : 2 * couples * atoms],
                        preferred_element_type=jnp.float32,
                    )
                    * scaling
                )
                return carry

            lax.fori_loop(0, chunks, forward, 0)

            def clear(chunk, carry):
                where = pl.ds(pl.multiple_of(chunk * chunk_rows, chunk_rows), chunk_rows)
                sum_ref[t, where, :] = jnp.zeros((chunk_rows, channels), jnp.float32)
                return carry

            lax.fori_loop(chunks, atoms // ROWS, clear, 0)

            def sums(r, m):
                first = (4 * r + m) * GROUP
                return jnp.concatenate(
                    [
                        sum_ref[t, g * group_rows + first : g * group_rows + first + GROUP, :]
                        for g in range(atoms // GROUP)
                    ],
                    axis=0,
                )

            parts = [sums(r, 0) for r in range(radials)]
            for r in range(radials):
                norm = None
                for m in range(1, 4):
                    value = sums(r, m)
                    norm = value * value if norm is None else norm + value * value
                parts.append(norm)
            invariant = jnp.concatenate([part.astype(jnp.bfloat16) for part in parts], axis=1)
            preact = jnp.dot(invariant, mixing_ref[...], preferred_element_type=jnp.float32)
            sigmoid = jax.nn.sigmoid(preact)
            row = lax.broadcasted_iota(jnp.int32, (atoms, channels), 0)
            valid = (row < count).astype(jnp.float32)
            grad_pre = valid * readout_ref[...] * sigmoid * (1.0 + preact * (1.0 - sigmoid))
            grad = lax.dot_general(
                grad_pre.astype(jnp.bfloat16),
                mixing_ref[...],
                NT,
                preferred_element_type=jnp.float32,
            )
            for r in range(radials):
                scalar = grad[:, r * channels : (r + 1) * channels] * scaling
                square = grad[:, (radials + r) * channels : (radials + r + 1) * channels]
                square = square * (2.0 * scaling)
                values = [scalar] + [square * sums(r, m) for m in range(1, 4)]
                for g in range(atoms // GROUP):
                    rows = slice(g * GROUP, (g + 1) * GROUP)
                    for k in range(2):
                        pair = jnp.concatenate(
                            [value[rows] for value in values[2 * k : 2 * k + 2]], axis=0
                        )
                        first = g * group_rows + (4 * r + 2 * k) * GROUP
                        seed_ref[t, first : first + 2 * GROUP, :] = pair.astype(jnp.bfloat16)
            for chunk in range(atoms // ROWS):
                rows = slice(chunk * chunk_rows, (chunk + 1) * chunk_rows)
                seed_t_ref[t, chunk] = jnp.transpose(seed_ref[t, rows, :])

            def distant():
                first = near // 2
                pairs.backward(
                    t,
                    chunks,
                    first,
                    (total_live + 1) // 2,
                    jnp.where(near % 2 == 1, first, -1),
                    couples + 1,
                    couples,
                    seed_ref,
                    seed_t_ref,
                    features_ref,
                    basis_ref,
                    near_grad_ref,
                    near_force_ref,
                    own_force_ref,
                    grad_refs,
                )
                for slot in range(1, slots):

                    def give(slot=slot):
                        tile = table_ref[t, slot]
                        plane = lax.div(tile, line[1])
                        tile = tile - line[0] * (plane + 1)
                        pairs.give(slot, tile, near_grad_ref, near_force_ref, ghost_ref)

                    pl.when((slot >= near) & (slot < total_live))(give)

            pl.when(total_live > near)(distant)

        pl.when(count > 0)(work)

    starts = starts_of(ghost_refs)
    for store in copies(
        [
            (ghost_ref.at[pl.ds(start, ref.shape[0])], ref)
            for ref, start in zip(ghost_refs, starts)
        ],
        out_sems,
    ):
        store.wait()


def line_kernel(
    outs,
    slots,
    line,
    counts_ref,
    table_ref,
    rates_ref,
    own_ref,
    other_ref,
    features_ref,
    basis_ref,
    seed_ref,
    seed_t_ref,
    far_force_ref,
    *refs,
):
    ghost_refs = refs[:outs]
    near_grad_ref, near_force_ref, own_force_ref, ghost_ref, out_sems, *grad_refs = refs[outs:]
    tiles, _, atoms, _ = own_ref.shape
    channels = features_ref.shape[2]
    couples = (slots + 1) // 2
    pairs = Pairs(rates_ref, own_ref, other_ref, channels, atoms)
    ghost_ref[...] = jnp.zeros_like(ghost_ref)
    for t in range(tiles):
        count = counts_ref[t]
        chunks = (count + (ROWS - 1)) // ROWS
        near = table_ref[t, slots]

        def work(t=t, chunks=chunks, near=near):
            own_force_ref[t] = far_force_ref[t]
            pairs.backward(
                t,
                chunks,
                jnp.zeros((), jnp.int32),
                (near + 1) // 2,
                jnp.where(near % 2 == 1, near // 2, -1),
                couples + 2,
                couples,
                seed_ref,
                seed_t_ref,
                features_ref,
                basis_ref,
                near_grad_ref,
                near_force_ref,
                own_force_ref,
                grad_refs,
            )
            for slot in range(slots):

                def give(slot=slot):
                    tile = table_ref[t, slot]
                    tile = tile - (line[1] - line[0]) * lax.div(tile, line[1])
                    pairs.give(slot, tile, near_grad_ref, near_force_ref, ghost_ref)

                pl.when(slot < near)(give)
            for m in range(3):
                ghost_ref[t, channels + m : channels + m + 1, :] += jnp.sum(
                    jnp.transpose(own_force_ref[t, m]), axis=0, keepdims=True
                )

        pl.when(count > 0)(work)
    starts = starts_of(ghost_refs)
    for store in copies(
        [
            (ghost_ref.at[pl.ds(start, ref.shape[0])], ref)
            for ref, start in zip(ghost_refs, starts)
        ],
        out_sems,
    ):
        store.wait()


def final_kernel(counts_ref, center_ref, *refs):
    coded_refs = refs[:-2]
    forces_ref, grads_ref = refs[-2:]
    tiles, channels, atoms = grads_ref.shape
    for t in range(tiles):
        rows = slice(t, t + 1)
        grads = center_ref[rows, :channels]
        forces = center_ref[rows, channels : channels + 3]
        for ref in coded_refs:
            one, two = decoded(ref, rows)
            grads, forces = grads + one, forces + two
        forces_ref[:, t, :] = forces[0]
        column = lax.broadcasted_iota(jnp.int32, (channels, atoms), 1)
        masked = jnp.where(column < counts_ref[t], grads[0], 0.0)
        grads_ref[t] = jnp.transpose(masked)


def step(positions, features, counts, neighbours, mix_weight, readout, radial_rates):
    tiles, atoms = positions.shape[3], positions.shape[5]
    channels = features.shape[5]
    slots = neighbours.shape[4]
    radials = radial_rates.shape[0]
    vmem = pl.BlockSpec(memory_space=pltpu.VMEM)
    smem = pl.BlockSpec(memory_space=pltpu.SMEM)
    hbm = pl.BlockSpec(memory_space=pl.ANY)
    small = pltpu.CompilerParams(vmem_limit_bytes=SMALL)

    def swap(value, axis):
        return [lax.ppermute(value, axis, pairs) for pairs in swaps(axis)]

    sides = tuple(len(swaps(axis)) for axis in ("gx", "gy", "gz"))
    own_counts = counts.reshape(tiles)
    points = jnp.transpose(positions, (0, 1, 2, 4, 3, 5)).reshape(3, tiles, atoms)
    packed = pl.pallas_call(
        pack_kernel,
        out_shape=jax.ShapeDtypeStruct((tiles, atoms + 16, channels), jnp.bfloat16),
        in_specs=[smem, vmem, vmem],
        out_specs=vmem,
        scratch_shapes=[pltpu.VMEM((tiles, 16, channels), jnp.float32)],
        compiler_params=pltpu.CompilerParams(vmem_limit_bytes=60 << 20),
        name="pack",
    )(own_counts, features.reshape(tiles, atoms, channels), points)
    along_z = swap(packed, "gz")
    own_counts, table, rates, points, readout, local = pl.pallas_call(
        functools.partial(side_kernel, sides),
        out_shape=[
            jax.ShapeDtypeStruct((tiles,), jnp.int32),
            jax.ShapeDtypeStruct((tiles, slots + 2), jnp.int32),
            jax.ShapeDtypeStruct((radials,), jnp.float32),
            jax.ShapeDtypeStruct((3, tiles, atoms), jnp.float32),
            jax.ShapeDtypeStruct((1, channels), jnp.float32),
            jax.ShapeDtypeStruct(packed.shape, packed.dtype),
        ],
        in_specs=[smem, smem, smem, smem, vmem, vmem, vmem],
        out_specs=[smem, smem, smem, vmem, vmem, vmem],
        compiler_params=small,
        name="sides",
    )(
        jnp.stack([lax.axis_index(axis) % 2 for axis in ("gx", "gy", "gz")]),
        own_counts,
        neighbours.reshape(tiles, slots),
        radial_rates,
        points,
        readout.reshape(1, channels),
        packed,
    )
    (line,) = join([list(range(1 + len(along_z)))], local, *along_z)
    lines = [line] + swap(line, "gy")
    pieces = [lines]
    for pairs in swaps("gx"):
        plane = [lax.ppermute(line, "gx", pairs)]
        pieces.append(plane + [lax.ppermute(piece, "gx", pairs) for piece in lines[1:]])
    flat = [piece for plane in pieces for piece in plane]

    total = sum(piece.shape[0] for piece in flat)
    couples = (slots + 1) // 2
    bases = 4 * radials
    chunks = atoms // ROWS
    ghost_rows = channels + EXTRA
    counts_of = (line.shape[0], total // len(pieces))

    def ghost_shapes(arrays):
        return [
            jax.ShapeDtypeStruct((array.shape[0], ghost_rows, atoms), jnp.float32)
            for array in arrays
        ]

    far_shapes = ghost_shapes([piece for plane in pieces for piece in plane[1:]])
    line_shapes = ghost_shapes([plane[0] for plane in pieces])
    state_shapes = [
        jax.ShapeDtypeStruct((tiles, 3, atoms, atoms), jnp.float32),
        jax.ShapeDtypeStruct((tiles, 2 * couples + 2, 3, GROUP, atoms), jnp.float32),
        jax.ShapeDtypeStruct((tiles, (2 * couples + 6) * atoms, channels), jnp.bfloat16),
        jax.ShapeDtypeStruct((tiles, 2 * couples, bases * atoms, atoms), jnp.bfloat16),
        jax.ShapeDtypeStruct((tiles, bases * atoms, channels), jnp.bfloat16),
        jax.ShapeDtypeStruct((tiles, chunks, channels, bases * ROWS), jnp.bfloat16),
        jax.ShapeDtypeStruct((tiles, 3, atoms, atoms), jnp.float32),
    ]
    sums = [
        pltpu.VMEM((couples + 1, channels, 2 * atoms), jnp.float32),
        pltpu.VMEM((couples + 1, 2, 3, GROUP, atoms), jnp.float32),
    ]
    buffers = [pltpu.VMEM((bases * ROWS, 2 * atoms), jnp.float32)] * 4
    large = pltpu.CompilerParams(vmem_limit_bytes=LARGE)
    results = pl.pallas_call(
        functools.partial(main_kernel, len(flat), len(far_shapes), slots, counts_of),
        out_shape=far_shapes + state_shapes,
        in_specs=[smem] * 3 + [vmem] * 3 + [hbm] * len(flat),
        out_specs=[hbm] * len(far_shapes) + [vmem] * len(state_shapes),
        scratch_shapes=[
            pltpu.VMEM((total, atoms + 16, channels), jnp.bfloat16),
            pltpu.VMEM((tiles, bases * atoms, channels), jnp.float32),
            *sums,
            pltpu.VMEM(
                (sum(shape.shape[0] for shape in far_shapes), ghost_rows, atoms), jnp.float32
            ),
            pltpu.SemaphoreType.DMA((len(flat),)),
            pltpu.SemaphoreType.DMA((len(far_shapes),)),
            *buffers,
        ],
        compiler_params=large,
        name="pairs",
    )(own_counts, table, rates, points, mix_weight, readout, *flat)
    state = results[len(far_shapes) :]
    line_ghosts = pl.pallas_call(
        functools.partial(line_kernel, len(line_shapes), slots, counts_of),
        out_shape=line_shapes,
        in_specs=[smem] * 3 + [vmem] * len(state),
        out_specs=[hbm] * len(line_shapes),
        scratch_shapes=[
            *sums,
            pltpu.VMEM((tiles, 3, atoms, atoms), jnp.float32),
            pltpu.VMEM(
                (sum(shape.shape[0] for shape in line_shapes), ghost_rows, atoms), jnp.float32
            ),
            pltpu.SemaphoreType.DMA((len(line_shapes),)),
            *buffers,
        ],
        compiler_params=large,
        name="lines",
    )(own_counts, table, rates, *state)
    width = len(pieces[0]) - 1
    ghosts = [
        [line_ghosts[k]] + list(results[k * width : (k + 1) * width]) for k in range(len(pieces))
    ]

    def gather(k):
        arrays = [ghosts[0][k]]
        for plane, pairs in zip(ghosts[1:], swaps("gx")):
            arrays.append(lax.ppermute(plane[k], "gx", pairs))
        return arrays

    received = []
    for k, pairs in enumerate(swaps("gy")):
        arrays = gather(k + 1)
        (value,) = fold([(0, arrays[0].shape[0], True)], arrays, [])
        received.append(send(value, "gy", pairs))
    arrays = gather(0)
    cuts = [(k * tiles, (k + 1) * tiles, k > 0) for k in range(sides[2] + 1)]
    center, *along_z = fold(cuts, arrays, received)
    parts = [center]
    for value, pairs in zip(along_z, swaps("gz")):
        parts.append(send(value, "gz", pairs))

    forces, grads = pl.pallas_call(
        final_kernel,
        out_shape=[
            jax.ShapeDtypeStruct((3, tiles, atoms), jnp.float32),
            jax.ShapeDtypeStruct((tiles, channels, atoms), jnp.float32),
        ],
        in_specs=[smem] + [vmem] * len(parts),
        out_specs=[vmem, vmem],
        compiler_params=small,
        name="finish",
    )(own_counts, *parts)
    forces = jnp.transpose(forces.reshape(1, 1, 1, 3, tiles, atoms), (0, 1, 2, 4, 3, 5))
    return forces, grads.reshape(1, 1, 1, tiles, atoms, channels)


def solution(mesh):
    in_specs = (
        P("gx", "gy", "gz", None, None, None),
        P("gx", "gy", "gz", None, None, None),
        P("gx", "gy", "gz", None),
        P("gx", "gy", "gz", None, None),
        P(),
        P(),
        P(),
    )
    out_specs = (P("gx", "gy", "gz", None, None, None), P("gx", "gy", "gz", None, None, None))
    return jax.shard_map(step, mesh=mesh, in_specs=in_specs, out_specs=out_specs, check_vma=False)
```

```python
import functools

import jax
import jax.numpy as jnp
from jax import lax
from jax.experimental import pallas as pl
from jax.experimental.pallas import tpu as pltpu
from jax.sharding import PartitionSpec as P


ROWS = 32
EXTRA = 8
TOP = 14.0
TINY = 1e-30
GROUP = 8
LOG2E = 1.4426950408889634
SMALL = 8 << 20
LARGE = 20 << 20
NT = (((1,), (1,)), ((), ()))


def swaps(axis):
    count = lax.axis_size(axis)
    result = []
    for first in (0, 1):
        pairs = [(i, i + 1) for i in range(first, count - 1, 2)]
        if pairs:
            result.append(pairs + [(b, a) for a, b in pairs])
    return result


def side_of(step, parity, sides):
    side = jnp.where((step == 1) == (parity == 0), 1, 2)
    return jnp.minimum(jnp.where(step == 0, 0, side), sides)


def pack_kernel(counts_ref, features_ref, points_ref, packed_ref, extra_ref):
    tiles, atoms, _ = features_ref.shape
    extra_ref[...] = jnp.zeros_like(extra_ref)
    for t in range(tiles):
        count = counts_ref[t]
        rows = lax.broadcasted_iota(jnp.int32, features_ref.shape[1:], 0)
        values = features_ref[t].astype(jnp.float32)
        packed_ref[t, :atoms] = jnp.where(rows < count, values, 0.0).astype(jnp.bfloat16)
        rest = points_ref[:, t, :]
        for term in range(3):
            part = rest.astype(jnp.bfloat16).astype(jnp.float32)
            extra_ref[t, 3 * term : 3 * term + 3] = part
            rest = rest - part
        packed_ref[t, atoms:] = extra_ref[t].astype(jnp.bfloat16)


def side_kernel(
    sides,
    axis_ref,
    counts_ref,
    neighbours_ref,
    packed_ref,
    out_counts_ref,
    out_table_ref,
    out_packed_ref,
):
    tiles, slots = neighbours_ref.shape
    for t in range(tiles):
        out_counts_ref[t] = counts_ref[t]
        spots = []
        for k in range(slots):
            target = jnp.maximum(neighbours_ref[t, k], 0)
            block = lax.div(target, tiles)
            steps = (lax.div(block, 9), lax.rem(lax.div(block, 3), 3), lax.rem(block, 3))
            x, y, z = (side_of(steps[m] - 1, axis_ref[m], sides[m]) for m in range(3))
            block = (x * (sides[1] + 1) + y) * (sides[2] + 1) + z
            live = neighbours_ref[t, k] >= 0
            spots.append((block * tiles + lax.rem(target, tiles), live, live & (y == 0)))
            out_table_ref[t, k] = -1
        near = sum(jnp.where(line, 1, 0) for _, _, line in spots)
        total = sum(jnp.where(live, 1, 0) for _, live, _ in spots)
        out_table_ref[t, slots] = near
        out_table_ref[t, slots + 1] = total
        at_near, at_far = jnp.zeros((), jnp.int32), near
        for spot, live, line in spots:

            def put(spot=spot, at=jnp.where(line, at_near, at_far)):
                out_table_ref[t, at] = spot

            pl.when(live)(put)
            at_near = at_near + jnp.where(line, 1, 0)
            at_far = at_far + jnp.where(live & ~line, 1, 0)
    out_packed_ref[...] = packed_ref[...]


def stage_kernel(rates_ref, points_ref, readout_ref, mixing_ref, *out_refs):
    for r in range(rates_ref.shape[0]):
        out_refs[0][r] = rates_ref[r]
    out_refs[1][...] = points_ref[...]
    out_refs[2][...] = readout_ref[...]
    out_refs[3][...] = mixing_ref[...]


def join_kernel(groups, *refs):
    inputs = refs[: -len(groups)]
    for group, out_ref in zip(groups, refs[-len(groups) :]):
        at = 0
        for k in group:
            count = inputs[k].shape[0]
            out_ref[at : at + count] = inputs[k][...]
            at += count


def join(groups, *arrays):
    shapes = [
        jax.ShapeDtypeStruct(
            (sum(arrays[k].shape[0] for k in group),) + arrays[0].shape[1:], arrays[0].dtype
        )
        for group in groups
    ]
    vmem = pl.BlockSpec(memory_space=pltpu.VMEM)
    return pl.pallas_call(
        functools.partial(join_kernel, groups),
        out_shape=shapes,
        in_specs=[vmem] * len(arrays),
        out_specs=[vmem] * len(groups),
        compiler_params=pltpu.CompilerParams(vmem_limit_bytes=SMALL),
        name="join",
    )(*arrays)


def decoded(ref, rows):
    value = ref[rows]
    channels = value.shape[1] - EXTRA
    grads = value[:, :channels] * jnp.exp2(value[:, channels + 3 : channels + 4] - TOP)
    forces = value[:, channels : channels + 3] * jnp.exp2(
        value[:, channels + 4 : channels + 5] - TOP
    )
    return grads, forces


def fold_kernel(cuts, plain, coded, *refs):
    plain_refs, coded_refs = refs[:plain], refs[plain : plain + coded]
    for (low, high, code), out_ref in zip(cuts, refs[plain + coded :]):
        channels = out_ref.shape[1] - EXTRA
        rows = slice(low, high)
        grads = forces = None
        for ref in plain_refs:
            part = ref[rows]
            grads = part[:, :channels] if grads is None else grads + part[:, :channels]
            part = part[:, channels : channels + 3]
            forces = part if forces is None else forces + part
        for ref in coded_refs:
            one, two = decoded(ref, rows)
            grads, forces = grads + one, forces + two
        if not code:
            out_ref[:, :channels] = grads
            out_ref[:, channels : channels + 3] = forces
            continue
        for first, value, at in ((0, grads, 3), (channels, forces, 4)):
            bound = jnp.max(jnp.abs(value), axis=1, keepdims=True)
            exponent = jnp.ceil(jnp.log2(jnp.maximum(bound, TINY)))
            out_ref[:, first : first + value.shape[1]] = value * jnp.exp2(TOP - exponent)
            out_ref[:, channels + at : channels + at + 1] = exponent


def fold(cuts, plain, coded):
    arrays = list(plain) + list(coded)
    shapes = [
        jax.ShapeDtypeStruct((high - low,) + arrays[0].shape[1:], jnp.float32)
        for low, high, _ in cuts
    ]
    vmem = pl.BlockSpec(memory_space=pltpu.VMEM)
    return pl.pallas_call(
        functools.partial(fold_kernel, cuts, len(plain), len(coded)),
        out_shape=shapes,
        in_specs=[vmem] * len(arrays),
        out_specs=[vmem] * len(cuts),
        compiler_params=pltpu.CompilerParams(vmem_limit_bytes=SMALL),
        name="fold",
    )(*arrays)


def send(value, axis, pairs):
    return lax.ppermute(value.astype(jnp.float16), axis, pairs).astype(jnp.float32)


class Pairs:
    def __init__(self, rates_ref, own_ref, other_ref, channels, atoms):
        self.rates = [rates_ref[r] for r in range(rates_ref.shape[0])]
        self.powers = [-rate * LOG2E for rate in self.rates]
        self.own_ref, self.other_ref = own_ref, other_ref
        self.channels, self.atoms = channels, atoms
        self.group_rows = 4 * len(self.rates) * GROUP
        self.groups = ROWS // GROUP
        self.chunk_rows = self.group_rows * self.groups

    def geometry(self, t, slot, where):
        offset = [self.other_ref[t, slot, m] - self.own_ref[t, m, where, :] for m in range(3)]
        square = offset[0] * offset[0] + offset[1] * offset[1] + offset[2] * offset[2]
        return offset, [jnp.exp2(power * square) for power in self.powers]

    def backward(
        self,
        chunks,
        firsts,
        lasts,
        masked,
        block,
        couples,
        seed_ref,
        seed_t_ref,
        features_ref,
        basis_ref,
        near_grad_ref,
        near_force_ref,
        own_force_ref,
        grad_refs,
    ):
        atoms, group_rows, chunk_rows = self.atoms, self.group_rows, self.chunk_rows
        near_grad_ref[...] = jnp.zeros_like(near_grad_ref)
        near_force_ref[...] = jnp.zeros_like(near_force_ref)
        tiles = len(chunks)
        lengths = [(lasts[k] - firsts[k]) * chunks[k] for k in range(tiles)]
        steps = sum(lengths)
        zero = jnp.zeros((), jnp.int32)

        def of(values, t):
            result = values[-1]
            for k in reversed(range(tiles - 1)):
                result = jnp.where(t == k, values[k], result)
            return result

        def enter(start):
            t = jnp.full((), tiles, jnp.int32)
            for k in reversed(range(tiles)):
                t = jnp.where((start <= k) & (lengths[k] > 0), k, t)
            found = t < tiles
            t = jnp.minimum(t, tiles - 1)
            return t, jnp.where(found, of(firsts, t), couples), zero

        def following(place):
            t, couple, chunk = place
            wrap = chunk + 1 >= of(chunks, t)
            end = wrap & (couple + 1 >= of(lasts, t))
            tile, start, _ = enter(t + 1)
            inside = jnp.where(wrap, couple + 1, couple)
            return (
                jnp.where(end, tile, t),
                jnp.where(end, start, inside),
                jnp.where(wrap, 0, chunk + 1),
            )

        def multiply(place, grad_ref):
            t, couple, chunk = place
            base = pl.multiple_of(chunk * chunk_rows, chunk_rows)
            where = pl.ds(base, chunk_rows)
            spot = jnp.where(couple == of(masked, t), block, couple)
            spot = pl.multiple_of(spot * 2 * atoms, 2 * atoms)
            grad_ref[...] = lax.dot_general(
                seed_ref[t, where, :],
                features_ref[t, pl.ds(spot, 2 * atoms), :],
                NT,
                preferred_element_type=jnp.float32,
            )
            stored = jnp.minimum(couple, couples - 1)
            basis = [basis_ref[t, 2 * stored + half, where, :] for half in range(2)]
            near_grad_ref[t * (couples + 1) + couple] += jnp.dot(
                seed_t_ref[t, chunk],
                jnp.concatenate(basis, axis=1),
                preferred_element_type=jnp.float32,
            )

        def pull(place, grad_ref):
            t, couple, chunk = place
            start = pl.multiple_of(chunk * ROWS, ROWS)
            pulled = [[None] * 3 for _ in range(2)]
            for g in range(self.groups):
                rows = pl.ds(start + g * GROUP, GROUP)
                total = [None] * 3
                for half in range(2):
                    lanes = slice(half * atoms, (half + 1) * atoms)
                    offset, radial = self.geometry(t, 2 * couple + half, rows)
                    direct = [None] * 3
                    inner = None
                    for r, rate in enumerate(self.rates):
                        row = g * group_rows + 4 * r * GROUP
                        grad = [
                            grad_ref[row + m * GROUP : row + (m + 1) * GROUP, lanes]
                            for m in range(4)
                        ]
                        along = grad[0]
                        for m in range(3):
                            along = along + grad[m + 1] * offset[m]
                            part = radial[r] * grad[m + 1]
                            direct[m] = part if r == 0 else direct[m] + part
                        part = (radial[r] * (2.0 * rate)) * along
                        inner = part if r == 0 else inner + part
                    for m in range(3):
                        force = direct[m] - offset[m] * inner
                        total[m] = force if half == 0 else total[m] + force
                        old = pulled[half][m]
                        pulled[half][m] = force if g == 0 else old + force
                for m in range(3):
                    own_force_ref[t, m, rows, :] += total[m]
            for half in range(2):
                for m in range(3):
                    near_force_ref[t * (couples + 1) + couple, half, m] += pulled[half][m]

        one = enter(zero)
        two = following(one)
        multiply(one, grad_refs[0])
        multiply(two, grad_refs[1])

        def loop(k, places):
            one, two = places
            three = following(two)
            four = following(three)
            five = following(four)
            six = following(five)
            pull(one, grad_refs[0])
            multiply(three, grad_refs[2])
            pull(two, grad_refs[1])
            multiply(four, grad_refs[3])
            pull(three, grad_refs[2])
            multiply(five, grad_refs[0])
            pull(four, grad_refs[3])
            multiply(six, grad_refs[1])
            return five, six

        lax.fori_loop(0, (steps + 3) // 4, loop, (one, two))

    def give(self, row, half, tile, near_grad_ref, near_force_ref, ghost_ref):
        channels, atoms = self.channels, self.atoms
        lanes = slice(half * atoms, (half + 1) * atoms)
        ghost_ref[tile, :channels, :] += near_grad_ref[row, :, lanes]
        for m in range(3):
            ghost_ref[tile, channels + m : channels + m + 1, :] -= jnp.sum(
                near_force_ref[row, half, m], axis=0, keepdims=True
            )


def starts_of(piece_refs):
    return [sum(ref.shape[0] for ref in piece_refs[:k]) for k in range(len(piece_refs))]


def copies(pairs, sems):
    result = [
        pltpu.make_async_copy(source, target, sems.at[k])
        for k, (source, target) in enumerate(pairs)
    ]
    for copy in result:
        copy.start()
    return result


def main_kernel(
    pieces,
    outs,
    slots,
    line,
    counts_ref,
    table_ref,
    rates_ref,
    points_ref,
    mixing_ref,
    readout_ref,
    *refs,
):
    piece_refs = refs[:pieces]
    ghost_refs = refs[pieces : pieces + outs]
    (
        own_ref,
        other_ref,
        features_ref,
        basis_ref,
        seed_ref,
        seed_t_ref,
        own_force_ref,
        near_ref,
        sum_ref,
        near_grad_ref,
        near_force_ref,
        ghost_ref,
        in_sems,
        out_sems,
        *grad_refs,
    ) = refs[pieces + outs :]
    _, tiles, atoms = points_ref.shape
    channels = readout_ref.shape[1]
    couples = (slots + 1) // 2
    scaling = (slots * atoms) ** (-0.5)
    starts = starts_of(piece_refs)
    loads = copies(
        [
            (ref, near_ref.at[pl.ds(start, ref.shape[0])])
            for ref, start in zip(piece_refs, starts)
        ],
        in_sems,
    )

    for t in range(tiles):
        lines = [points_ref[m, t : t + 1, :] for m in range(3)]
        lines.append(jnp.zeros((atoms - 3, atoms), jnp.float32))
        columns = jnp.transpose(jnp.concatenate(lines, axis=0))
        for m in range(3):
            own_ref[t, m] = jnp.broadcast_to(columns[:, m : m + 1], (atoms, atoms))
    ghost_ref[...] = jnp.zeros_like(ghost_ref)
    own_force_ref[...] = jnp.zeros_like(own_force_ref)

    for load in loads:
        load.wait()

    pairs = Pairs(rates_ref, own_ref, other_ref, channels, atoms)
    radials, groups = len(pairs.rates), pairs.groups
    group_rows, chunk_rows = pairs.group_rows, pairs.chunk_rows

    for t in range(tiles):
        count = counts_ref[t]
        chunks = (count + (ROWS - 1)) // ROWS
        near = table_ref[t, slots]

        def work(t=t, count=count, chunks=chunks, near=near):
            for k in range(slots):
                tile = table_ref[t, k]
                live = tile >= 0
                tile = jnp.maximum(tile, 0)
                values = near_ref[tile, :atoms, :]
                features_ref[t, k * atoms : (k + 1) * atoms] = jnp.where(
                    live, values, jnp.zeros_like(values)
                )
                extra = near_ref[tile, atoms:, :].astype(jnp.float32)
                total = extra[0:3] + extra[3:6] + extra[6:9]
                for m in range(3):
                    other_ref[t, k, m] = jnp.broadcast_to(total[m : m + 1, :], (GROUP, atoms))
            for k in range(slots, 2 * couples + 2):
                for m in range(3):
                    other_ref[t, k, m] = jnp.zeros((GROUP, atoms), jnp.float32)
            features_ref[t, slots * atoms :] = jnp.zeros(
                ((2 * couples + 6 - slots) * atoms, channels), jnp.bfloat16
            )
            ahead = pl.ds(pl.multiple_of(near * atoms, atoms), atoms)
            behind = pl.ds(pl.multiple_of((near - 1) * atoms, atoms), atoms)
            spare = (2 * couples + 2) * atoms
            features_ref[t, spare + atoms : spare + 2 * atoms] = features_ref[t, ahead, :]
            features_ref[t, spare + 2 * atoms : spare + 3 * atoms] = features_ref[t, behind, :]

            def forward(chunk, carry):
                start = pl.multiple_of(chunk * ROWS, ROWS)
                base = pl.multiple_of(chunk * chunk_rows, chunk_rows)
                for slot in range(2 * couples):
                    for g in range(groups):
                        where = pl.ds(start + g * GROUP, GROUP)
                        offset, radial = pairs.geometry(t, slot, where)
                        for r in range(radials):
                            values = [radial[r]] + [radial[r] * offset[m] for m in range(3)]
                            for k in range(2):
                                pair = jnp.concatenate(values[2 * k : 2 * k + 2], axis=0)
                                row = base + g * group_rows + (4 * r + 2 * k) * GROUP
                                basis_ref[t, slot, pl.ds(row, 2 * GROUP), :] = pair.astype(
                                    jnp.bfloat16
                                )
                where = pl.ds(base, chunk_rows)
                basis = [basis_ref[t, slot, where, :] for slot in range(2 * couples)]
                sum_ref[t, where, :] = (
                    jnp.dot(
                        jnp.concatenate(basis, axis=1),
                        features_ref[t, : 2 * couples * atoms],
                        preferred_element_type=jnp.float32,
                    )
                    * scaling
                )
                return carry

            lax.fori_loop(0, chunks, forward, 0)

            def clear(chunk, carry):
                where = pl.ds(pl.multiple_of(chunk * chunk_rows, chunk_rows), chunk_rows)
                sum_ref[t, where, :] = jnp.zeros((chunk_rows, channels), jnp.float32)
                return carry

            lax.fori_loop(chunks, atoms // ROWS, clear, 0)

            def sums(r, m):
                first = (4 * r + m) * GROUP
                return jnp.concatenate(
                    [
                        sum_ref[t, g * group_rows + first : g * group_rows + first + GROUP, :]
                        for g in range(atoms // GROUP)
                    ],
                    axis=0,
                )

            parts = [sums(r, 0) for r in range(radials)]
            for r in range(radials):
                norm = None
                for m in range(1, 4):
                    value = sums(r, m)
                    norm = value * value if norm is None else norm + value * value
                parts.append(norm)
            invariant = jnp.concatenate([part.astype(jnp.bfloat16) for part in parts], axis=1)
            preact = jnp.dot(invariant, mixing_ref[...], preferred_element_type=jnp.float32)
            sigmoid = jax.nn.sigmoid(preact)
            row = lax.broadcasted_iota(jnp.int32, (atoms, channels), 0)
            valid = (row < count).astype(jnp.float32)
            grad_pre = valid * readout_ref[...] * sigmoid * (1.0 + preact * (1.0 - sigmoid))
            grad = lax.dot_general(
                grad_pre.astype(jnp.bfloat16),
                mixing_ref[...],
                NT,
                preferred_element_type=jnp.float32,
            )
            for r in range(radials):
                scalar = grad[:, r * channels : (r + 1) * channels] * scaling
                square = grad[:, (radials + r) * channels : (radials + r + 1) * channels]
                square = square * (2.0 * scaling)
                values = [scalar] + [square * sums(r, m) for m in range(1, 4)]
                for g in range(atoms // GROUP):
                    rows = slice(g * GROUP, (g + 1) * GROUP)
                    for k in range(2):
                        pair = jnp.concatenate(
                            [value[rows] for value in values[2 * k : 2 * k + 2]], axis=0
                        )
                        first = g * group_rows + (4 * r + 2 * k) * GROUP
                        seed_ref[t, first : first + 2 * GROUP, :] = pair.astype(jnp.bfloat16)
            for chunk in range(atoms // ROWS):
                rows = slice(chunk * chunk_rows, (chunk + 1) * chunk_rows)
                seed_t_ref[t, chunk] = jnp.transpose(seed_ref[t, rows, :])

        pl.when(count > 0)(work)

    counts = [counts_ref[t] for t in range(tiles)]
    nears = [table_ref[t, slots] for t in range(tiles)]
    totals = [table_ref[t, slots + 1] for t in range(tiles)]
    active = [(counts[t] > 0) & (totals[t] > nears[t]) for t in range(tiles)]
    firsts = [nears[t] // 2 for t in range(tiles)]
    lasts = [jnp.where(active[t], (totals[t] + 1) // 2, firsts[t]) for t in range(tiles)]

    def distant():
        pairs.backward(
            [(count + (ROWS - 1)) // ROWS for count in counts],
            firsts,
            lasts,
            [jnp.where(nears[t] % 2 == 1, firsts[t], -1) for t in range(tiles)],
            couples + 1,
            couples,
            seed_ref,
            seed_t_ref,
            features_ref,
            basis_ref,
            near_grad_ref,
            near_force_ref,
            own_force_ref,
            grad_refs,
        )
        for t in range(tiles):
            for slot in range(1, slots):

                def give(t=t, slot=slot):
                    tile = table_ref[t, slot]
                    plane = lax.div(tile, line[1])
                    tile = tile - line[0] * (plane + 1)
                    row = t * (couples + 1) + slot // 2
                    pairs.give(row, slot % 2, tile, near_grad_ref, near_force_ref, ghost_ref)

                pl.when(active[t] & (slot >= nears[t]) & (slot < totals[t]))(give)

    some = active[0]
    for t in range(1, tiles):
        some = some | active[t]
    pl.when(some)(distant)

    starts = starts_of(ghost_refs)
    for store in copies(
        [
            (ghost_ref.at[pl.ds(start, ref.shape[0])], ref)
            for ref, start in zip(ghost_refs, starts)
        ],
        out_sems,
    ):
        store.wait()


def line_kernel(
    outs,
    slots,
    line,
    counts_ref,
    table_ref,
    rates_ref,
    own_ref,
    other_ref,
    features_ref,
    basis_ref,
    seed_ref,
    seed_t_ref,
    far_force_ref,
    *refs,
):
    ghost_refs = refs[:outs]
    near_grad_ref, near_force_ref, own_force_ref, ghost_ref, out_sems, *grad_refs = refs[outs:]
    tiles, _, atoms, _ = own_ref.shape
    channels = features_ref.shape[2]
    couples = (slots + 1) // 2
    pairs = Pairs(rates_ref, own_ref, other_ref, channels, atoms)
    ghost_ref[...] = jnp.zeros_like(ghost_ref)
    own_force_ref[...] = far_force_ref[...]
    counts = [counts_ref[t] for t in range(tiles)]
    nears = [table_ref[t, slots] for t in range(tiles)]
    zero = jnp.zeros((), jnp.int32)

    def linear():
        pairs.backward(
            [(count + (ROWS - 1)) // ROWS for count in counts],
            [zero] * tiles,
            [jnp.where(counts[t] > 0, (nears[t] + 1) // 2, 0) for t in range(tiles)],
            [jnp.where(nears[t] % 2 == 1, nears[t] // 2, -1) for t in range(tiles)],
            couples + 2,
            couples,
            seed_ref,
            seed_t_ref,
            features_ref,
            basis_ref,
            near_grad_ref,
            near_force_ref,
            own_force_ref,
            grad_refs,
        )
        for t in range(tiles):
            for slot in range(slots):

                def give(t=t, slot=slot):
                    tile = table_ref[t, slot]
                    tile = tile - (line[1] - line[0]) * lax.div(tile, line[1])
                    row = t * (couples + 1) + slot // 2
                    pairs.give(row, slot % 2, tile, near_grad_ref, near_force_ref, ghost_ref)

                pl.when((counts[t] > 0) & (slot < nears[t]))(give)

            def own(t=t):
                for m in range(3):
                    ghost_ref[t, channels + m : channels + m + 1, :] += jnp.sum(
                        jnp.transpose(own_force_ref[t, m]), axis=0, keepdims=True
                    )

            pl.when(counts[t] > 0)(own)

    some = counts[0] > 0
    for t in range(1, tiles):
        some = some | (counts[t] > 0)
    pl.when(some)(linear)
    starts = starts_of(ghost_refs)
    for store in copies(
        [
            (ghost_ref.at[pl.ds(start, ref.shape[0])], ref)
            for ref, start in zip(ghost_refs, starts)
        ],
        out_sems,
    ):
        store.wait()


def final_kernel(counts_ref, center_ref, *refs):
    coded_refs = refs[:-2]
    forces_ref, grads_ref = refs[-2:]
    tiles, channels, atoms = grads_ref.shape
    for t in range(tiles):
        rows = slice(t, t + 1)
        grads = center_ref[rows, :channels]
        forces = center_ref[rows, channels : channels + 3]
        for ref in coded_refs:
            one, two = decoded(ref, rows)
            grads, forces = grads + one, forces + two
        forces_ref[:, t, :] = forces[0]
        column = lax.broadcasted_iota(jnp.int32, (channels, atoms), 1)
        masked = jnp.where(column < counts_ref[t], grads[0], 0.0)
        grads_ref[t] = jnp.transpose(masked)


def step(positions, features, counts, neighbours, mix_weight, readout, radial_rates):
    tiles, atoms = positions.shape[3], positions.shape[5]
    channels = features.shape[5]
    slots = neighbours.shape[4]
    radials = radial_rates.shape[0]
    vmem = pl.BlockSpec(memory_space=pltpu.VMEM)
    smem = pl.BlockSpec(memory_space=pltpu.SMEM)
    hbm = pl.BlockSpec(memory_space=pl.ANY)
    small = pltpu.CompilerParams(vmem_limit_bytes=SMALL)

    def swap(value, axis):
        return [lax.ppermute(value, axis, pairs) for pairs in swaps(axis)]

    sides = tuple(len(swaps(axis)) for axis in ("gx", "gy", "gz"))
    own_counts = counts.reshape(tiles)
    points = jnp.transpose(positions, (0, 1, 2, 4, 3, 5)).reshape(3, tiles, atoms)
    packed = pl.pallas_call(
        pack_kernel,
        out_shape=jax.ShapeDtypeStruct((tiles, atoms + 16, channels), jnp.bfloat16),
        in_specs=[smem, vmem, vmem],
        out_specs=vmem,
        scratch_shapes=[pltpu.VMEM((tiles, 16, channels), jnp.float32)],
        compiler_params=pltpu.CompilerParams(vmem_limit_bytes=60 << 20),
        name="pack",
    )(own_counts, features.reshape(tiles, atoms, channels), points)
    along_z = swap(packed, "gz")
    own_counts, table, local = pl.pallas_call(
        functools.partial(side_kernel, sides),
        out_shape=[
            jax.ShapeDtypeStruct((tiles,), jnp.int32),
            jax.ShapeDtypeStruct((tiles, slots + 2), jnp.int32),
            jax.ShapeDtypeStruct(packed.shape, packed.dtype),
        ],
        in_specs=[smem, smem, smem, vmem],
        out_specs=[smem, smem, vmem],
        compiler_params=small,
        name="sides",
    )(
        jnp.stack([lax.axis_index(axis) % 2 for axis in ("gx", "gy", "gz")]),
        own_counts,
        neighbours.reshape(tiles, slots),
        packed,
    )
    (line,) = join([list(range(1 + len(along_z)))], local, *along_z)
    lines = [line] + swap(line, "gy")
    rates, points, readout, mix_weight = pl.pallas_call(
        stage_kernel,
        out_shape=[
            jax.ShapeDtypeStruct((radials,), jnp.float32),
            jax.ShapeDtypeStruct((3, tiles, atoms), jnp.float32),
            jax.ShapeDtypeStruct((1, channels), jnp.float32),
            jax.ShapeDtypeStruct(mix_weight.shape, mix_weight.dtype),
        ],
        in_specs=[smem, vmem, vmem, vmem],
        out_specs=[smem, vmem, vmem, vmem],
        compiler_params=small,
        name="stage",
    )(radial_rates, points, readout.reshape(1, channels), mix_weight)
    pieces = [lines]
    for pairs in swaps("gx"):
        plane = [lax.ppermute(line, "gx", pairs)]
        pieces.append(plane + [lax.ppermute(piece, "gx", pairs) for piece in lines[1:]])
    flat = [piece for plane in pieces for piece in plane]

    total = sum(piece.shape[0] for piece in flat)
    couples = (slots + 1) // 2
    bases = 4 * radials
    chunks = atoms // ROWS
    ghost_rows = channels + EXTRA
    counts_of = (line.shape[0], total // len(pieces))

    def ghost_shapes(arrays):
        return [
            jax.ShapeDtypeStruct((array.shape[0], ghost_rows, atoms), jnp.float32)
            for array in arrays
        ]

    far_shapes = ghost_shapes([piece for plane in pieces for piece in plane[1:]])
    line_shapes = ghost_shapes([plane[0] for plane in pieces])
    state_shapes = [
        jax.ShapeDtypeStruct((tiles, 3, atoms, atoms), jnp.float32),
        jax.ShapeDtypeStruct((tiles, 2 * couples + 2, 3, GROUP, atoms), jnp.float32),
        jax.ShapeDtypeStruct((tiles, (2 * couples + 6) * atoms, channels), jnp.bfloat16),
        jax.ShapeDtypeStruct((tiles, 2 * couples, bases * atoms, atoms), jnp.bfloat16),
        jax.ShapeDtypeStruct((tiles, bases * atoms, channels), jnp.bfloat16),
        jax.ShapeDtypeStruct((tiles, chunks, channels, bases * ROWS), jnp.bfloat16),
        jax.ShapeDtypeStruct((tiles, 3, atoms, atoms), jnp.float32),
    ]
    sums = [
        pltpu.VMEM((tiles * (couples + 1), channels, 2 * atoms), jnp.float32),
        pltpu.VMEM((tiles * (couples + 1), 2, 3, GROUP, atoms), jnp.float32),
    ]
    buffers = [pltpu.VMEM((bases * ROWS, 2 * atoms), jnp.float32)] * 4
    large = pltpu.CompilerParams(vmem_limit_bytes=LARGE)
    results = pl.pallas_call(
        functools.partial(main_kernel, len(flat), len(far_shapes), slots, counts_of),
        out_shape=far_shapes + state_shapes,
        in_specs=[smem] * 3 + [vmem] * 3 + [hbm] * len(flat),
        out_specs=[hbm] * len(far_shapes) + [vmem] * len(state_shapes),
        scratch_shapes=[
            pltpu.VMEM((total, atoms + 16, channels), jnp.bfloat16),
            pltpu.VMEM((tiles, bases * atoms, channels), jnp.float32),
            *sums,
            pltpu.VMEM(
                (sum(shape.shape[0] for shape in far_shapes), ghost_rows, atoms), jnp.float32
            ),
            pltpu.SemaphoreType.DMA((len(flat),)),
            pltpu.SemaphoreType.DMA((len(far_shapes),)),
            *buffers,
        ],
        compiler_params=large,
        name="pairs",
    )(own_counts, table, rates, points, mix_weight, readout, *flat)
    state = results[len(far_shapes) :]
    line_ghosts = pl.pallas_call(
        functools.partial(line_kernel, len(line_shapes), slots, counts_of),
        out_shape=line_shapes,
        in_specs=[smem] * 3 + [vmem] * len(state),
        out_specs=[hbm] * len(line_shapes),
        scratch_shapes=[
            *sums,
            pltpu.VMEM((tiles, 3, atoms, atoms), jnp.float32),
            pltpu.VMEM(
                (sum(shape.shape[0] for shape in line_shapes), ghost_rows, atoms), jnp.float32
            ),
            pltpu.SemaphoreType.DMA((len(line_shapes),)),
            *buffers,
        ],
        compiler_params=large,
        name="lines",
    )(own_counts, table, rates, *state)
    width = len(pieces[0]) - 1
    ghosts = [
        [line_ghosts[k]] + list(results[k * width : (k + 1) * width]) for k in range(len(pieces))
    ]

    def gather(k):
        arrays = [ghosts[0][k]]
        for plane, pairs in zip(ghosts[1:], swaps("gx")):
            arrays.append(lax.ppermute(plane[k], "gx", pairs))
        return arrays

    received = []
    for k, pairs in enumerate(swaps("gy")):
        arrays = gather(k + 1)
        (value,) = fold([(0, arrays[0].shape[0], True)], arrays, [])
        received.append(send(value, "gy", pairs))
    arrays = gather(0)
    cuts = [(k * tiles, (k + 1) * tiles, k > 0) for k in range(sides[2] + 1)]
    center, *along_z = fold(cuts, arrays, received)
    parts = [center]
    for value, pairs in zip(along_z, swaps("gz")):
        parts.append(send(value, "gz", pairs))

    forces, grads = pl.pallas_call(
        final_kernel,
        out_shape=[
            jax.ShapeDtypeStruct((3, tiles, atoms), jnp.float32),
            jax.ShapeDtypeStruct((tiles, channels, atoms), jnp.float32),
        ],
        in_specs=[smem] + [vmem] * len(parts),
        out_specs=[vmem, vmem],
        compiler_params=small,
        name="finish",
    )(own_counts, *parts)
    forces = jnp.transpose(forces.reshape(1, 1, 1, 3, tiles, atoms), (0, 1, 2, 4, 3, 5))
    return forces, grads.reshape(1, 1, 1, tiles, atoms, channels)


def solution(mesh):
    in_specs = (
        P("gx", "gy", "gz", None, None, None),
        P("gx", "gy", "gz", None, None, None),
        P("gx", "gy", "gz", None),
        P("gx", "gy", "gz", None, None),
        P(),
        P(),
        P(),
    )
    out_specs = (P("gx", "gy", "gz", None, None, None), P("gx", "gy", "gz", None, None, None))
    return jax.shard_map(step, mesh=mesh, in_specs=in_specs, out_specs=out_specs, check_vma=False)
```

```python
import functools

import jax
import jax.numpy as jnp
from jax import lax
from jax.experimental import pallas as pl
from jax.experimental.pallas import tpu as pltpu
from jax.sharding import PartitionSpec as P


ROWS = 32
EXTRA = 8
TOP = 14.0
TINY = 1e-30
GROUP = 8
LOG2E = 1.4426950408889634
SMALL = 8 << 20
LARGE = 20 << 20
NT = (((1,), (1,)), ((), ()))


def swaps(axis):
    count = lax.axis_size(axis)
    result = []
    for first in (0, 1):
        pairs = [(i, i + 1) for i in range(first, count - 1, 2)]
        if pairs:
            result.append(pairs + [(b, a) for a, b in pairs])
    return result


def side_of(step, parity, sides):
    side = jnp.where((step == 1) == (parity == 0), 1, 2)
    return jnp.minimum(jnp.where(step == 0, 0, side), sides)


def pack_kernel(counts_ref, features_ref, points_ref, packed_ref, extra_ref):
    tiles, atoms, _ = features_ref.shape
    extra_ref[...] = jnp.zeros_like(extra_ref)
    for t in range(tiles):
        count = counts_ref[t]
        rows = lax.broadcasted_iota(jnp.int32, features_ref.shape[1:], 0)
        values = features_ref[t].astype(jnp.float32)
        packed_ref[t, :atoms] = jnp.where(rows < count, values, 0.0).astype(jnp.bfloat16)
        rest = points_ref[:, t, :]
        for term in range(3):
            part = rest.astype(jnp.bfloat16).astype(jnp.float32)
            extra_ref[t, 3 * term : 3 * term + 3] = part
            rest = rest - part
        packed_ref[t, atoms:] = extra_ref[t].astype(jnp.bfloat16)


def side_kernel(
    sides,
    axis_ref,
    counts_ref,
    neighbours_ref,
    packed_ref,
    out_counts_ref,
    out_table_ref,
    out_packed_ref,
):
    tiles, slots = neighbours_ref.shape
    for t in range(tiles):
        out_counts_ref[t] = counts_ref[t]
        spots = []
        for k in range(slots):
            target = jnp.maximum(neighbours_ref[t, k], 0)
            block = lax.div(target, tiles)
            steps = (lax.div(block, 9), lax.rem(lax.div(block, 3), 3), lax.rem(block, 3))
            x, y, z = (side_of(steps[m] - 1, axis_ref[m], sides[m]) for m in range(3))
            block = (x * (sides[1] + 1) + y) * (sides[2] + 1) + z
            live = neighbours_ref[t, k] >= 0
            spots.append((block * tiles + lax.rem(target, tiles), live, live & (y == 0)))
            out_table_ref[t, k] = -1
        near = sum(jnp.where(line, 1, 0) for _, _, line in spots)
        total = sum(jnp.where(live, 1, 0) for _, live, _ in spots)
        out_table_ref[t, slots] = near
        out_table_ref[t, slots + 1] = total
        at_near, at_far = jnp.zeros((), jnp.int32), near
        for spot, live, line in spots:

            def put(spot=spot, at=jnp.where(line, at_near, at_far)):
                out_table_ref[t, at] = spot

            pl.when(live)(put)
            at_near = at_near + jnp.where(line, 1, 0)
            at_far = at_far + jnp.where(live & ~line, 1, 0)
    out_packed_ref[...] = packed_ref[...]


def stage_kernel(rates_ref, points_ref, readout_ref, mixing_ref, *out_refs):
    for r in range(rates_ref.shape[0]):
        out_refs[0][r] = rates_ref[r]
    out_refs[1][...] = points_ref[...]
    out_refs[2][...] = readout_ref[...]
    out_refs[3][...] = mixing_ref[...]


def join_kernel(groups, *refs):
    inputs = refs[: -len(groups)]
    for group, out_ref in zip(groups, refs[-len(groups) :]):
        at = 0
        for k in group:
            count = inputs[k].shape[0]
            out_ref[at : at + count] = inputs[k][...]
            at += count


def join(groups, *arrays):
    shapes = [
        jax.ShapeDtypeStruct(
            (sum(arrays[k].shape[0] for k in group),) + arrays[0].shape[1:], arrays[0].dtype
        )
        for group in groups
    ]
    vmem = pl.BlockSpec(memory_space=pltpu.VMEM)
    return pl.pallas_call(
        functools.partial(join_kernel, groups),
        out_shape=shapes,
        in_specs=[vmem] * len(arrays),
        out_specs=[vmem] * len(groups),
        compiler_params=pltpu.CompilerParams(vmem_limit_bytes=SMALL),
        name="join",
    )(*arrays)


def decoded(ref, rows):
    value = ref[rows]
    channels = value.shape[1] - EXTRA
    grads = value[:, :channels] * jnp.exp2(value[:, channels + 3 : channels + 4] - TOP)
    forces = value[:, channels : channels + 3] * jnp.exp2(
        value[:, channels + 4 : channels + 5] - TOP
    )
    return grads, forces


def fold_kernel(cuts, plain, coded, *refs):
    plain_refs, coded_refs = refs[:plain], refs[plain : plain + coded]
    for (low, high, code), out_ref in zip(cuts, refs[plain + coded :]):
        channels = out_ref.shape[1] - EXTRA
        rows = slice(low, high)
        grads = forces = None
        for ref in plain_refs:
            part = ref[rows]
            grads = part[:, :channels] if grads is None else grads + part[:, :channels]
            part = part[:, channels : channels + 3]
            forces = part if forces is None else forces + part
        for ref in coded_refs:
            one, two = decoded(ref, rows)
            grads, forces = grads + one, forces + two
        if not code:
            out_ref[:, :channels] = grads
            out_ref[:, channels : channels + 3] = forces
            continue
        for first, value, at in ((0, grads, 3), (channels, forces, 4)):
            bound = jnp.max(jnp.abs(value), axis=1, keepdims=True)
            exponent = jnp.ceil(jnp.log2(jnp.maximum(bound, TINY)))
            out_ref[:, first : first + value.shape[1]] = value * jnp.exp2(TOP - exponent)
            out_ref[:, channels + at : channels + at + 1] = exponent


def fold(cuts, plain, coded):
    arrays = list(plain) + list(coded)
    shapes = [
        jax.ShapeDtypeStruct((high - low,) + arrays[0].shape[1:], jnp.float32)
        for low, high, _ in cuts
    ]
    vmem = pl.BlockSpec(memory_space=pltpu.VMEM)
    return pl.pallas_call(
        functools.partial(fold_kernel, cuts, len(plain), len(coded)),
        out_shape=shapes,
        in_specs=[vmem] * len(arrays),
        out_specs=[vmem] * len(cuts),
        compiler_params=pltpu.CompilerParams(vmem_limit_bytes=SMALL),
        name="fold",
    )(*arrays)


def send(value, axis, pairs):
    return lax.ppermute(value.astype(jnp.float16), axis, pairs).astype(jnp.float32)


class Pairs:
    def __init__(self, rates_ref, own_ref, other_ref, channels, atoms):
        self.rates = [rates_ref[r] for r in range(rates_ref.shape[0])]
        self.powers = [-rate * LOG2E for rate in self.rates]
        self.own_ref, self.other_ref = own_ref, other_ref
        self.channels, self.atoms = channels, atoms
        self.group_rows = 4 * len(self.rates) * GROUP
        self.groups = ROWS // GROUP
        self.chunk_rows = self.group_rows * self.groups

    def geometry(self, t, slot, where):
        offset = [self.other_ref[t, slot, m] - self.own_ref[t, m, where, :] for m in range(3)]
        square = offset[0] * offset[0] + offset[1] * offset[1] + offset[2] * offset[2]
        return offset, [jnp.exp2(power * square) for power in self.powers]

    def backward(
        self,
        chunks,
        firsts,
        lasts,
        masked,
        block,
        couples,
        seed_ref,
        seed_t_ref,
        features_ref,
        basis_ref,
        near_grad_ref,
        near_force_ref,
        own_force_ref,
        grad_refs,
    ):
        atoms, group_rows, chunk_rows = self.atoms, self.group_rows, self.chunk_rows
        near_grad_ref[...] = jnp.zeros_like(near_grad_ref)
        near_force_ref[...] = jnp.zeros_like(near_force_ref)
        tiles = len(chunks)
        lengths = [(lasts[k] - firsts[k]) * chunks[k] for k in range(tiles)]
        steps = sum(lengths)
        zero = jnp.zeros((), jnp.int32)

        def of(values, t):
            result = values[-1]
            for k in reversed(range(tiles - 1)):
                result = jnp.where(t == k, values[k], result)
            return result

        def enter(start):
            t = jnp.full((), tiles, jnp.int32)
            for k in reversed(range(tiles)):
                t = jnp.where((start <= k) & (lengths[k] > 0), k, t)
            found = t < tiles
            t = jnp.minimum(t, tiles - 1)
            return t, jnp.where(found, of(firsts, t), couples), zero

        def following(place):
            t, couple, chunk = place
            wrap = chunk + 1 >= of(chunks, t)
            end = wrap & (couple + 1 >= of(lasts, t))
            tile, start, _ = enter(t + 1)
            inside = jnp.where(wrap, couple + 1, couple)
            return (
                jnp.where(end, tile, t),
                jnp.where(end, start, inside),
                jnp.where(wrap, 0, chunk + 1),
            )

        def multiply(place, grad_ref):
            t, couple, chunk = place
            base = pl.multiple_of(chunk * chunk_rows, chunk_rows)
            where = pl.ds(base, chunk_rows)
            spot = jnp.where(couple == of(masked, t), block, couple)
            spot = pl.multiple_of(spot * 2 * atoms, 2 * atoms)
            grad_ref[...] = lax.dot_general(
                seed_ref[t, where, :],
                features_ref[t, pl.ds(spot, 2 * atoms), :],
                NT,
                preferred_element_type=jnp.float32,
            )
            stored = jnp.minimum(couple, couples - 1)
            basis = [basis_ref[t, 2 * stored + half, where, :] for half in range(2)]
            near_grad_ref[t * (couples + 1) + couple] += jnp.dot(
                seed_t_ref[t, chunk],
                jnp.concatenate(basis, axis=1),
                preferred_element_type=jnp.float32,
            )

        def pull(place, grad_ref):
            t, couple, chunk = place
            start = pl.multiple_of(chunk * ROWS, ROWS)
            pulled = [[None] * 3 for _ in range(2)]
            for g in range(self.groups):
                rows = pl.ds(start + g * GROUP, GROUP)
                total = [None] * 3
                for half in range(2):
                    lanes = slice(half * atoms, (half + 1) * atoms)
                    offset, radial = self.geometry(t, 2 * couple + half, rows)
                    direct = [None] * 3
                    inner = None
                    for r, rate in enumerate(self.rates):
                        row = g * group_rows + 4 * r * GROUP
                        grad = [
                            grad_ref[row + m * GROUP : row + (m + 1) * GROUP, lanes]
                            for m in range(4)
                        ]
                        along = grad[0]
                        for m in range(3):
                            along = along + grad[m + 1] * offset[m]
                            part = radial[r] * grad[m + 1]
                            direct[m] = part if r == 0 else direct[m] + part
                        part = (radial[r] * (2.0 * rate)) * along
                        inner = part if r == 0 else inner + part
                    for m in range(3):
                        force = direct[m] - offset[m] * inner
                        total[m] = force if half == 0 else total[m] + force
                        old = pulled[half][m]
                        pulled[half][m] = force if g == 0 else old + force
                for m in range(3):
                    own_force_ref[t, m, rows, :] += total[m]
            for half in range(2):
                for m in range(3):
                    near_force_ref[t * (couples + 1) + couple, half, m] += pulled[half][m]

        one = enter(zero)
        two = following(one)
        multiply(one, grad_refs[0])
        multiply(two, grad_refs[1])

        def loop(k, places):
            one, two = places
            three = following(two)
            four = following(three)
            five = following(four)
            six = following(five)
            pull(one, grad_refs[0])
            multiply(three, grad_refs[2])
            pull(two, grad_refs[1])
            multiply(four, grad_refs[3])
            pull(three, grad_refs[2])
            multiply(five, grad_refs[0])
            pull(four, grad_refs[3])
            multiply(six, grad_refs[1])
            return five, six

        lax.fori_loop(0, (steps + 3) // 4, loop, (one, two))

    def give(self, row, half, tile, near_grad_ref, near_force_ref, ghost_ref):
        channels, atoms = self.channels, self.atoms
        lanes = slice(half * atoms, (half + 1) * atoms)
        ghost_ref[tile, :channels, :] += near_grad_ref[row, :, lanes]
        for m in range(3):
            ghost_ref[tile, channels + m : channels + m + 1, :] -= jnp.sum(
                near_force_ref[row, half, m], axis=0, keepdims=True
            )


def starts_of(piece_refs):
    return [sum(ref.shape[0] for ref in piece_refs[:k]) for k in range(len(piece_refs))]


def copies(pairs, sems):
    result = [
        pltpu.make_async_copy(source, target, sems.at[k])
        for k, (source, target) in enumerate(pairs)
    ]
    for copy in result:
        copy.start()
    return result


def main_kernel(
    pieces,
    outs,
    slots,
    line,
    counts_ref,
    table_ref,
    rates_ref,
    points_ref,
    mixing_ref,
    readout_ref,
    *refs,
):
    piece_refs = refs[:pieces]
    ghost_refs = refs[pieces : pieces + outs]
    (
        own_ref,
        other_ref,
        features_ref,
        basis_ref,
        seed_ref,
        seed_t_ref,
        own_force_ref,
        near_ref,
        sum_ref,
        near_grad_ref,
        near_force_ref,
        ghost_ref,
        in_sems,
        out_sems,
        *grad_refs,
    ) = refs[pieces + outs :]
    _, tiles, atoms = points_ref.shape
    channels = readout_ref.shape[1]
    couples = (slots + 1) // 2
    scaling = (slots * atoms) ** (-0.5)
    starts = starts_of(piece_refs)
    loads = copies(
        [
            (ref, near_ref.at[pl.ds(start, ref.shape[0])])
            for ref, start in zip(piece_refs, starts)
        ],
        in_sems,
    )

    for t in range(tiles):
        lines = [points_ref[m, t : t + 1, :] for m in range(3)]
        lines.append(jnp.zeros((atoms - 3, atoms), jnp.float32))
        columns = jnp.transpose(jnp.concatenate(lines, axis=0))
        for m in range(3):
            own_ref[t, m] = jnp.broadcast_to(columns[:, m : m + 1], (atoms, atoms))
    ghost_ref[...] = jnp.zeros_like(ghost_ref)
    own_force_ref[...] = jnp.zeros_like(own_force_ref)

    for load in loads:
        load.wait()

    pairs = Pairs(rates_ref, own_ref, other_ref, channels, atoms)
    radials, groups = len(pairs.rates), pairs.groups
    group_rows, chunk_rows = pairs.group_rows, pairs.chunk_rows

    for t in range(tiles):
        count = counts_ref[t]
        chunks = (count + (ROWS - 1)) // ROWS
        near = table_ref[t, slots]

        def work(t=t, count=count, chunks=chunks, near=near):
            for k in range(slots):
                tile = table_ref[t, k]
                live = tile >= 0
                tile = jnp.maximum(tile, 0)
                values = near_ref[tile, :atoms, :]
                features_ref[t, k * atoms : (k + 1) * atoms] = jnp.where(
                    live, values, jnp.zeros_like(values)
                )
                extra = near_ref[tile, atoms:, :].astype(jnp.float32)
                total = extra[0:3] + extra[3:6] + extra[6:9]
                for m in range(3):
                    other_ref[t, k, m] = jnp.broadcast_to(total[m : m + 1, :], (GROUP, atoms))
            for k in range(slots, 2 * couples + 2):
                for m in range(3):
                    other_ref[t, k, m] = jnp.zeros((GROUP, atoms), jnp.float32)
            features_ref[t, slots * atoms :] = jnp.zeros(
                ((2 * couples + 6 - slots) * atoms, channels), jnp.bfloat16
            )
            ahead = pl.ds(pl.multiple_of(near * atoms, atoms), atoms)
            behind = pl.ds(pl.multiple_of((near - 1) * atoms, atoms), atoms)
            spare = (2 * couples + 2) * atoms
            features_ref[t, spare + atoms : spare + 2 * atoms] = features_ref[t, ahead, :]
            features_ref[t, spare + 2 * atoms : spare + 3 * atoms] = features_ref[t, behind, :]

            def forward(chunk, carry):
                start = pl.multiple_of(chunk * ROWS, ROWS)
                base = pl.multiple_of(chunk * chunk_rows, chunk_rows)
                for slot in range(2 * couples):
                    for g in range(groups):
                        where = pl.ds(start + g * GROUP, GROUP)
                        offset, radial = pairs.geometry(t, slot, where)
                        for r in range(radials):
                            values = [radial[r]] + [radial[r] * offset[m] for m in range(3)]
                            for k in range(2):
                                pair = jnp.concatenate(values[2 * k : 2 * k + 2], axis=0)
                                row = base + g * group_rows + (4 * r + 2 * k) * GROUP
                                basis_ref[t, slot, pl.ds(row, 2 * GROUP), :] = pair.astype(
                                    jnp.bfloat16
                                )
                where = pl.ds(base, chunk_rows)
                basis = [basis_ref[t, slot, where, :] for slot in range(2 * couples)]
                sum_ref[t, where, :] = (
                    jnp.dot(
                        jnp.concatenate(basis, axis=1),
                        features_ref[t, : 2 * couples * atoms],
                        preferred_element_type=jnp.float32,
                    )
                    * scaling
                )
                return carry

            lax.fori_loop(0, chunks, forward, 0)

            def clear(chunk, carry):
                where = pl.ds(pl.multiple_of(chunk * chunk_rows, chunk_rows), chunk_rows)
                sum_ref[t, where, :] = jnp.zeros((chunk_rows, channels), jnp.float32)
                return carry

            lax.fori_loop(chunks, atoms // ROWS, clear, 0)

            def sums(r, m):
                first = (4 * r + m) * GROUP
                return jnp.concatenate(
                    [
                        sum_ref[t, g * group_rows + first : g * group_rows + first + GROUP, :]
                        for g in range(atoms // GROUP)
                    ],
                    axis=0,
                )

            parts = [sums(r, 0) for r in range(radials)]
            for r in range(radials):
                norm = None
                for m in range(1, 4):
                    value = sums(r, m)
                    norm = value * value if norm is None else norm + value * value
                parts.append(norm)
            invariant = jnp.concatenate([part.astype(jnp.bfloat16) for part in parts], axis=1)
            preact = jnp.dot(invariant, mixing_ref[...], preferred_element_type=jnp.float32)
            sigmoid = jax.nn.sigmoid(preact)
            row = lax.broadcasted_iota(jnp.int32, (atoms, channels), 0)
            valid = (row < count).astype(jnp.float32)
            grad_pre = valid * readout_ref[...] * sigmoid * (1.0 + preact * (1.0 - sigmoid))
            grad = lax.dot_general(
                grad_pre.astype(jnp.bfloat16),
                mixing_ref[...],
                NT,
                preferred_element_type=jnp.float32,
            )
            for r in range(radials):
                scalar = grad[:, r * channels : (r + 1) * channels] * scaling
                square = grad[:, (radials + r) * channels : (radials + r + 1) * channels]
                square = square * (2.0 * scaling)
                values = [scalar] + [square * sums(r, m) for m in range(1, 4)]
                for g in range(atoms // GROUP):
                    rows = slice(g * GROUP, (g + 1) * GROUP)
                    for k in range(2):
                        pair = jnp.concatenate(
                            [value[rows] for value in values[2 * k : 2 * k + 2]], axis=0
                        )
                        first = g * group_rows + (4 * r + 2 * k) * GROUP
                        seed_ref[t, first : first + 2 * GROUP, :] = pair.astype(jnp.bfloat16)
            for chunk in range(atoms // ROWS):
                rows = slice(chunk * chunk_rows, (chunk + 1) * chunk_rows)
                seed_t_ref[t, chunk] = jnp.transpose(seed_ref[t, rows, :])

        pl.when(count > 0)(work)

    counts = [counts_ref[t] for t in range(tiles)]
    nears = [table_ref[t, slots] for t in range(tiles)]
    totals = [table_ref[t, slots + 1] for t in range(tiles)]
    active = [(counts[t] > 0) & (totals[t] > nears[t]) for t in range(tiles)]
    firsts = [nears[t] // 2 for t in range(tiles)]
    lasts = [jnp.where(active[t], (totals[t] + 1) // 2, firsts[t]) for t in range(tiles)]

    def distant():
        pairs.backward(
            [(count + (ROWS - 1)) // ROWS for count in counts],
            firsts,
            lasts,
            [jnp.where(nears[t] % 2 == 1, firsts[t], -1) for t in range(tiles)],
            couples + 1,
            couples,
            seed_ref,
            seed_t_ref,
            features_ref,
            basis_ref,
            near_grad_ref,
            near_force_ref,
            own_force_ref,
            grad_refs,
        )
        for t in range(tiles):
            for slot in range(1, slots):

                def give(t=t, slot=slot):
                    tile = table_ref[t, slot]
                    plane = lax.div(tile, line[1])
                    tile = tile - line[0] * (plane + 1)
                    row = t * (couples + 1) + slot // 2
                    pairs.give(row, slot % 2, tile, near_grad_ref, near_force_ref, ghost_ref)

                pl.when(active[t] & (slot >= nears[t]) & (slot < totals[t]))(give)

    some = active[0]
    for t in range(1, tiles):
        some = some | active[t]
    pl.when(some)(distant)

    starts = starts_of(ghost_refs)
    for store in copies(
        [
            (ghost_ref.at[pl.ds(start, ref.shape[0])], ref)
            for ref, start in zip(ghost_refs, starts)
        ],
        out_sems,
    ):
        store.wait()


def line_kernel(
    outs,
    slots,
    line,
    counts_ref,
    table_ref,
    rates_ref,
    own_ref,
    other_ref,
    features_ref,
    basis_ref,
    seed_ref,
    seed_t_ref,
    far_force_ref,
    *refs,
):
    ghost_refs = refs[:outs]
    near_grad_ref, near_force_ref, own_force_ref, ghost_ref, out_sems, *grad_refs = refs[outs:]
    tiles, _, atoms, _ = own_ref.shape
    channels = features_ref.shape[2]
    couples = (slots + 1) // 2
    pairs = Pairs(rates_ref, own_ref, other_ref, channels, atoms)
    ghost_ref[...] = jnp.zeros_like(ghost_ref)
    own_force_ref[...] = far_force_ref[...]
    counts = [counts_ref[t] for t in range(tiles)]
    nears = [table_ref[t, slots] for t in range(tiles)]
    zero = jnp.zeros((), jnp.int32)

    def linear():
        pairs.backward(
            [(count + (ROWS - 1)) // ROWS for count in counts],
            [zero] * tiles,
            [jnp.where(counts[t] > 0, (nears[t] + 1) // 2, 0) for t in range(tiles)],
            [jnp.where(nears[t] % 2 == 1, nears[t] // 2, -1) for t in range(tiles)],
            couples + 2,
            couples,
            seed_ref,
            seed_t_ref,
            features_ref,
            basis_ref,
            near_grad_ref,
            near_force_ref,
            own_force_ref,
            grad_refs,
        )
        for t in range(tiles):
            for slot in range(slots):

                def give(t=t, slot=slot):
                    tile = table_ref[t, slot]
                    tile = tile - (line[1] - line[0]) * lax.div(tile, line[1])
                    row = t * (couples + 1) + slot // 2
                    pairs.give(row, slot % 2, tile, near_grad_ref, near_force_ref, ghost_ref)

                pl.when((counts[t] > 0) & (slot < nears[t]))(give)

            def own(t=t):
                for m in range(3):
                    ghost_ref[t, channels + m : channels + m + 1, :] += jnp.sum(
                        jnp.transpose(own_force_ref[t, m]), axis=0, keepdims=True
                    )

            pl.when(counts[t] > 0)(own)

    some = counts[0] > 0
    for t in range(1, tiles):
        some = some | (counts[t] > 0)
    pl.when(some)(linear)
    starts = starts_of(ghost_refs)
    for store in copies(
        [
            (ghost_ref.at[pl.ds(start, ref.shape[0])], ref)
            for ref, start in zip(ghost_refs, starts)
        ],
        out_sems,
    ):
        store.wait()


def final_kernel(counts_ref, center_ref, *refs):
    coded_refs = refs[:-2]
    forces_ref, grads_ref = refs[-2:]
    tiles, channels, atoms = grads_ref.shape
    for t in range(tiles):
        rows = slice(t, t + 1)
        grads = center_ref[rows, :channels]
        forces = center_ref[rows, channels : channels + 3]
        for ref in coded_refs:
            one, two = decoded(ref, rows)
            grads, forces = grads + one, forces + two
        forces_ref[:, t, :] = forces[0]
        column = lax.broadcasted_iota(jnp.int32, (channels, atoms), 1)
        masked = jnp.where(column < counts_ref[t], grads[0], 0.0)
        grads_ref[t] = jnp.transpose(masked)


def step(positions, features, counts, neighbours, mix_weight, readout, radial_rates):
    tiles, atoms = positions.shape[3], positions.shape[5]
    channels = features.shape[5]
    slots = neighbours.shape[4]
    radials = radial_rates.shape[0]
    vmem = pl.BlockSpec(memory_space=pltpu.VMEM)
    smem = pl.BlockSpec(memory_space=pltpu.SMEM)
    hbm = pl.BlockSpec(memory_space=pl.ANY)
    small = pltpu.CompilerParams(vmem_limit_bytes=SMALL)

    def swap(value, axis):
        return [lax.ppermute(value, axis, pairs) for pairs in swaps(axis)]

    sides = tuple(len(swaps(axis)) for axis in ("gx", "gy", "gz"))
    own_counts = counts.reshape(tiles)
    points = jnp.transpose(positions, (0, 1, 2, 4, 3, 5)).reshape(3, tiles, atoms)
    packed = pl.pallas_call(
        pack_kernel,
        out_shape=jax.ShapeDtypeStruct((tiles, atoms + 16, channels), jnp.bfloat16),
        in_specs=[smem, vmem, vmem],
        out_specs=vmem,
        scratch_shapes=[pltpu.VMEM((tiles, 16, channels), jnp.float32)],
        compiler_params=pltpu.CompilerParams(vmem_limit_bytes=60 << 20),
        name="pack",
    )(own_counts, features.reshape(tiles, atoms, channels), points)
    along_z = swap(packed, "gz")
    own_counts, table, local = pl.pallas_call(
        functools.partial(side_kernel, sides),
        out_shape=[
            jax.ShapeDtypeStruct((tiles,), jnp.int32),
            jax.ShapeDtypeStruct((tiles, slots + 2), jnp.int32),
            jax.ShapeDtypeStruct(packed.shape, packed.dtype),
        ],
        in_specs=[smem, smem, smem, vmem],
        out_specs=[smem, smem, vmem],
        compiler_params=small,
        name="sides",
    )(
        jnp.stack([lax.axis_index(axis) % 2 for axis in ("gx", "gy", "gz")]),
        own_counts,
        neighbours.reshape(tiles, slots),
        packed,
    )
    (line,) = join([list(range(1 + len(along_z)))], local, *along_z)
    lines = [line] + swap(line, "gy")
    rates, points, readout, mix_weight = pl.pallas_call(
        stage_kernel,
        out_shape=[
            jax.ShapeDtypeStruct((radials,), jnp.float32),
            jax.ShapeDtypeStruct((3, tiles, atoms), jnp.float32),
            jax.ShapeDtypeStruct((1, channels), jnp.float32),
            jax.ShapeDtypeStruct(mix_weight.shape, mix_weight.dtype),
        ],
        in_specs=[smem, vmem, vmem, vmem],
        out_specs=[smem, vmem, vmem, vmem],
        compiler_params=small,
        name="stage",
    )(radial_rates, points, readout.reshape(1, channels), mix_weight)
    pieces = [lines]
    for pairs in swaps("gx"):
        plane = [lax.ppermute(line, "gx", pairs)]
        pieces.append(plane + [lax.ppermute(piece, "gx", pairs) for piece in lines[1:]])
    flat = [piece for plane in pieces for piece in plane]

    total = sum(piece.shape[0] for piece in flat)
    couples = (slots + 1) // 2
    bases = 4 * radials
    chunks = atoms // ROWS
    ghost_rows = channels + EXTRA
    counts_of = (line.shape[0], total // len(pieces))

    def ghost_shapes(arrays):
        return [
            jax.ShapeDtypeStruct((array.shape[0], ghost_rows, atoms), jnp.float32)
            for array in arrays
        ]

    far_shapes = ghost_shapes([piece for plane in pieces for piece in plane[1:]])
    line_shapes = ghost_shapes([plane[0] for plane in pieces])
    state_shapes = [
        jax.ShapeDtypeStruct((tiles, 3, atoms, atoms), jnp.float32),
        jax.ShapeDtypeStruct((tiles, 2 * couples + 2, 3, GROUP, atoms), jnp.float32),
        jax.ShapeDtypeStruct((tiles, (2 * couples + 6) * atoms, channels), jnp.bfloat16),
        jax.ShapeDtypeStruct((tiles, 2 * couples, bases * atoms, atoms), jnp.bfloat16),
        jax.ShapeDtypeStruct((tiles, bases * atoms, channels), jnp.bfloat16),
        jax.ShapeDtypeStruct((tiles, chunks, channels, bases * ROWS), jnp.bfloat16),
        jax.ShapeDtypeStruct((tiles, 3, atoms, atoms), jnp.float32),
    ]
    sums = [
        pltpu.VMEM((tiles * (couples + 1), channels, 2 * atoms), jnp.float32),
        pltpu.VMEM((tiles * (couples + 1), 2, 3, GROUP, atoms), jnp.float32),
    ]
    buffers = [pltpu.VMEM((bases * ROWS, 2 * atoms), jnp.float32)] * 4
    large = pltpu.CompilerParams(vmem_limit_bytes=LARGE)
    results = pl.pallas_call(
        functools.partial(main_kernel, len(flat), len(far_shapes), slots, counts_of),
        out_shape=far_shapes + state_shapes,
        in_specs=[smem] * 3 + [vmem] * 3 + [hbm] * len(flat),
        out_specs=[hbm] * len(far_shapes) + [vmem] * len(state_shapes),
        scratch_shapes=[
            pltpu.VMEM((total, atoms + 16, channels), jnp.bfloat16),
            pltpu.VMEM((tiles, bases * atoms, channels), jnp.float32),
            *sums,
            pltpu.VMEM(
                (sum(shape.shape[0] for shape in far_shapes), ghost_rows, atoms), jnp.float32
            ),
            pltpu.SemaphoreType.DMA((len(flat),)),
            pltpu.SemaphoreType.DMA((len(far_shapes),)),
            *buffers,
        ],
        compiler_params=large,
        name="pairs",
    )(own_counts, table, rates, points, mix_weight, readout, *flat)
    state = results[len(far_shapes) :]
    line_ghosts = pl.pallas_call(
        functools.partial(line_kernel, len(line_shapes), slots, counts_of),
        out_shape=line_shapes,
        in_specs=[smem] * 3 + [vmem] * len(state),
        out_specs=[hbm] * len(line_shapes),
        scratch_shapes=[
            *sums,
            pltpu.VMEM((tiles, 3, atoms, atoms), jnp.float32),
            pltpu.VMEM(
                (sum(shape.shape[0] for shape in line_shapes), ghost_rows, atoms), jnp.float32
            ),
            pltpu.SemaphoreType.DMA((len(line_shapes),)),
            *buffers,
        ],
        compiler_params=large,
        name="lines",
    )(own_counts, table, rates, *state)
    width = len(pieces[0]) - 1
    ghosts = [
        [line_ghosts[k]] + list(results[k * width : (k + 1) * width]) for k in range(len(pieces))
    ]

    def gather(k):
        coded = []
        for plane, pairs in zip(ghosts[1:], swaps("gx")):
            (value,) = fold([(0, plane[k].shape[0], True)], [plane[k]], [])
            coded.append(send(value, "gx", pairs))
        return [ghosts[0][k]], coded

    received = []
    for k, pairs in enumerate(swaps("gy")):
        plain, coded = gather(k + 1)
        (value,) = fold([(0, plain[0].shape[0], True)], plain, coded)
        received.append(send(value, "gy", pairs))
    plain, coded = gather(0)
    cuts = [(k * tiles, (k + 1) * tiles, k > 0) for k in range(sides[2] + 1)]
    center, *along_z = fold(cuts, plain, coded + received)
    parts = [center]
    for value, pairs in zip(along_z, swaps("gz")):
        parts.append(send(value, "gz", pairs))

    forces, grads = pl.pallas_call(
        final_kernel,
        out_shape=[
            jax.ShapeDtypeStruct((3, tiles, atoms), jnp.float32),
            jax.ShapeDtypeStruct((tiles, channels, atoms), jnp.float32),
        ],
        in_specs=[smem] + [vmem] * len(parts),
        out_specs=[vmem, vmem],
        compiler_params=small,
        name="finish",
    )(own_counts, *parts)
    forces = jnp.transpose(forces.reshape(1, 1, 1, 3, tiles, atoms), (0, 1, 2, 4, 3, 5))
    return forces, grads.reshape(1, 1, 1, tiles, atoms, channels)


def solution(mesh):
    in_specs = (
        P("gx", "gy", "gz", None, None, None),
        P("gx", "gy", "gz", None, None, None),
        P("gx", "gy", "gz", None),
        P("gx", "gy", "gz", None, None),
        P(),
        P(),
        P(),
    )
    out_specs = (P("gx", "gy", "gz", None, None, None), P("gx", "gy", "gz", None, None, None))
    return jax.shard_map(step, mesh=mesh, in_specs=in_specs, out_specs=out_specs, check_vma=False)
```

```python
import functools

import jax
import jax.numpy as jnp
from jax import lax
from jax.experimental import pallas as pl
from jax.experimental.pallas import tpu as pltpu
from jax.sharding import PartitionSpec as P


ROWS = 32
EXTRA = 8
TOP = 14.0
TINY = 1e-30
GROUP = 8
LOG2E = 1.4426950408889634
SMALL = 8 << 20
LARGE = 20 << 20
NT = (((1,), (1,)), ((), ()))


def swaps(axis):
    count = lax.axis_size(axis)
    result = []
    for first in (0, 1):
        pairs = [(i, i + 1) for i in range(first, count - 1, 2)]
        if pairs:
            result.append(pairs + [(b, a) for a, b in pairs])
    return result


def side_of(step, parity, sides):
    side = jnp.where((step == 1) == (parity == 0), 1, 2)
    return jnp.minimum(jnp.where(step == 0, 0, side), sides)


def pack_kernel(counts_ref, features_ref, points_ref, packed_ref, extra_ref):
    tiles, atoms, _ = features_ref.shape
    extra_ref[...] = jnp.zeros_like(extra_ref)
    for t in range(tiles):
        count = counts_ref[t]
        rows = lax.broadcasted_iota(jnp.int32, features_ref.shape[1:], 0)
        values = features_ref[t].astype(jnp.float32)
        packed_ref[t, :atoms] = jnp.where(rows < count, values, 0.0).astype(jnp.bfloat16)
        rest = points_ref[:, t, :]
        for term in range(3):
            part = rest.astype(jnp.bfloat16).astype(jnp.float32)
            extra_ref[t, 3 * term : 3 * term + 3] = part
            rest = rest - part
        packed_ref[t, atoms:] = extra_ref[t].astype(jnp.bfloat16)


def side_kernel(
    sides,
    axis_ref,
    counts_ref,
    neighbours_ref,
    packed_ref,
    out_counts_ref,
    out_table_ref,
    out_packed_ref,
):
    tiles, slots = neighbours_ref.shape
    for t in range(tiles):
        out_counts_ref[t] = counts_ref[t]
        spots = []
        for k in range(slots):
            target = jnp.maximum(neighbours_ref[t, k], 0)
            block = lax.div(target, tiles)
            steps = (lax.div(block, 9), lax.rem(lax.div(block, 3), 3), lax.rem(block, 3))
            x, y, z = (side_of(steps[m] - 1, axis_ref[m], sides[m]) for m in range(3))
            block = (x * (sides[1] + 1) + y) * (sides[2] + 1) + z
            live = neighbours_ref[t, k] >= 0
            spots.append((block * tiles + lax.rem(target, tiles), live, live & (y == 0)))
            out_table_ref[t, k] = -1
        near = sum(jnp.where(line, 1, 0) for _, _, line in spots)
        total = sum(jnp.where(live, 1, 0) for _, live, _ in spots)
        out_table_ref[t, slots] = near
        out_table_ref[t, slots + 1] = total
        at_near, at_far = jnp.zeros((), jnp.int32), near
        for spot, live, line in spots:

            def put(spot=spot, at=jnp.where(line, at_near, at_far)):
                out_table_ref[t, at] = spot

            pl.when(live)(put)
            at_near = at_near + jnp.where(line, 1, 0)
            at_far = at_far + jnp.where(live & ~line, 1, 0)
    out_packed_ref[...] = packed_ref[...]


def stage_kernel(rates_ref, points_ref, readout_ref, mixing_ref, *out_refs):
    for r in range(rates_ref.shape[0]):
        out_refs[0][r] = rates_ref[r]
    out_refs[1][...] = points_ref[...]
    out_refs[2][...] = readout_ref[...]
    out_refs[3][...] = mixing_ref[...]


def join_kernel(groups, *refs):
    inputs = refs[: -len(groups)]
    for group, out_ref in zip(groups, refs[-len(groups) :]):
        at = 0
        for k in group:
            count = inputs[k].shape[0]
            out_ref[at : at + count] = inputs[k][...]
            at += count


def join(groups, *arrays):
    shapes = [
        jax.ShapeDtypeStruct(
            (sum(arrays[k].shape[0] for k in group),) + arrays[0].shape[1:], arrays[0].dtype
        )
        for group in groups
    ]
    vmem = pl.BlockSpec(memory_space=pltpu.VMEM)
    return pl.pallas_call(
        functools.partial(join_kernel, groups),
        out_shape=shapes,
        in_specs=[vmem] * len(arrays),
        out_specs=[vmem] * len(groups),
        compiler_params=pltpu.CompilerParams(vmem_limit_bytes=SMALL),
        name="join",
    )(*arrays)


def decoded(ref, rows):
    value = ref[rows]
    channels = value.shape[1] - EXTRA
    grads = value[:, :channels] * jnp.exp2(value[:, channels + 3 : channels + 4] - TOP)
    forces = value[:, channels : channels + 3] * jnp.exp2(
        value[:, channels + 4 : channels + 5] - TOP
    )
    return grads, forces


def fold_kernel(cuts, plain, coded, *refs):
    plain_refs, coded_refs = refs[:plain], refs[plain : plain + coded]
    for (low, high, code), out_ref in zip(cuts, refs[plain + coded :]):
        channels = out_ref.shape[1] - EXTRA
        rows = slice(low, high)
        grads = forces = None
        for ref in plain_refs:
            part = ref[rows]
            grads = part[:, :channels] if grads is None else grads + part[:, :channels]
            part = part[:, channels : channels + 3]
            forces = part if forces is None else forces + part
        for ref in coded_refs:
            one, two = decoded(ref, rows)
            grads, forces = grads + one, forces + two
        if not code:
            out_ref[:, :channels] = grads
            out_ref[:, channels : channels + 3] = forces
            continue
        for first, value, at in ((0, grads, 3), (channels, forces, 4)):
            bound = jnp.max(jnp.abs(value), axis=1, keepdims=True)
            exponent = jnp.ceil(jnp.log2(jnp.maximum(bound, TINY)))
            out_ref[:, first : first + value.shape[1]] = value * jnp.exp2(TOP - exponent)
            out_ref[:, channels + at : channels + at + 1] = exponent


def fold(cuts, plain, coded):
    arrays = list(plain) + list(coded)
    shapes = [
        jax.ShapeDtypeStruct((high - low,) + arrays[0].shape[1:], jnp.float32)
        for low, high, _ in cuts
    ]
    vmem = pl.BlockSpec(memory_space=pltpu.VMEM)
    return pl.pallas_call(
        functools.partial(fold_kernel, cuts, len(plain), len(coded)),
        out_shape=shapes,
        in_specs=[vmem] * len(arrays),
        out_specs=[vmem] * len(cuts),
        compiler_params=pltpu.CompilerParams(vmem_limit_bytes=SMALL),
        name="fold",
    )(*arrays)


def send(value, axis, pairs):
    return lax.ppermute(value.astype(jnp.float16), axis, pairs).astype(jnp.float32)


class Pairs:
    def __init__(self, rates_ref, own_ref, other_ref, channels, atoms):
        self.rates = [rates_ref[r] for r in range(rates_ref.shape[0])]
        self.powers = [-rate * LOG2E for rate in self.rates]
        self.own_ref, self.other_ref = own_ref, other_ref
        self.channels, self.atoms = channels, atoms
        self.group_rows = 4 * len(self.rates) * GROUP
        self.groups = ROWS // GROUP
        self.chunk_rows = self.group_rows * self.groups

    def geometry(self, t, slot, where):
        offset = [self.other_ref[t, slot, m] - self.own_ref[t, m, where, :] for m in range(3)]
        square = offset[0] * offset[0] + offset[1] * offset[1] + offset[2] * offset[2]
        return offset, [jnp.exp2(power * square) for power in self.powers]

    def backward(
        self,
        chunks,
        firsts,
        lasts,
        masked,
        block,
        couples,
        seed_ref,
        seed_t_ref,
        features_ref,
        basis_ref,
        near_grad_ref,
        near_force_ref,
        own_force_ref,
        grad_refs,
    ):
        atoms, group_rows, chunk_rows = self.atoms, self.group_rows, self.chunk_rows
        near_grad_ref[...] = jnp.zeros_like(near_grad_ref)
        near_force_ref[...] = jnp.zeros_like(near_force_ref)
        tiles = len(chunks)
        lengths = [(lasts[k] - firsts[k]) * chunks[k] for k in range(tiles)]
        steps = sum(lengths)
        zero = jnp.zeros((), jnp.int32)

        def of(values, t):
            result = values[-1]
            for k in reversed(range(tiles - 1)):
                result = jnp.where(t == k, values[k], result)
            return result

        def enter(start):
            t = jnp.full((), tiles, jnp.int32)
            for k in reversed(range(tiles)):
                t = jnp.where((start <= k) & (lengths[k] > 0), k, t)
            found = t < tiles
            t = jnp.minimum(t, tiles - 1)
            return t, jnp.where(found, of(firsts, t), couples), zero

        def following(place):
            t, couple, chunk = place
            wrap = chunk + 1 >= of(chunks, t)
            end = wrap & (couple + 1 >= of(lasts, t))
            tile, start, _ = enter(t + 1)
            inside = jnp.where(wrap, couple + 1, couple)
            return (
                jnp.where(end, tile, t),
                jnp.where(end, start, inside),
                jnp.where(wrap, 0, chunk + 1),
            )

        def multiply(place, grad_ref):
            t, couple, chunk = place
            base = pl.multiple_of(chunk * chunk_rows, chunk_rows)
            where = pl.ds(base, chunk_rows)
            spot = jnp.where(couple == of(masked, t), block, couple)
            spot = pl.multiple_of(spot * 2 * atoms, 2 * atoms)
            grad_ref[...] = lax.dot_general(
                seed_ref[t, where, :],
                features_ref[t, pl.ds(spot, 2 * atoms), :],
                NT,
                preferred_element_type=jnp.float32,
            )
            stored = jnp.minimum(couple, couples - 1)
            basis = [basis_ref[t, 2 * stored + half, where, :] for half in range(2)]
            near_grad_ref[t * (couples + 1) + couple] += jnp.dot(
                seed_t_ref[t, chunk],
                jnp.concatenate(basis, axis=1),
                preferred_element_type=jnp.float32,
            )

        def pull(place, grad_ref):
            t, couple, chunk = place
            start = pl.multiple_of(chunk * ROWS, ROWS)
            pulled = [[None] * 3 for _ in range(2)]
            for g in range(self.groups):
                rows = pl.ds(start + g * GROUP, GROUP)
                total = [None] * 3
                for half in range(2):
                    lanes = slice(half * atoms, (half + 1) * atoms)
                    offset, radial = self.geometry(t, 2 * couple + half, rows)
                    direct = [None] * 3
                    inner = None
                    for r, rate in enumerate(self.rates):
                        row = g * group_rows + 4 * r * GROUP
                        grad = [
                            grad_ref[row + m * GROUP : row + (m + 1) * GROUP, lanes]
                            for m in range(4)
                        ]
                        along = grad[0]
                        for m in range(3):
                            along = along + grad[m + 1] * offset[m]
                            part = radial[r] * grad[m + 1]
                            direct[m] = part if r == 0 else direct[m] + part
                        part = (radial[r] * (2.0 * rate)) * along
                        inner = part if r == 0 else inner + part
                    for m in range(3):
                        force = direct[m] - offset[m] * inner
                        total[m] = force if half == 0 else total[m] + force
                        old = pulled[half][m]
                        pulled[half][m] = force if g == 0 else old + force
                for m in range(3):
                    own_force_ref[t, m, rows, :] += total[m]
            for half in range(2):
                for m in range(3):
                    near_force_ref[t * (couples + 1) + couple, half, m] += pulled[half][m]

        one = enter(zero)
        two = following(one)
        multiply(one, grad_refs[0])
        multiply(two, grad_refs[1])

        def loop(k, places):
            one, two = places
            three = following(two)
            four = following(three)
            five = following(four)
            six = following(five)
            pull(one, grad_refs[0])
            multiply(three, grad_refs[2])
            pull(two, grad_refs[1])
            multiply(four, grad_refs[3])
            pull(three, grad_refs[2])
            multiply(five, grad_refs[0])
            pull(four, grad_refs[3])
            multiply(six, grad_refs[1])
            return five, six

        lax.fori_loop(0, (steps + 3) // 4, loop, (one, two))

    def give(self, row, half, tile, near_grad_ref, near_force_ref, ghost_ref):
        channels, atoms = self.channels, self.atoms
        lanes = slice(half * atoms, (half + 1) * atoms)
        ghost_ref[tile, :channels, :] += near_grad_ref[row, :, lanes]
        for m in range(3):
            ghost_ref[tile, channels + m : channels + m + 1, :] -= jnp.sum(
                near_force_ref[row, half, m], axis=0, keepdims=True
            )


def starts_of(piece_refs):
    return [sum(ref.shape[0] for ref in piece_refs[:k]) for k in range(len(piece_refs))]


def copies(pairs, sems):
    result = [
        pltpu.make_async_copy(source, target, sems.at[k])
        for k, (source, target) in enumerate(pairs)
    ]
    for copy in result:
        copy.start()
    return result


def main_kernel(
    pieces,
    outs,
    slots,
    line,
    counts_ref,
    table_ref,
    rates_ref,
    points_ref,
    mixing_ref,
    readout_ref,
    *refs,
):
    piece_refs = refs[:pieces]
    ghost_refs = refs[pieces : pieces + outs]
    (
        own_ref,
        other_ref,
        features_ref,
        basis_ref,
        seed_ref,
        seed_t_ref,
        own_force_ref,
        near_ref,
        sum_ref,
        near_grad_ref,
        near_force_ref,
        ghost_ref,
        in_sems,
        out_sems,
        *grad_refs,
    ) = refs[pieces + outs :]
    _, tiles, atoms = points_ref.shape
    channels = readout_ref.shape[1]
    couples = (slots + 1) // 2
    scaling = (slots * atoms) ** (-0.5)
    starts = starts_of(piece_refs)
    loads = copies(
        [
            (ref, near_ref.at[pl.ds(start, ref.shape[0])])
            for ref, start in zip(piece_refs, starts)
        ],
        in_sems,
    )

    for t in range(tiles):
        lines = [points_ref[m, t : t + 1, :] for m in range(3)]
        lines.append(jnp.zeros((atoms - 3, atoms), jnp.float32))
        columns = jnp.transpose(jnp.concatenate(lines, axis=0))
        for m in range(3):
            own_ref[t, m] = jnp.broadcast_to(columns[:, m : m + 1], (atoms, atoms))
    ghost_ref[...] = jnp.zeros_like(ghost_ref)
    own_force_ref[...] = jnp.zeros_like(own_force_ref)

    for load in loads:
        load.wait()

    pairs = Pairs(rates_ref, own_ref, other_ref, channels, atoms)
    radials, groups = len(pairs.rates), pairs.groups
    group_rows, chunk_rows = pairs.group_rows, pairs.chunk_rows

    for t in range(tiles):
        count = counts_ref[t]
        chunks = (count + (ROWS - 1)) // ROWS
        near = table_ref[t, slots]

        def work(t=t, count=count, chunks=chunks, near=near):
            for k in range(slots):
                tile = table_ref[t, k]
                live = tile >= 0
                tile = jnp.maximum(tile, 0)
                values = near_ref[tile, :atoms, :]
                features_ref[t, k * atoms : (k + 1) * atoms] = jnp.where(
                    live, values, jnp.zeros_like(values)
                )
                extra = near_ref[tile, atoms:, :].astype(jnp.float32)
                total = extra[0:3] + extra[3:6] + extra[6:9]
                for m in range(3):
                    other_ref[t, k, m] = jnp.broadcast_to(total[m : m + 1, :], (GROUP, atoms))
            for k in range(slots, 2 * couples + 2):
                for m in range(3):
                    other_ref[t, k, m] = jnp.zeros((GROUP, atoms), jnp.float32)
            features_ref[t, slots * atoms :] = jnp.zeros(
                ((2 * couples + 6 - slots) * atoms, channels), jnp.bfloat16
            )
            ahead = pl.ds(pl.multiple_of(near * atoms, atoms), atoms)
            behind = pl.ds(pl.multiple_of((near - 1) * atoms, atoms), atoms)
            spare = (2 * couples + 2) * atoms
            features_ref[t, spare + atoms : spare + 2 * atoms] = features_ref[t, ahead, :]
            features_ref[t, spare + 2 * atoms : spare + 3 * atoms] = features_ref[t, behind, :]

            def forward(used, chunk, carry):
                start = pl.multiple_of(chunk * ROWS, ROWS)
                base = pl.multiple_of(chunk * chunk_rows, chunk_rows)
                for slot in range(2 * used):
                    for g in range(groups):
                        where = pl.ds(start + g * GROUP, GROUP)
                        offset, radial = pairs.geometry(t, slot, where)
                        for r in range(radials):
                            values = [radial[r]] + [radial[r] * offset[m] for m in range(3)]
                            for k in range(2):
                                pair = jnp.concatenate(values[2 * k : 2 * k + 2], axis=0)
                                row = base + g * group_rows + (4 * r + 2 * k) * GROUP
                                basis_ref[t, slot, pl.ds(row, 2 * GROUP), :] = pair.astype(
                                    jnp.bfloat16
                                )
                where = pl.ds(base, chunk_rows)
                basis = [basis_ref[t, slot, where, :] for slot in range(2 * used)]
                sum_ref[t, where, :] = (
                    jnp.dot(
                        jnp.concatenate(basis, axis=1),
                        features_ref[t, : 2 * used * atoms],
                        preferred_element_type=jnp.float32,
                    )
                    * scaling
                )
                return carry

            for used in range(1, couples + 1):

                def run(used=used):
                    lax.fori_loop(0, chunks, functools.partial(forward, used), 0)

                pl.when((table_ref[t, slots + 1] + 1) // 2 == used)(run)

            def clear(chunk, carry):
                where = pl.ds(pl.multiple_of(chunk * chunk_rows, chunk_rows), chunk_rows)
                sum_ref[t, where, :] = jnp.zeros((chunk_rows, channels), jnp.float32)
                return carry

            lax.fori_loop(chunks, atoms // ROWS, clear, 0)

            def sums(r, m):
                first = (4 * r + m) * GROUP
                return jnp.concatenate(
                    [
                        sum_ref[t, g * group_rows + first : g * group_rows + first + GROUP, :]
                        for g in range(atoms // GROUP)
                    ],
                    axis=0,
                )

            parts = [sums(r, 0) for r in range(radials)]
            for r in range(radials):
                norm = None
                for m in range(1, 4):
                    value = sums(r, m)
                    norm = value * value if norm is None else norm + value * value
                parts.append(norm)
            invariant = jnp.concatenate([part.astype(jnp.bfloat16) for part in parts], axis=1)
            preact = jnp.dot(invariant, mixing_ref[...], preferred_element_type=jnp.float32)
            sigmoid = jax.nn.sigmoid(preact)
            row = lax.broadcasted_iota(jnp.int32, (atoms, channels), 0)
            valid = (row < count).astype(jnp.float32)
            grad_pre = valid * readout_ref[...] * sigmoid * (1.0 + preact * (1.0 - sigmoid))
            grad = lax.dot_general(
                grad_pre.astype(jnp.bfloat16),
                mixing_ref[...],
                NT,
                preferred_element_type=jnp.float32,
            )
            for r in range(radials):
                scalar = grad[:, r * channels : (r + 1) * channels] * scaling
                square = grad[:, (radials + r) * channels : (radials + r + 1) * channels]
                square = square * (2.0 * scaling)
                values = [scalar] + [square * sums(r, m) for m in range(1, 4)]
                for g in range(atoms // GROUP):
                    rows = slice(g * GROUP, (g + 1) * GROUP)
                    for k in range(2):
                        pair = jnp.concatenate(
                            [value[rows] for value in values[2 * k : 2 * k + 2]], axis=0
                        )
                        first = g * group_rows + (4 * r + 2 * k) * GROUP
                        seed_ref[t, first : first + 2 * GROUP, :] = pair.astype(jnp.bfloat16)
            for chunk in range(atoms // ROWS):
                rows = slice(chunk * chunk_rows, (chunk + 1) * chunk_rows)
                seed_t_ref[t, chunk] = jnp.transpose(seed_ref[t, rows, :])

        pl.when(count > 0)(work)

    counts = [counts_ref[t] for t in range(tiles)]
    nears = [table_ref[t, slots] for t in range(tiles)]
    totals = [table_ref[t, slots + 1] for t in range(tiles)]
    active = [(counts[t] > 0) & (totals[t] > nears[t]) for t in range(tiles)]
    firsts = [nears[t] // 2 for t in range(tiles)]
    lasts = [jnp.where(active[t], (totals[t] + 1) // 2, firsts[t]) for t in range(tiles)]

    def distant():
        pairs.backward(
            [(count + (ROWS - 1)) // ROWS for count in counts],
            firsts,
            lasts,
            [jnp.where(nears[t] % 2 == 1, firsts[t], -1) for t in range(tiles)],
            couples + 1,
            couples,
            seed_ref,
            seed_t_ref,
            features_ref,
            basis_ref,
            near_grad_ref,
            near_force_ref,
            own_force_ref,
            grad_refs,
        )
        for t in range(tiles):
            for slot in range(1, slots):

                def give(t=t, slot=slot):
                    tile = table_ref[t, slot]
                    plane = lax.div(tile, line[1])
                    tile = tile - line[0] * (plane + 1)
                    row = t * (couples + 1) + slot // 2
                    pairs.give(row, slot % 2, tile, near_grad_ref, near_force_ref, ghost_ref)

                pl.when(active[t] & (slot >= nears[t]) & (slot < totals[t]))(give)

    some = active[0]
    for t in range(1, tiles):
        some = some | active[t]
    pl.when(some)(distant)

    starts = starts_of(ghost_refs)
    for store in copies(
        [
            (ghost_ref.at[pl.ds(start, ref.shape[0])], ref)
            for ref, start in zip(ghost_refs, starts)
        ],
        out_sems,
    ):
        store.wait()


def line_kernel(
    outs,
    slots,
    line,
    counts_ref,
    table_ref,
    rates_ref,
    own_ref,
    other_ref,
    features_ref,
    basis_ref,
    seed_ref,
    seed_t_ref,
    far_force_ref,
    *refs,
):
    ghost_refs = refs[:outs]
    near_grad_ref, near_force_ref, own_force_ref, ghost_ref, out_sems, *grad_refs = refs[outs:]
    tiles, _, atoms, _ = own_ref.shape
    channels = features_ref.shape[2]
    couples = (slots + 1) // 2
    pairs = Pairs(rates_ref, own_ref, other_ref, channels, atoms)
    ghost_ref[...] = jnp.zeros_like(ghost_ref)
    own_force_ref[...] = far_force_ref[...]
    counts = [counts_ref[t] for t in range(tiles)]
    nears = [table_ref[t, slots] for t in range(tiles)]
    zero = jnp.zeros((), jnp.int32)

    def linear():
        pairs.backward(
            [(count + (ROWS - 1)) // ROWS for count in counts],
            [zero] * tiles,
            [jnp.where(counts[t] > 0, (nears[t] + 1) // 2, 0) for t in range(tiles)],
            [jnp.where(nears[t] % 2 == 1, nears[t] // 2, -1) for t in range(tiles)],
            couples + 2,
            couples,
            seed_ref,
            seed_t_ref,
            features_ref,
            basis_ref,
            near_grad_ref,
            near_force_ref,
            own_force_ref,
            grad_refs,
        )
        for t in range(tiles):
            for slot in range(slots):

                def give(t=t, slot=slot):
                    tile = table_ref[t, slot]
                    tile = tile - (line[1] - line[0]) * lax.div(tile, line[1])
                    row = t * (couples + 1) + slot // 2
                    pairs.give(row, slot % 2, tile, near_grad_ref, near_force_ref, ghost_ref)

                pl.when((counts[t] > 0) & (slot < nears[t]))(give)

            def own(t=t):
                for m in range(3):
                    ghost_ref[t, channels + m : channels + m + 1, :] += jnp.sum(
                        jnp.transpose(own_force_ref[t, m]), axis=0, keepdims=True
                    )

            pl.when(counts[t] > 0)(own)

    some = counts[0] > 0
    for t in range(1, tiles):
        some = some | (counts[t] > 0)
    pl.when(some)(linear)
    starts = starts_of(ghost_refs)
    for store in copies(
        [
            (ghost_ref.at[pl.ds(start, ref.shape[0])], ref)
            for ref, start in zip(ghost_refs, starts)
        ],
        out_sems,
    ):
        store.wait()


def final_kernel(counts_ref, center_ref, *refs):
    coded_refs = refs[:-2]
    forces_ref, grads_ref = refs[-2:]
    tiles, channels, atoms = grads_ref.shape
    for t in range(tiles):
        rows = slice(t, t + 1)
        grads = center_ref[rows, :channels]
        forces = center_ref[rows, channels : channels + 3]
        for ref in coded_refs:
            one, two = decoded(ref, rows)
            grads, forces = grads + one, forces + two
        forces_ref[:, t, :] = forces[0]
        column = lax.broadcasted_iota(jnp.int32, (channels, atoms), 1)
        masked = jnp.where(column < counts_ref[t], grads[0], 0.0)
        grads_ref[t] = jnp.transpose(masked)


def step(positions, features, counts, neighbours, mix_weight, readout, radial_rates):
    tiles, atoms = positions.shape[3], positions.shape[5]
    channels = features.shape[5]
    slots = neighbours.shape[4]
    radials = radial_rates.shape[0]
    vmem = pl.BlockSpec(memory_space=pltpu.VMEM)
    smem = pl.BlockSpec(memory_space=pltpu.SMEM)
    hbm = pl.BlockSpec(memory_space=pl.ANY)
    small = pltpu.CompilerParams(vmem_limit_bytes=SMALL)

    def swap(value, axis):
        return [lax.ppermute(value, axis, pairs) for pairs in swaps(axis)]

    sides = tuple(len(swaps(axis)) for axis in ("gx", "gy", "gz"))
    own_counts = counts.reshape(tiles)
    points = jnp.transpose(positions, (0, 1, 2, 4, 3, 5)).reshape(3, tiles, atoms)
    packed = pl.pallas_call(
        pack_kernel,
        out_shape=jax.ShapeDtypeStruct((tiles, atoms + 16, channels), jnp.bfloat16),
        in_specs=[smem, vmem, vmem],
        out_specs=vmem,
        scratch_shapes=[pltpu.VMEM((tiles, 16, channels), jnp.float32)],
        compiler_params=pltpu.CompilerParams(vmem_limit_bytes=60 << 20),
        name="pack",
    )(own_counts, features.reshape(tiles, atoms, channels), points)
    along_z = swap(packed, "gz")
    own_counts, table, local = pl.pallas_call(
        functools.partial(side_kernel, sides),
        out_shape=[
            jax.ShapeDtypeStruct((tiles,), jnp.int32),
            jax.ShapeDtypeStruct((tiles, slots + 2), jnp.int32),
            jax.ShapeDtypeStruct(packed.shape, packed.dtype),
        ],
        in_specs=[smem, smem, smem, vmem],
        out_specs=[smem, smem, vmem],
        compiler_params=small,
        name="sides",
    )(
        jnp.stack([lax.axis_index(axis) % 2 for axis in ("gx", "gy", "gz")]),
        own_counts,
        neighbours.reshape(tiles, slots),
        packed,
    )
    (line,) = join([list(range(1 + len(along_z)))], local, *along_z)
    lines = [line] + swap(line, "gy")
    rates, points, readout, mix_weight = pl.pallas_call(
        stage_kernel,
        out_shape=[
            jax.ShapeDtypeStruct((radials,), jnp.float32),
            jax.ShapeDtypeStruct((3, tiles, atoms), jnp.float32),
            jax.ShapeDtypeStruct((1, channels), jnp.float32),
            jax.ShapeDtypeStruct(mix_weight.shape, mix_weight.dtype),
        ],
        in_specs=[smem, vmem, vmem, vmem],
        out_specs=[smem, vmem, vmem, vmem],
        compiler_params=small,
        name="stage",
    )(radial_rates, points, readout.reshape(1, channels), mix_weight)
    pieces = [lines]
    for pairs in swaps("gx"):
        plane = [lax.ppermute(line, "gx", pairs)]
        pieces.append(plane + [lax.ppermute(piece, "gx", pairs) for piece in lines[1:]])
    flat = [piece for plane in pieces for piece in plane]

    total = sum(piece.shape[0] for piece in flat)
    couples = (slots + 1) // 2
    bases = 4 * radials
    chunks = atoms // ROWS
    ghost_rows = channels + EXTRA
    counts_of = (line.shape[0], total // len(pieces))

    def ghost_shapes(arrays):
        return [
            jax.ShapeDtypeStruct((array.shape[0], ghost_rows, atoms), jnp.float32)
            for array in arrays
        ]

    far_shapes = ghost_shapes([piece for plane in pieces for piece in plane[1:]])
    line_shapes = ghost_shapes([plane[0] for plane in pieces])
    state_shapes = [
        jax.ShapeDtypeStruct((tiles, 3, atoms, atoms), jnp.float32),
        jax.ShapeDtypeStruct((tiles, 2 * couples + 2, 3, GROUP, atoms), jnp.float32),
        jax.ShapeDtypeStruct((tiles, (2 * couples + 6) * atoms, channels), jnp.bfloat16),
        jax.ShapeDtypeStruct((tiles, 2 * couples, bases * atoms, atoms), jnp.bfloat16),
        jax.ShapeDtypeStruct((tiles, bases * atoms, channels), jnp.bfloat16),
        jax.ShapeDtypeStruct((tiles, chunks, channels, bases * ROWS), jnp.bfloat16),
        jax.ShapeDtypeStruct((tiles, 3, atoms, atoms), jnp.float32),
    ]
    sums = [
        pltpu.VMEM((tiles * (couples + 1), channels, 2 * atoms), jnp.float32),
        pltpu.VMEM((tiles * (couples + 1), 2, 3, GROUP, atoms), jnp.float32),
    ]
    buffers = [pltpu.VMEM((bases * ROWS, 2 * atoms), jnp.float32)] * 4
    large = pltpu.CompilerParams(vmem_limit_bytes=LARGE)
    results = pl.pallas_call(
        functools.partial(main_kernel, len(flat), len(far_shapes), slots, counts_of),
        out_shape=far_shapes + state_shapes,
        in_specs=[smem] * 3 + [vmem] * 3 + [hbm] * len(flat),
        out_specs=[hbm] * len(far_shapes) + [vmem] * len(state_shapes),
        scratch_shapes=[
            pltpu.VMEM((total, atoms + 16, channels), jnp.bfloat16),
            pltpu.VMEM((tiles, bases * atoms, channels), jnp.float32),
            *sums,
            pltpu.VMEM(
                (sum(shape.shape[0] for shape in far_shapes), ghost_rows, atoms), jnp.float32
            ),
            pltpu.SemaphoreType.DMA((len(flat),)),
            pltpu.SemaphoreType.DMA((len(far_shapes),)),
            *buffers,
        ],
        compiler_params=large,
        name="pairs",
    )(own_counts, table, rates, points, mix_weight, readout, *flat)
    state = results[len(far_shapes) :]
    line_ghosts = pl.pallas_call(
        functools.partial(line_kernel, len(line_shapes), slots, counts_of),
        out_shape=line_shapes,
        in_specs=[smem] * 3 + [vmem] * len(state),
        out_specs=[hbm] * len(line_shapes),
        scratch_shapes=[
            *sums,
            pltpu.VMEM((tiles, 3, atoms, atoms), jnp.float32),
            pltpu.VMEM(
                (sum(shape.shape[0] for shape in line_shapes), ghost_rows, atoms), jnp.float32
            ),
            pltpu.SemaphoreType.DMA((len(line_shapes),)),
            *buffers,
        ],
        compiler_params=large,
        name="lines",
    )(own_counts, table, rates, *state)
    width = len(pieces[0]) - 1
    ghosts = [
        [line_ghosts[k]] + list(results[k * width : (k + 1) * width]) for k in range(len(pieces))
    ]

    def gather(k):
        coded = []
        for plane, pairs in zip(ghosts[1:], swaps("gx")):
            (value,) = fold([(0, plane[k].shape[0], True)], [plane[k]], [])
            coded.append(send(value, "gx", pairs))
        return [ghosts[0][k]], coded

    received = []
    for k, pairs in enumerate(swaps("gy")):
        plain, coded = gather(k + 1)
        (value,) = fold([(0, plain[0].shape[0], True)], plain, coded)
        received.append(send(value, "gy", pairs))
    plain, coded = gather(0)
    cuts = [(k * tiles, (k + 1) * tiles, k > 0) for k in range(sides[2] + 1)]
    center, *along_z = fold(cuts, plain, coded + received)
    parts = [center]
    for value, pairs in zip(along_z, swaps("gz")):
        parts.append(send(value, "gz", pairs))

    forces, grads = pl.pallas_call(
        final_kernel,
        out_shape=[
            jax.ShapeDtypeStruct((3, tiles, atoms), jnp.float32),
            jax.ShapeDtypeStruct((tiles, channels, atoms), jnp.float32),
        ],
        in_specs=[smem] + [vmem] * len(parts),
        out_specs=[vmem, vmem],
        compiler_params=small,
        name="finish",
    )(own_counts, *parts)
    forces = jnp.transpose(forces.reshape(1, 1, 1, 3, tiles, atoms), (0, 1, 2, 4, 3, 5))
    return forces, grads.reshape(1, 1, 1, tiles, atoms, channels)


def solution(mesh):
    in_specs = (
        P("gx", "gy", "gz", None, None, None),
        P("gx", "gy", "gz", None, None, None),
        P("gx", "gy", "gz", None),
        P("gx", "gy", "gz", None, None),
        P(),
        P(),
        P(),
    )
    out_specs = (P("gx", "gy", "gz", None, None, None), P("gx", "gy", "gz", None, None, None))
    return jax.shard_map(step, mesh=mesh, in_specs=in_specs, out_specs=out_specs, check_vma=False)
```
